32 devices in a mesh: dp: 8 (over z, x), fsdp: 4 (over y, core).
Axes of the slice: x: 2, y: 2, z: 4, core: 2. Of those that a mesh axis runs over, the one named last changes fastest.
Arguments:
- tokens: bfloat16 [8, 1024, 1536], P('dp', 'fsdp'), may hold values from -6 to 6
- caption: bfloat16 [8, 256, 4096], P('dp', 'fsdp'), may hold values from -6 to 6
- caption_mask: int32 [8, 256], P('dp'), may hold values from 0 to 1, as said below
- item_lengths: int32 [8], P('dp'), may hold values from 512 to 1024, as said below
- item_band: int32 [8], P('dp'), may hold values from 0 to 7
- positions: int32 [8, 2, 1024], P('dp', None, 'fsdp'), may hold values from 0 to 255, as said below
- band_table: bfloat16 [8, 1024], replicated, may hold values from -6 to 6
- adaln_weight: bfloat16 [1024, 9216], P('fsdp'), may hold values from -0.1875 to 0.1875
- adaln_bias: bfloat16 [9216], P('fsdp'), may hold values from -1.5 to 1.5
- query_weight: bfloat16 [1536, 1536], P('fsdp'), may hold values from -0.15625 to 0.15625
- key_weight: bfloat16 [1536, 1536], P('fsdp'), may hold values from -0.15625 to 0.15625
- value_weight: bfloat16 [1536, 1536], P('fsdp'), may hold values from -0.15625 to 0.15625
- outproj_weight: bfloat16 [1536, 1536], P('fsdp'), may hold values from -1.75 to 1.75
- capkey_weight: bfloat16 [4096, 1536], P('fsdp'), may hold values from -0.09375 to 0.09375
- capvalue_weight: bfloat16 [4096, 1536], P('fsdp'), may hold values from -0.09375 to 0.09375
- norm_gains: bfloat16 [5, 1536], P(None, 'fsdp'), may hold values from 0.5 to 1.5
- head_gate: bfloat16 [24], replicated, may hold values from -1.5 to 1.5
- gate_weight: bfloat16 [1536, 4096], P('fsdp'), may hold values from -0.15625 to 0.15625
- up_weight: bfloat16 [1536, 4096], P('fsdp'), may hold values from -0.15625 to 0.15625
- down_weight: bfloat16 [4096, 1536], P('fsdp'), may hold values from -0.1875 to 0.1875
- cotangent: bfloat16 [8, 1024, 1536], P('dp', 'fsdp'), may hold values from -6 to 6
Outputs:
- block_out: bfloat16 [8, 1024, 1536], P('dp', 'fsdp')
- tokens_grad: bfloat16 [8, 1024, 1536], P('dp', 'fsdp')
- adaln_wgrad: float32 [1024, 9216], P(('dp', 'fsdp'))
- adaln_bgrad: float32 [9216], P(('dp', 'fsdp'))
- query_grad: float32 [1536, 1536], P(('dp', 'fsdp'))
- key_grad: float32 [1536, 1536], P(('dp', 'fsdp'))
- value_grad: float32 [1536, 1536], P(('dp', 'fsdp'))
- outproj_grad: float32 [1536, 1536], P(('dp', 'fsdp'))
- capkey_grad: float32 [4096, 1536], P(('dp', 'fsdp'))
- capvalue_grad: float32 [4096, 1536], P(('dp', 'fsdp'))
- gains_grad: float32 [5, 1536], P(None, ('dp', 'fsdp'))
- headgate_grad: float32 [24], replicated
- gate_grad: float32 [1536, 4096], P(('dp', 'fsdp'))
- up_grad: float32 [1536, 4096], P(('dp', 'fsdp'))
- down_grad: float32 [4096, 1536], P(('dp', 'fsdp'))
The draws below stay inside these ranges and needn't reach their ends.
Inputs may be any that keep to these rules, and one draw needn't show every extreme that they name: `item_lengths`: one item has 1024 live patches and another 1024 // 2. `positions`: row and column of each live patch in its item's row-major grid of at most 64 columns; 0 on padding slots. `caption_mask`: each item's live caption tokens come first; between 64 and 256 of them, both reached.
All inputs are finite; a program needn't handle non-finite values.
Results may differ from the reference program's by a relative error of at most 0.02.
Values may be sent and summed in bfloat16 or wider, within the bound.
No kernel may reach another device: no remote copies, remote signals or barrier semaphores. Data moves between devices by JAX's collectives and lax.ppermute only.
A program may use at most 384 MiB of HBM per device.

```python
import math
import jax
import jax.numpy as jnp
import numpy as np
from jax import lax

H = 24
D = 1536
FF = 4096
YD = 4096
CD = 1024
SEQ = 1024
TEXT = 256
BANDS = 8
ITEMS = 8


def item_shapes(key):
    sub_key = jax.random.fold_in(key, 11)
    length_key, width_key, full_key, short_key = jax.random.split(sub_key, 4)
    lengths = jax.random.randint(length_key, (ITEMS,), SEQ // 2, SEQ + 1)
    widths = jax.random.randint(width_key, (ITEMS,), 4, min(65, SEQ // 4 + 1))
    full_item = jax.random.randint(full_key, (), 0, ITEMS)
    short_item = (full_item + 1 + jax.random.randint(short_key, (), 0, ITEMS - 1)) % ITEMS
    item_ids = jnp.arange(ITEMS)
    lengths = jnp.where(item_ids == full_item, SEQ, jnp.where(item_ids == short_item, SEQ // 2, lengths))
    widths = jnp.where(item_ids == full_item, 4, widths)
    return (lengths.astype(jnp.int32), widths.astype(jnp.int32))


def draw_item_lengths(key, part):
    return item_shapes(key)[0]


def draw_positions(key, part):
    lengths, widths = item_shapes(key)
    places = jnp.arange(SEQ, dtype=jnp.int32)[None, :]
    live_slot = places < lengths[:, None]
    row_place = jnp.where(live_slot, places // widths[:, None], 0)
    col_place = jnp.where(live_slot, places % widths[:, None], 0)
    return jnp.stack([row_place, col_place], axis=1).astype(jnp.int32)


def draw_caption_mask(key, part):
    sub_key = jax.random.fold_in(key, 23)
    length_key, full_key, short_key = jax.random.split(sub_key, 3)
    text_lengths = jax.random.randint(length_key, (ITEMS,), TEXT // 4, TEXT + 1)
    full_item = jax.random.randint(full_key, (), 0, ITEMS)
    short_item = (full_item + 1 + jax.random.randint(short_key, (), 0, ITEMS - 1)) % ITEMS
    item_ids = jnp.arange(ITEMS)
    text_lengths = jnp.where(item_ids == full_item, TEXT, jnp.where(item_ids == short_item, TEXT // 4, text_lengths))
    return (jnp.arange(TEXT)[None, :] < text_lengths[:, None]).astype(jnp.int32)


def touch_ends(entries, key, smallest, largest):
    spot = [jax.random.randint(jax.random.fold_in(key, axis), (), 0, length) for axis, length in enumerate(entries.shape)]
    longest = entries.shape.index(max(entries.shape))
    neighbour = spot[:longest] + [(spot[longest] + 1) % entries.shape[longest]] + spot[longest + 1:]
    return entries.at[tuple(spot)].set(smallest).at[tuple(neighbour)].set(largest)


def level_of(key, dims, cuts, low, largest):
    level = 1.0
    for dim, parts in cuts:
        steps = jax.random.uniform(jax.random.fold_in(jax.random.fold_in(key, 6), dim), (parts,), jnp.float32, low / len(cuts), largest / len(cuts))
        level = level * jnp.repeat(jnp.exp(steps), dims[dim] // parts).reshape((-1,) + (1,) * (len(dims) - 1 - dim))
    return level


def rank_bounds(count, lean):
    weights = [(1 << 20) // math.isqrt(grade ** lean) + 1 for grade in range(1, count + 1)]
    scale = 1 + sum(weights) // (1 << 30)
    return np.cumsum(np.array([max(1, weight // scale) for weight in weights]))


def ranked(key, shape, amount, skew):
    table = rank_bounds(amount, skew)
    ticket = jax.random.randint(jax.random.fold_in(key, 1), shape, 0, int(table[amount - 1]))
    standing = jnp.searchsorted(jnp.asarray(table, jnp.int32), ticket, side="right")
    return jax.random.permutation(jax.random.fold_in(key, 2), amount)[standing].astype(jnp.int32)


def bell_draw(key, extent, spread, most, cuts=(), kind=jnp.bfloat16):
    entries = jax.random.normal(key, extent, jnp.float32) * spread
    if len(cuts) > 0:
        entries = level_of(key, extent, cuts, -0.22, 0.18) * entries
    return jnp.clip(entries, min=-most, max=most).astype(kind)


def setup_inputs(seed: int = 0) -> dict:
    streams_of = jax.random.split(jax.random.key(seed), 22)
    tokens = bell_draw(streams_of[0], (ITEMS, SEQ, D), 1.0, 6.0, ((0, 8), (1, 4)))
    caption = bell_draw(streams_of[1], (ITEMS, TEXT, YD), 1.0, 6.0, ((0, 8), (1, 4)))
    caption_mask = draw_caption_mask(jax.random.fold_in(streams_of[21], 71), 0)
    item_lengths = draw_item_lengths(jax.random.fold_in(streams_of[21], 71), 0)
    item_band = touch_ends(ranked(streams_of[4], (ITEMS,), BANDS, 2), jax.random.fold_in(streams_of[4], 3), 0, BANDS - 1).astype(jnp.int32)
    positions = draw_positions(jax.random.fold_in(streams_of[21], 71), 0)
    band_table = bell_draw(streams_of[6], (BANDS, CD), 1.0, 6.0)
    adaln_weight = bell_draw(streams_of[7], (CD, 6 * D), CD ** -0.5, 0.1875, ((0, 4),))
    adaln_bias = bell_draw(streams_of[8], (6 * D,), 0.3, 1.5, ((0, 4),))
    query_weight = bell_draw(streams_of[9], (D, D), D ** -0.5, 0.15625, ((0, 4),))
    key_weight = bell_draw(streams_of[10], (D, D), D ** -0.5, 0.15625, ((0, 4),))
    value_weight = bell_draw(streams_of[11], (D, D), D ** -0.5, 0.15625, ((0, 4),))
    outproj_weight = bell_draw(streams_of[12], (D, D), (D // 128) ** -0.5, 1.75, ((0, 4),))
    capkey_weight = bell_draw(streams_of[13], (YD, D), YD ** -0.5, 0.09375, ((0, 4),))
    capvalue_weight = bell_draw(streams_of[14], (YD, D), YD ** -0.5, 0.09375, ((0, 4),))
    norm_gains = jnp.clip(1.0 + 0.1 * jax.random.normal(streams_of[15], (5, D), jnp.float32), 0.5, 1.5).astype(jnp.bfloat16)
    head_gate = jnp.clip(jax.random.uniform(streams_of[16], (H,), jnp.float32, -1.5, 1.5), -1.5, 1.5).astype(jnp.bfloat16)
    gate_weight = bell_draw(streams_of[17], (D, FF), D ** -0.5, 0.15625, ((0, 4),))
    up_weight = bell_draw(streams_of[18], (D, FF), D ** -0.5, 0.15625, ((0, 4),))
    down_weight = bell_draw(streams_of[19], (FF, D), (FF // 4) ** -0.5, 0.1875, ((0, 4),))
    cotangent = bell_draw(streams_of[20], (ITEMS, SEQ, D), 1.0, 6.0, ((0, 8), (1, 4)))
    return {"tokens": tokens, "caption": caption, "caption_mask": caption_mask, "item_lengths": item_lengths, "item_band": item_band, "positions": positions, "band_table": band_table, "adaln_weight": adaln_weight, "adaln_bias": adaln_bias, "query_weight": query_weight, "key_weight": key_weight, "value_weight": value_weight, "outproj_weight": outproj_weight, "capkey_weight": capkey_weight, "capvalue_weight": capvalue_weight, "norm_gains": norm_gains, "head_gate": head_gate, "gate_weight": gate_weight, "up_weight": up_weight, "down_weight": down_weight, "cotangent": cotangent}


@jax.custom_vjp
def low(v):
    return lax.optimization_barrier(v.astype(jnp.bfloat16)).astype(jnp.float32)

@jax.custom_vjp
def low_back(v):
    return v

def low_keep(v):
    return (low(v), None)

def low_pass(kept, grad):
    return (grad,)

def back_keep(v):
    return (v, None)

def back_low(kept, grad):
    return (low(grad),)
low.defvjp(low_keep, low_pass)
low_back.defvjp(back_keep, back_low)
norm_eps = 1e-06
rope_base = 10000.0
masked_score = -1e+30

def highest(left_side, right_side):
    return jnp.dot(left_side, right_side, precision=lax.Precision.HIGHEST)

def rms_scale(values, gain):
    return values * lax.rsqrt(lax.optimization_barrier(jnp.mean(values * values, axis=-1, keepdims=True)) + norm_eps) * gain

def angle_table(places, quarter):
    frequency = jnp.exp(-jnp.log(rope_base) * jnp.arange(quarter, dtype=jnp.float32) / quarter)
    return places.astype(jnp.float32)[..., None] * frequency

def rotate(values, cosines, sines):
    quarter = values.shape[-1] // 4
    first_part = values[..., :quarter]
    second_part = values[..., quarter:2 * quarter]
    third_part = values[..., 2 * quarter:3 * quarter]
    fourth_part = values[..., 3 * quarter:]
    return jnp.concatenate([first_part * cosines[0] - second_part * sines[0], second_part * cosines[0] + first_part * sines[0], third_part * cosines[1] - fourth_part * sines[1], fourth_part * cosines[1] + third_part * sines[1]], axis=-1)

def attend(query_rows, key_rows, value_rows, live_slots):
    score_scale = query_rows.shape[-1] ** (-0.5)
    scores = low_back(jnp.einsum('qhd,khd->hqk', query_rows, key_rows, precision=lax.Precision.HIGHEST) * score_scale)
    scores = jnp.where(live_slots[None, None, :] > 0, scores, masked_score)
    probs = low(jax.nn.softmax(scores, axis=-1))
    return jnp.einsum('hqk,khd->qhd', probs, value_rows, precision=lax.Precision.HIGHEST)

def one_item(tokens, caption, live_slots, text_live, places, band_vector, params):
    adaln_weight, adaln_bias, query_weight, key_weight, value_weight, outproj_weight, capkey_weight, capvalue_weight, norm_gains, head_gate, gate_weight, up_weight, down_weight = params
    head_count = head_gate.shape[0]
    feature_width = tokens.shape[-1]
    head_size = feature_width // head_count
    modulation = highest(low(jax.nn.silu(band_vector))[None, :], adaln_weight)[0] + adaln_bias
    shift_mix, scale_mix, gate_mix, shift_feed, scale_feed, gate_feed = jnp.split(modulation, 6)
    row_angles = angle_table(places[0], head_size // 4)[:, None, :]
    col_angles = angle_table(places[1], head_size // 4)[:, None, :]
    cosines = (jnp.cos(row_angles), jnp.cos(col_angles))
    sines = (jnp.sin(row_angles), jnp.sin(col_angles))
    split_shape = (tokens.shape[0], head_count, head_size)
    text_shape = (caption.shape[0], head_count, head_size)
    normed_mix = low(rms_scale(tokens, norm_gains[0]) * (1.0 + scale_mix) + shift_mix)
    query_low = low(rotate(rms_scale(low_back(highest(normed_mix, query_weight)), norm_gains[1]).reshape(split_shape), cosines, sines))
    key_low = low(rotate(rms_scale(low_back(highest(normed_mix, key_weight)), norm_gains[2]).reshape(split_shape), cosines, sines))
    value_low = low(low_back(highest(normed_mix, value_weight))).reshape(split_shape)
    capkey_low = low(rms_scale(low_back(highest(caption, capkey_weight)), norm_gains[3])).reshape(text_shape)
    capvalue_low = low(low_back(highest(caption, capvalue_weight))).reshape(text_shape)
    self_part = attend(query_low, key_low, value_low, live_slots)
    cross_part = attend(query_low, capkey_low, capvalue_low, text_live)
    attended = low(low_back(self_part + jnp.tanh(head_gate)[None, :, None] * cross_part)).reshape(tokens.shape)
    branch = low_back(highest(attended, outproj_weight))
    middle = tokens + gate_mix * branch
    normed_feed = low(rms_scale(middle, norm_gains[4]) * (1.0 + scale_feed) + shift_feed)
    gate_pre = low_back(highest(normed_feed, gate_weight))
    up_pre = low_back(highest(normed_feed, up_weight))
    hidden = low(jax.nn.silu(gate_pre) * up_pre)
    ffn_out = low_back(highest(hidden, down_weight))
    return middle + gate_feed * ffn_out

def reference(tokens, caption, caption_mask, item_lengths, item_band, positions, band_table, adaln_weight, adaln_bias, query_weight, key_weight, value_weight, outproj_weight, capkey_weight, capvalue_weight, norm_gains, head_gate, gate_weight, up_weight, down_weight, cotangent):
    params = tuple((weight.astype(jnp.float32) for weight in (adaln_weight, adaln_bias, query_weight, key_weight, value_weight, outproj_weight, capkey_weight, capvalue_weight, norm_gains, head_gate, gate_weight, up_weight, down_weight)))
    token_float = tokens.astype(jnp.float32)
    caption_float = caption.astype(jnp.float32)
    live_slots = (jnp.arange(SEQ, dtype=jnp.int32)[None, :] < item_lengths[:, None]).astype(jnp.float32)
    text_live = caption_mask.astype(jnp.float32)
    band_vectors = band_table.astype(jnp.float32)[item_band]

    def forward(token_values, param_values):

        def one_step(pieces):
            return jax.checkpoint(one_item)(pieces[0], pieces[1], pieces[2], pieces[3], pieces[4], pieces[5], param_values)
        return lax.map(one_step, (token_values, caption_float, live_slots, text_live, positions, band_vectors))
    block_out, pullback = jax.vjp(forward, token_float, params)
    grad_out = cotangent.astype(jnp.float32) * live_slots[:, :, None]
    tokens_grad, param_grads = pullback(grad_out)
    return (block_out.astype(jnp.bfloat16), tokens_grad.astype(jnp.bfloat16), param_grads[0], param_grads[1], param_grads[2], param_grads[3], param_grads[4], param_grads[5], param_grads[6], param_grads[7], param_grads[8], param_grads[9], param_grads[10], param_grads[11], param_grads[12])
```

```python
import jax
import jax.numpy as jnp
from jax import lax
from jax.experimental import pallas as pl
from jax.experimental.pallas import tpu as pltpu
from jax.sharding import PartitionSpec as P

norm_eps = 1e-06
rope_base = 10000.0
masked_score = -1e30
f32 = jnp.float32
bf16 = jnp.bfloat16


def mm(left_side, right_side):
    return lax.dot_general(
        left_side, right_side, (((1,), (0,)), ((), ())), preferred_element_type=f32
    )


def mm_nt(left_side, right_side):
    return lax.dot_general(
        left_side, right_side, (((1,), (1,)), ((), ())), preferred_element_type=f32
    )


def mm_tn(left_side, right_side):
    return lax.dot_general(
        left_side, right_side, (((0,), (0,)), ((), ())), preferred_element_type=f32
    )


def rms_parts(values):
    inverse = lax.rsqrt(jnp.mean(values * values, axis=-1, keepdims=True) + norm_eps)
    return (values * inverse, inverse)


def rms_back(unit_rows, inverse, grad_unit):
    return inverse * (
        grad_unit - unit_rows * jnp.mean(grad_unit * unit_rows, axis=-1, keepdims=True)
    )


def hop(values, mask):
    count = lax.axis_size("fsdp")
    return lax.ppermute(values, "fsdp", [(i, i ^ mask) for i in range(count)])


def gather_rel(values):
    inner = hop(values, 1)
    outer = hop(values, 2)
    diagonal = hop(outer, 1)
    return [values, inner, outer, diagonal]


def scatter_rel(blocks):
    from_inner = hop(jnp.stack([blocks[1], blocks[3]]).astype(bf16), 1).astype(f32)
    kept = blocks[0].astype(f32) + from_inner[0]
    passed = (blocks[2].astype(f32) + from_inner[1]).astype(bf16)
    return kept + hop(passed, 2).astype(f32)


def swap_blocks(values, mask, count):
    rows = values.shape[0] // count
    return jnp.concatenate(
        [values[(m ^ mask) * rows : ((m ^ mask) + 1) * rows] for m in range(count)], axis=0
    )


def sum_rows_rel(values, count):
    total = values
    for mask in (1, 2, 3):
        total = total + swap_blocks(hop(values, mask), mask, count)
    return total


def reduce_dp(partial):
    data_count = lax.axis_size("dp")
    line = data_count // 2
    place = lax.axis_index("dp")
    far, near = place // 2, place % 2
    rows, columns = partial.shape[0] // data_count, partial.shape[1]
    blocks = partial.reshape(line, 2, rows, columns)
    sent = lax.dynamic_index_in_dim(blocks, 1 - near, 1, keepdims=False)
    arrived = lax.ppermute(sent, "dp", [(i, i ^ 1) for i in range(data_count)])

    def pair_sum(step):
        index = lax.rem(far + step, line)
        mine = lax.dynamic_slice(blocks, (index, near, 0, 0), (1, 1, rows, columns))[0, 0]
        other = lax.dynamic_index_in_dim(arrived, index, 0, keepdims=False)
        return mine.astype(f32) + other.astype(f32)

    total = pair_sum(0)
    for step in range(1, line):
        total = total + lax.ppermute(
            pair_sum(step).astype(bf16),
            "dp",
            [(i, ((i // 2 + step) % line) * 2 + i % 2) for i in range(data_count)],
        ).astype(f32)
    return total


def spread_rows(total, own, groups):
    count = lax.axis_size("fsdp")
    rows = total.shape[0] // count
    width = total.shape[1] // groups
    low = total.astype(bf16)
    result = jnp.zeros((rows, groups, count, width), f32)

    def put(result, piece, source):
        return lax.dynamic_update_slice(
            result, piece.astype(f32).reshape(rows, groups, 1, width), (0, 0, source, 0)
        )

    result = put(result, lax.dynamic_slice_in_dim(total, own * rows, rows, 0), own)
    for mask in (1, 2, 3):
        piece = hop(lax.dynamic_slice_in_dim(low, (own ^ mask) * rows, rows, 0), mask)
        result = put(result, piece, own ^ mask)
    result = result.reshape(rows, groups, count * width)
    return [result[:, i] for i in range(groups)]


def to_owner(total):
    data_count, count = lax.axis_size("dp"), lax.axis_size("fsdp")
    pairs = [(d * count + f, f * data_count + d) for d in range(data_count) for f in range(count)]
    return lax.ppermute(total.astype(bf16), ("dp", "fsdp"), pairs).astype(f32)


def lane_of(shape):
    return lax.broadcasted_iota(jnp.int32, shape, len(shape) - 1)


def rotate_lanes(values, cosines, sines):
    lanes = lane_of(values.shape)
    even = lax.rem(lax.div(lanes, 16), 2) == 0
    width = values.shape[-1]
    partner = jnp.where(even, pltpu.roll(values, width - 16, 1), pltpu.roll(values, 16, 1))
    return values * cosines + partner * sines


def head_lanes(values, head, spare):
    lanes = lane_of(values.shape)
    mine = (lanes < 64) if head == 0 else (lanes >= 64)
    mark = 64 if head == 0 else 0
    return jnp.where(mine, values, jnp.where(lanes == mark, spare, jnp.zeros_like(values)))


def attend_body(
    q_ref, k_ref, v_ref, qinv_ref, kinv_ref, qg_ref, kg_ref, cosq_ref, sinq_ref, cosk_ref, sink_ref,
    ck_ref, cv_ref, live_ref, text_ref, tanh_ref,
    out_ref, qlow_ref, klow_ref, vlow_ref, lse_ref,
    km, vm, cm, cvm,
):
    @pl.when(pl.program_id(1) == 0)
    def _():
        key = rotate_lanes(
            k_ref[...] * kinv_ref[...] * kg_ref[...], cosk_ref[...], sink_ref[...]
        ).astype(bf16)
        value = v_ref[...].astype(bf16)
        klow_ref[...] = key
        vlow_ref[...] = value
        one = jnp.ones((), bf16)
        for head in range(2):
            km[head] = head_lanes(key, head, live_ref[...].astype(bf16))
            vm[head] = head_lanes(value, head, one)
            cm[head] = head_lanes(ck_ref[...], head, text_ref[...].astype(bf16))
            cvm[head] = head_lanes(cv_ref[...], head, one)

    query = rotate_lanes(
        q_ref[...] * qinv_ref[...] * qg_ref[...], cosq_ref[...], sinq_ref[...]
    ).astype(bf16)
    qlow_ref[...] = query
    scaled = query * jnp.asarray(0.125, bf16)
    lanes = lane_of(out_ref.shape)
    results, stats = [], []
    for head in range(2):
        part = head_lanes(scaled, head, jnp.ones((), bf16))
        mark = 64 if head == 0 else 0

        def one_side(keys, values):
            scores = mm_nt(part, keys)
            peak = jnp.max(scores, axis=-1, keepdims=True)
            weights = jnp.exp(scores - peak).astype(bf16)
            mixed = mm(weights, values)
            amount = mixed[:, mark : mark + 1]
            stats.append(peak + jnp.log(amount))
            return mixed / amount

        own = one_side(km[head], vm[head])
        text = one_side(cm[head], cvm[head])
        results.append(own + tanh_ref[...] * text)
    out_ref[...] = jnp.where(lanes < 64, results[0], results[1]).astype(bf16)
    table = jnp.where(lanes == 0, stats[0], stats[1])
    table = jnp.where(lanes == 2, stats[2], table)
    lse_ref[...] = jnp.where(lanes == 3, stats[3], table)


def attend_forward(qkv, inverses, gains, tables, capkey, capvalue, live_bias, text_bias, tanh_lane, rows):
    seq, width = qkv.shape[0], qkv.shape[1] // 3
    pairs, text = width // 128, capkey.shape[0]
    full = lambda p, i: (0, p)
    block = lambda p, i: (i, p)
    qrow = lambda p, i: (i, 0)
    whole = lambda p, i: (0, 0)
    return pl.pallas_call(
        attend_body,
        grid=(pairs, seq // rows),
        in_specs=[
            pl.BlockSpec((rows, 128), block),
            pl.BlockSpec((seq, 128), lambda p, i: (0, p + pairs)),
            pl.BlockSpec((seq, 128), lambda p, i: (0, p + 2 * pairs)),
            pl.BlockSpec((rows, 1), qrow),
            pl.BlockSpec((seq, 1), whole),
            pl.BlockSpec((1, 128), full),
            pl.BlockSpec((1, 128), full),
            pl.BlockSpec((rows, 128), qrow),
            pl.BlockSpec((rows, 128), qrow),
            pl.BlockSpec((seq, 128), whole),
            pl.BlockSpec((seq, 128), whole),
            pl.BlockSpec((text, 128), full),
            pl.BlockSpec((text, 128), full),
            pl.BlockSpec((seq, 1), whole),
            pl.BlockSpec((text, 1), whole),
            pl.BlockSpec((1, 128), full),
        ],
        out_specs=[
            pl.BlockSpec((rows, 128), block),
            pl.BlockSpec((rows, 128), block),
            pl.BlockSpec((seq, 128), full),
            pl.BlockSpec((seq, 128), full),
            pl.BlockSpec((rows, 128), block),
        ],
        out_shape=[
            jax.ShapeDtypeStruct((seq, width), bf16),
            jax.ShapeDtypeStruct((seq, width), bf16),
            jax.ShapeDtypeStruct((seq, width), bf16),
            jax.ShapeDtypeStruct((seq, width), bf16),
            jax.ShapeDtypeStruct((seq, width), f32),
        ],
        scratch_shapes=[
            pltpu.VMEM((2, seq, 128), bf16),
            pltpu.VMEM((2, seq, 128), bf16),
            pltpu.VMEM((2, text, 128), bf16),
            pltpu.VMEM((2, text, 128), bf16),
        ],
        compiler_params=pltpu.CompilerParams(
            dimension_semantics=("arbitrary", "arbitrary"), vmem_limit_bytes=40 << 20
        ),
        cost_estimate=pl.CostEstimate(
            flops=16 * seq * (seq + text) * width,
            transcendentals=seq * (seq + text) * width // 64,
            bytes_accessed=seq * width * 24,
        ),
        name="attend_forward",
    )(
        qkv, qkv, qkv, inverses[0], inverses[1], gains[0], gains[1], tables[0], tables[1],
        tables[0], tables[1], capkey, capvalue, live_bias, text_bias, tanh_lane,
    )


def attend_back_body(
    q_ref, k_ref, v_ref, ck_ref, cv_ref, do_ref, lse_ref, cosq_ref, sinq_ref, cosk_ref, sink_ref,
    live_ref, text_ref, tanh_ref,
    dq_ref, dk_ref, dv_ref, dck_ref, dcv_ref, dtanh_ref,
    km, cm, dk, dv, dck, dcv,
):
    step = pl.program_id(1)

    @pl.when(step == 0)
    def _():
        for head in range(2):
            km[head] = head_lanes(k_ref[...], head, live_ref[...].astype(bf16))
            cm[head] = head_lanes(ck_ref[...], head, text_ref[...].astype(bf16))
        dk[...] = jnp.zeros_like(dk)
        dv[...] = jnp.zeros_like(dv)
        dck[...] = jnp.zeros_like(dck)
        dcv[...] = jnp.zeros_like(dcv)
        dtanh_ref[...] = jnp.zeros_like(dtanh_ref)

    query = q_ref[...]
    scaled = query * jnp.asarray(0.125, bf16)
    grad = do_ref[...]
    lse = lse_ref[...]
    grads = []
    for head in range(2):
        part = head_lanes(scaled, head, jnp.ones((), bf16))
        grad_part = head_lanes(grad, head, jnp.zeros((), bf16))
        lanes_tanh = tanh_ref[:, 64 * head : 64 * head + 1]

        probs = jnp.exp(mm_nt(part, km[head]) - lse[:, 2 * head : 2 * head + 1])
        dprob = mm_nt(grad_part, v_ref[...])
        total = jnp.sum(probs * dprob, axis=-1, keepdims=True)
        dscore = (probs * (dprob - total)).astype(bf16)
        probs_low = probs.astype(bf16)

        text_probs = jnp.exp(mm_nt(part, cm[head]) - lse[:, 2 * head + 1 : 2 * head + 2])
        text_dprob = mm_nt(grad_part, cv_ref[...])
        text_total = jnp.sum(text_probs * text_dprob, axis=-1, keepdims=True)
        text_dscore = (text_probs * (text_dprob - text_total) * lanes_tanh).astype(bf16)
        text_low = text_probs.astype(bf16)

        grads.append(mm(dscore, k_ref[...]) + mm(text_dscore, ck_ref[...]))

        def add(target, update):
            lanes = lane_of(target.shape)
            mine = (lanes < 64) if head == 0 else (lanes >= 64)
            target[...] += jnp.where(mine, update, jnp.zeros_like(update))

        add(dk, mm_tn(dscore, scaled))
        add(dv, mm_tn(probs_low, grad))
        add(dck, mm_tn(text_dscore, scaled))
        add(dcv, mm_tn(text_low, grad))
        add(dtanh_ref, jnp.broadcast_to(jnp.sum(text_total, axis=0, keepdims=True), dtanh_ref.shape))
    lanes = lane_of(dq_ref.shape)
    dq_ref[...] = rotate_lanes(
        jnp.where(lanes < 64, grads[0], grads[1]) * 0.125, cosq_ref[...], -sinq_ref[...]
    )

    @pl.when(step == pl.num_programs(1) - 1)
    def _():
        dk_ref[...] = rotate_lanes(dk[...], cosk_ref[...], -sink_ref[...])
        dv_ref[...] = dv[...].astype(bf16)
        dck_ref[...] = dck[...]
        dcv_ref[...] = (dcv[...] * tanh_ref[...]).astype(bf16)


def attend_backward(query, key, value, capkey, capvalue, grad, lse, tables, live_bias, text_bias, tanh_lane, rows):
    seq, width = query.shape
    pairs, text = width // 128, capkey.shape[0]
    full = lambda p, i: (0, p)
    block = lambda p, i: (i, p)
    qrow = lambda p, i: (i, 0)
    whole = lambda p, i: (0, 0)
    return pl.pallas_call(
        attend_back_body,
        grid=(pairs, seq // rows),
        in_specs=[
            pl.BlockSpec((rows, 128), block),
            pl.BlockSpec((seq, 128), full),
            pl.BlockSpec((seq, 128), full),
            pl.BlockSpec((text, 128), full),
            pl.BlockSpec((text, 128), full),
            pl.BlockSpec((rows, 128), block),
            pl.BlockSpec((rows, 128), block),
            pl.BlockSpec((rows, 128), qrow),
            pl.BlockSpec((rows, 128), qrow),
            pl.BlockSpec((seq, 128), whole),
            pl.BlockSpec((seq, 128), whole),
            pl.BlockSpec((seq, 1), whole),
            pl.BlockSpec((text, 1), whole),
            pl.BlockSpec((1, 128), full),
        ],
        out_specs=[
            pl.BlockSpec((rows, 128), block),
            pl.BlockSpec((seq, 128), full),
            pl.BlockSpec((seq, 128), full),
            pl.BlockSpec((text, 128), full),
            pl.BlockSpec((text, 128), full),
            pl.BlockSpec((8, 128), full),
        ],
        out_shape=[
            jax.ShapeDtypeStruct((seq, width), f32),
            jax.ShapeDtypeStruct((seq, width), f32),
            jax.ShapeDtypeStruct((seq, width), bf16),
            jax.ShapeDtypeStruct((text, width), f32),
            jax.ShapeDtypeStruct((text, width), bf16),
            jax.ShapeDtypeStruct((8, width), f32),
        ],
        scratch_shapes=[
            pltpu.VMEM((2, seq, 128), bf16),
            pltpu.VMEM((2, text, 128), bf16),
            pltpu.VMEM((seq, 128), f32),
            pltpu.VMEM((seq, 128), f32),
            pltpu.VMEM((text, 128), f32),
            pltpu.VMEM((text, 128), f32),
        ],
        compiler_params=pltpu.CompilerParams(
            dimension_semantics=("arbitrary", "arbitrary"), vmem_limit_bytes=40 << 20
        ),
        cost_estimate=pl.CostEstimate(
            flops=40 * seq * (seq + text) * width,
            transcendentals=seq * (seq + text) * width // 64,
            bytes_accessed=seq * width * 28,
        ),
        name="attend_backward",
    )(
        query, key, value, capkey, capvalue, grad, lse, tables[0], tables[1], tables[0], tables[1],
        live_bias, text_bias, tanh_lane,
    )


def on_device(
    tokens,
    caption,
    caption_mask,
    item_lengths,
    item_band,
    positions,
    band_table,
    adaln_weight,
    adaln_bias,
    query_weight,
    key_weight,
    value_weight,
    outproj_weight,
    capkey_weight,
    capvalue_weight,
    norm_gains,
    head_gate,
    gate_weight,
    up_weight,
    down_weight,
    cotangent,
):
    own = lax.axis_index("fsdp")
    place = lax.axis_index("dp")
    count = lax.axis_size("fsdp")
    data_count = lax.axis_size("dp")
    rows, width = tokens.shape[1:]
    seq = rows * count
    part = width // count
    head_count = head_gate.shape[0]
    head_size = width // head_count
    own_heads = head_count // count
    units = down_weight.shape[0]
    text_rows = caption.shape[1]
    text = text_rows * count
    cap_depth = capkey_weight.shape[0]

    token_own = tokens[0]
    token_all = jnp.concatenate(gather_rel(token_own), axis=0)
    caption_all = jnp.concatenate(gather_rel(caption[0]), axis=0)

    def head_columns(target):
        return jnp.concatenate(
            [
                lax.dynamic_slice_in_dim(w, target * part, part, 1)
                for w in (query_weight, key_weight, value_weight)
            ],
            axis=1,
        )

    qkv_weight = jnp.zeros((width, 3 * part), bf16)
    depth = query_weight.shape[0]
    qkv_weight = lax.dynamic_update_slice(qkv_weight, head_columns(own), (own * depth, 0))
    for mask in (1, 2, 3):
        qkv_weight = lax.dynamic_update_slice(
            qkv_weight, hop(head_columns(own ^ mask), mask), ((own ^ mask) * depth, 0)
        )

    thin = gate_weight.shape[0] // data_count

    def unit_columns(target):
        return jnp.concatenate(
            [
                lax.dynamic_slice(w, (place * thin, target * units), (thin, units))
                for w in (gate_weight, up_weight)
            ],
            axis=1,
        )

    thin_all = jnp.zeros((count, thin, 2 * units), bf16)
    thin_all = lax.dynamic_update_slice(thin_all, unit_columns(own)[None], (own, 0, 0))
    for mask in (1, 2, 3):
        thin_all = lax.dynamic_update_slice(
            thin_all, hop(unit_columns(own ^ mask), mask)[None], (own ^ mask, 0, 0)
        )
    gateup_weight = lax.all_gather(thin_all, "dp", axis=1, tiled=True).reshape(width, 2 * units)

    band_onehot = (item_band[:, None] == jnp.arange(band_table.shape[0], dtype=jnp.int32)[None, :])
    band_vector = jnp.dot(band_onehot.astype(bf16), band_table, preferred_element_type=f32)
    silu_low = jax.nn.silu(band_vector).astype(bf16)
    slice_depth = adaln_weight.shape[0]
    modulation_part = mm(
        lax.dynamic_slice_in_dim(silu_low, own * slice_depth, slice_depth, 1), adaln_weight
    )[0]
    modulation_part = modulation_part + lax.dynamic_update_slice(
        jnp.zeros_like(modulation_part), adaln_bias.astype(f32), (own * adaln_bias.shape[0],)
    )
    gains_part = lax.dynamic_update_slice(
        jnp.zeros((2, width), f32), norm_gains[0::4].astype(f32), (0, own * part)
    )
    places_part = lax.dynamic_update_slice(
        jnp.zeros((2, seq), f32), positions[0].astype(f32), (0, own * rows)
    )
    small = jnp.concatenate([modulation_part, gains_part.reshape(-1), places_part.reshape(-1)])
    small = small + hop(small, 1) + (hop(small, 2) + hop(small, 3))
    modulation = small[: 6 * width].reshape(6, 1, width)
    shift_mix, scale_mix, gate_mix, shift_feed, scale_feed, gate_feed = [modulation[i] for i in range(6)]
    gain_mix = small[6 * width : 7 * width][None]
    gain_feed = small[7 * width : 8 * width][None]
    places = small[8 * width :].reshape(2, count, rows)
    order = own ^ jnp.arange(count, dtype=jnp.int32)
    places_rel = places[:, order].reshape(2, seq)
    slots_rel = (order[:, None] * rows + jnp.arange(rows, dtype=jnp.int32)[None]).reshape(seq)
    text_slots = (
        order[:, None] * text_rows + jnp.arange(text_rows, dtype=jnp.int32)[None]
    ).reshape(text)
    live_bias = jnp.where(slots_rel < item_lengths[0], 0.0, masked_score).astype(f32)[:, None]
    text_live = caption_mask[0].reshape(count, text_rows)[order].reshape(text) > 0
    text_bias = jnp.where(text_live, 0.0, masked_score).astype(f32)[:, None]
    quarter = head_size // 4
    lane = jnp.arange(128, dtype=jnp.int32)
    frequency = jnp.exp(-jnp.log(rope_base) * (lane % quarter).astype(f32) / quarter)[None]
    by_row = (lane % head_size < 2 * quarter)[None]
    angles = jnp.where(by_row, places_rel[0][:, None], places_rel[1][:, None]) * frequency
    sign = jnp.where((lane // quarter) % 2 == 0, -1.0, 1.0).astype(f32)[None]
    tables = (jnp.cos(angles), jnp.sin(angles) * sign)

    caption_part = lax.dynamic_slice_in_dim(caption_all, own * cap_depth, cap_depth, 1)
    cap_partial = jnp.concatenate(
        [mm(caption_part, capkey_weight).astype(bf16), mm(caption_part, capvalue_weight).astype(bf16)],
        axis=0,
    )

    def cap_columns(mask):
        return lax.dynamic_slice_in_dim(cap_partial, (own ^ mask) * part, part, 1)

    def align(values, mask):
        return jnp.concatenate(
            [swap_blocks(values[:text], mask, count), swap_blocks(values[text:], mask, count)], axis=0
        )

    cap_inner = hop(jnp.stack([cap_columns(1), cap_columns(3)]), 1)
    cap_kept = cap_columns(0).astype(f32) + align(cap_inner[0], 1).astype(f32)
    cap_passed = (cap_columns(2).astype(f32) + align(cap_inner[1], 1).astype(f32)).astype(bf16)
    cap_raw = cap_kept + align(hop(cap_passed, 2), 2).astype(f32)
    capkey_raw, capvalue_low = cap_raw[:text], cap_raw[text:].astype(bf16)
    cap_square = sum_rows_rel(jnp.sum(capkey_raw * capkey_raw, axis=-1, keepdims=True), count)
    capkey_inverse = lax.rsqrt(cap_square / width + norm_eps)
    capkey_unit = capkey_raw * capkey_inverse
    own_gains = norm_gains.astype(f32)
    capkey_low = (capkey_unit * own_gains[3:4]).astype(bf16)

    token_float_all = token_all.astype(f32)
    unit_all, _ = rms_parts(token_float_all)
    normed_all = (unit_all * gain_mix * (1.0 + scale_mix) + shift_mix).astype(bf16)
    qkv = mm(normed_all, qkv_weight)
    squares = jnp.concatenate(
        [
            jnp.sum(jnp.square(qkv[:, :part]), axis=-1, keepdims=True),
            jnp.sum(jnp.square(qkv[:, part : 2 * part]), axis=-1, keepdims=True),
        ],
        axis=1,
    )
    squares = sum_rows_rel(squares, count)
    inverses = lax.rsqrt(squares / width + norm_eps)
    query_inverse, key_inverse = inverses[:, :1], inverses[:, 1:]
    tanh_gate = jnp.tanh(head_gate.astype(f32))
    own_tanh = lax.dynamic_slice_in_dim(tanh_gate, own * own_heads, own_heads, 0)
    tanh_lane = jnp.repeat(own_tanh, head_size)[None]
    block_rows = 256 if seq % 256 == 0 else seq
    attended, query_low, key_low, value_low, lse = attend_forward(
        qkv, (query_inverse, key_inverse), (own_gains[1:2], own_gains[2:3]), tables,
        capkey_low, capvalue_low, live_bias, text_bias, tanh_lane, block_rows,
    )

    def split_rel(values):
        return [values[m * rows : (m + 1) * rows] for m in range(count)]

    branch = scatter_rel(split_rel(mm(attended, outproj_weight).astype(bf16)))
    token_float = token_own.astype(f32)
    middle = token_float + gate_mix * branch

    query_live = (own * rows + jnp.arange(rows, dtype=jnp.int32)) < item_lengths[0]
    grad_out = cotangent[0].astype(f32) * query_live[:, None].astype(f32)
    grad_ffn_all = jnp.concatenate(gather_rel((gate_feed * grad_out).astype(bf16)), axis=0)
    grad_hidden = mm_nt(grad_ffn_all, down_weight)

    unit_feed, inverse_feed = rms_parts(middle)
    normed_feed = (unit_feed * gain_feed * (1.0 + scale_feed) + shift_feed).astype(bf16)
    feed_all = jnp.concatenate(gather_rel(normed_feed), axis=0)
    gate_pre = mm(feed_all, gateup_weight[:, :units])
    up_pre = mm(feed_all, gateup_weight[:, units:])
    gate_sigmoid = jax.nn.sigmoid(gate_pre)
    gate_silu = gate_pre * gate_sigmoid
    hidden = (gate_silu * up_pre).astype(bf16)
    silu_slope = gate_sigmoid * (1.0 + gate_pre * (1.0 - gate_sigmoid))
    grad_gateup = jnp.concatenate(
        [(grad_hidden * up_pre * silu_slope).astype(bf16), (grad_hidden * gate_silu).astype(bf16)],
        axis=1,
    )
    grad_normfeed = scatter_rel(split_rel(mm_nt(grad_gateup, gateup_weight).astype(bf16)))
    down_sum = reduce_dp(mm_tn(hidden, grad_ffn_all).astype(bf16))
    gateup_sum = reduce_dp(mm_tn(feed_all, grad_gateup).astype(bf16))
    ffn_out = scatter_rel(split_rel(mm(hidden, down_weight).astype(bf16)))
    block_out = (middle + gate_feed * ffn_out).astype(bf16)
    dgate_feed = jnp.sum(grad_out * ffn_out, axis=0)

    dshift_feed = jnp.sum(grad_normfeed, axis=0)
    dscale_feed = jnp.sum(grad_normfeed * (unit_feed * gain_feed), axis=0)
    grad_scaledfeed = grad_normfeed * (1.0 + scale_feed)
    gain_feed_grad = jnp.sum(grad_scaledfeed * unit_feed, axis=0)
    grad_middle = grad_out + rms_back(unit_feed, inverse_feed, grad_scaledfeed * gain_feed)
    dgate_mix = jnp.sum(grad_middle * branch, axis=0)

    grad_branch_all = jnp.concatenate(gather_rel((gate_mix * grad_middle).astype(bf16)), axis=0)
    grad_attended = mm_nt(grad_branch_all, outproj_weight).astype(bf16)
    outproj_sum = reduce_dp(mm_tn(attended, grad_branch_all).astype(bf16))
    query_unrot, key_unrot, grad_value, dcapkey, grad_capvalue, dtanh = attend_backward(
        query_low, key_low, value_low, capkey_low, capvalue_low, grad_attended, lse, tables,
        live_bias, text_bias, tanh_lane, block_rows,
    )
    capkey_scaled = dcapkey * own_gains[3:4]
    cap_dot = sum_rows_rel(jnp.sum(capkey_scaled * capkey_unit, axis=-1, keepdims=True), count)
    grad_capkey = (
        capkey_inverse * (capkey_scaled - capkey_unit * (cap_dot / width))
    ).astype(bf16)
    gain_capkey_grad = jnp.sum(dcapkey * capkey_unit, axis=0)
    grad_cap = jnp.concatenate([grad_capkey, grad_capvalue], axis=1)
    cap_sum = reduce_dp(mm_tn(caption_all, grad_cap).astype(bf16))

    query_unit = qkv[:, :part] * query_inverse
    key_unit = qkv[:, part : 2 * part] * key_inverse
    query_scaled = query_unrot * own_gains[1:2]
    key_scaled = key_unrot * own_gains[2:3]
    dots = sum_rows_rel(
        jnp.concatenate(
            [
                jnp.sum(query_scaled * query_unit, axis=-1, keepdims=True),
                jnp.sum(key_scaled * key_unit, axis=-1, keepdims=True),
            ],
            axis=1,
        ),
        count,
    )
    gain_query_grad = jnp.sum(query_unrot * query_unit, axis=0)
    gain_key_grad = jnp.sum(key_unrot * key_unit, axis=0)
    grad_qkv = jnp.concatenate(
        [
            (query_inverse * (query_scaled - query_unit * (dots[:, :1] / width))).astype(bf16),
            (key_inverse * (key_scaled - key_unit * (dots[:, 1:] / width))).astype(bf16),
            grad_value,
        ],
        axis=1,
    )
    qkv_sum = reduce_dp(mm_tn(normed_all, grad_qkv).astype(bf16))
    grad_normmix = scatter_rel(split_rel(mm_nt(grad_qkv, qkv_weight).astype(bf16)))

    unit_mix, inverse_mix = rms_parts(token_float)
    dshift_mix = jnp.sum(grad_normmix, axis=0)
    dscale_mix = jnp.sum(grad_normmix * (unit_mix * gain_mix), axis=0)
    grad_scaledmix = grad_normmix * (1.0 + scale_mix)
    gain_mix_grad = jnp.sum(grad_scaledmix * unit_mix, axis=0)
    tokens_grad = (
        grad_middle + rms_back(unit_mix, inverse_mix, grad_scaledmix * gain_mix)
    ).astype(bf16)

    own_rows = jnp.zeros((3, width), f32)
    own_rows = lax.dynamic_update_slice(
        own_rows, jnp.stack([gain_query_grad, gain_key_grad, gain_capkey_grad]), (0, own * part)
    )
    gate_sums = lax.dynamic_update_slice(
        jnp.zeros((head_count,), f32), dtanh[0, ::head_size], (own * own_heads,)
    )
    sums = jnp.concatenate([gain_mix_grad, own_rows.reshape(-1), gain_feed_grad, gate_sums])
    grad_modulation = jnp.concatenate(
        [dshift_mix, dscale_mix, dgate_mix, dshift_feed, dscale_feed, dgate_feed]
    )
    message = jnp.concatenate([grad_modulation, sums])
    message = message + hop(message, 1) + (hop(message, 2) + hop(message, 3))
    message = jnp.concatenate([message, silu_low[0].astype(f32)])
    line = data_count // 2
    both = jnp.stack(
        [message, lax.ppermute(message, "dp", [(i, i ^ 1) for i in range(data_count)])]
    )
    gathered = [both]
    for step in range(1, line):
        gathered.append(
            lax.ppermute(
                both,
                "dp",
                [(i, ((i // 2 + step) % line) * 2 + i % 2) for i in range(data_count)],
            )
        )
    gathered = jnp.concatenate(gathered, axis=0)
    mod_width = 6 * width
    modulation_rows = gathered[:, :mod_width]
    totals = jnp.sum(gathered[:, mod_width : mod_width + sums.shape[0]], axis=0)
    silu_rows = gathered[:, mod_width + sums.shape[0] :]
    owner = place * count + own
    devices = count * data_count
    cd_rows = silu_rows.shape[1] // devices
    adaln_wgrad = lax.dot_general(
        lax.dynamic_slice_in_dim(silu_rows, owner * cd_rows, cd_rows, 1),
        modulation_rows,
        (((0,), (0,)), ((), ())),
        precision=lax.Precision.HIGHEST,
        preferred_element_type=f32,
    )
    bias_rows = mod_width // devices
    adaln_bgrad = lax.dynamic_slice_in_dim(
        jnp.sum(modulation_rows, axis=0), owner * bias_rows, bias_rows, 0
    )
    gains_grad = lax.dynamic_slice_in_dim(
        totals[: 5 * width].reshape(5, width), owner * (width // devices), width // devices, 1
    )
    headgate_grad = totals[5 * width :] * (1.0 - tanh_gate * tanh_gate)

    query_grad, key_grad, value_grad = spread_rows(qkv_sum, own, 3)
    gate_grad, up_grad = spread_rows(gateup_sum, own, 2)
    capkey_grad, capvalue_grad = spread_rows(cap_sum, own, 2)
    down_grad = to_owner(down_sum)
    outproj_grad = to_owner(outproj_sum)
    return (
        block_out[None],
        tokens_grad[None],
        adaln_wgrad,
        adaln_bgrad,
        query_grad,
        key_grad,
        value_grad,
        outproj_grad,
        capkey_grad,
        capvalue_grad,
        gains_grad,
        headgate_grad,
        gate_grad,
        up_grad,
        down_grad,
    )


def solution(mesh):
    return jax.shard_map(
        on_device,
        mesh=mesh,
        in_specs=(
            P("dp", "fsdp", None),
            P("dp", "fsdp", None),
            P("dp", None),
            P("dp"),
            P("dp"),
            P("dp", None, "fsdp"),
            P(),
            P("fsdp", None),
            P("fsdp"),
            P("fsdp", None),
            P("fsdp", None),
            P("fsdp", None),
            P("fsdp", None),
            P("fsdp", None),
            P("fsdp", None),
            P(None, "fsdp"),
            P(),
            P("fsdp", None),
            P("fsdp", None),
            P("fsdp", None),
            P("dp", "fsdp", None),
        ),
        out_specs=(
            P("dp", "fsdp", None),
            P("dp", "fsdp", None),
            P(("dp", "fsdp"), None),
            P(("dp", "fsdp")),
            P(("dp", "fsdp"), None),
            P(("dp", "fsdp"), None),
            P(("dp", "fsdp"), None),
            P(("dp", "fsdp"), None),
            P(("dp", "fsdp"), None),
            P(("dp", "fsdp"), None),
            P(None, ("dp", "fsdp")),
            P(),
            P(("dp", "fsdp"), None),
            P(("dp", "fsdp"), None),
            P(("dp", "fsdp"), None),
        ),
        check_vma=False,
    )
```

```python
import jax
import jax.numpy as jnp
from jax import lax
from jax.experimental import pallas as pl
from jax.experimental.pallas import tpu as pltpu
from jax.sharding import PartitionSpec as P

norm_eps = 1e-06
rope_base = 10000.0
masked_score = -1e30
f32 = jnp.float32
bf16 = jnp.bfloat16


def mm(left_side, right_side):
    return lax.dot_general(
        left_side, right_side, (((1,), (0,)), ((), ())), preferred_element_type=f32
    )


def mm_nt(left_side, right_side):
    return lax.dot_general(
        left_side, right_side, (((1,), (1,)), ((), ())), preferred_element_type=f32
    )


def mm_tn(left_side, right_side):
    return lax.dot_general(
        left_side, right_side, (((0,), (0,)), ((), ())), preferred_element_type=f32
    )


def rms_parts(values):
    inverse = lax.rsqrt(jnp.mean(values * values, axis=-1, keepdims=True) + norm_eps)
    return (values * inverse, inverse)


def rms_back(unit_rows, inverse, grad_unit):
    return inverse * (
        grad_unit - unit_rows * jnp.mean(grad_unit * unit_rows, axis=-1, keepdims=True)
    )


def hop(values, mask):
    count = lax.axis_size("fsdp")
    return lax.ppermute(values, "fsdp", [(i, i ^ mask) for i in range(count)])


def gather_rel(values):
    two = jnp.stack([values, hop(values, 2)])
    other = hop(two, 1)
    return [values, other[0], two[1], other[1]]


def scatter_rel(blocks):
    arrived = hop(jnp.stack([blocks[3], blocks[1]]), 1)
    passed = hop((blocks[2].astype(f32) + arrived[0].astype(f32)).astype(bf16), 2)
    return blocks[0].astype(f32) + arrived[1].astype(f32) + passed.astype(f32)


def trade_rel(blocks, middle=None):
    far = hop(jnp.stack([blocks[2], blocks[3]]), 2)
    if middle is not None:
        far = middle(far)
    beside = hop(jnp.stack([blocks[1], far[1]]), 1)
    return [blocks[0], beside[0], far[0], beside[1]]


def swap_blocks(values, mask, count):
    rows = values.shape[0] // count
    return jnp.concatenate(
        [values[(m ^ mask) * rows : ((m ^ mask) + 1) * rows] for m in range(count)], axis=0
    )


def sum_rows_rel(columns, count):
    rows = columns[0].shape[0]
    total = jnp.concatenate(columns)
    for mask in (1, 2):
        arrived = hop(total, mask)
        total = total + jnp.concatenate(
            [swap_blocks(arrived[i * rows : (i + 1) * rows], mask, count) for i in range(len(columns))]
        )
    return [total[i * rows : (i + 1) * rows] for i in range(len(columns))]


def natural_order(pieces, own):
    far, near = own // 2, own % 2
    mixed = [[jnp.where(near == 0, pieces[2 * i + j], pieces[2 * i + 1 - j]) for j in range(2)] for i in range(2)]
    return [jnp.where(far == 0, mixed[i][j], mixed[1 - i][j]) for i in range(2) for j in range(2)]


def join(*values):
    return lax.optimization_barrier(values)


def dp_bits():
    return lax.axis_size("dp").bit_length() - 1


def dp_hop(values, bit):
    count = lax.axis_size("dp")
    return lax.ppermute(values, "dp", [(i, i ^ (1 << bit)) for i in range(count)])


def dp_place(bit):
    return (lax.axis_index("dp") >> bit) & 1


def pick(values, axis, index):
    return lax.dynamic_index_in_dim(values, index, axis, keepdims=False)


def dp_first(partial):
    bits = dp_bits()
    blocks = partial.reshape((2,) * bits + (partial.shape[0] >> bits, partial.shape[1]))
    sent = pick(blocks, bits - 1, 1 - dp_place(0))
    return (pick(blocks, bits - 1, dp_place(0)), dp_hop(sent, 0))


def dp_sums(state, bit):
    kept, arrived = state
    axis = dp_bits() - 1 - bit

    def half(index):
        return (
            pick(kept, axis, index).astype(f32) + pick(arrived, axis, index).astype(f32)
        ).astype(bf16)

    return (half(dp_place(bit)), half(1 - dp_place(bit)))


def dp_next(state, bit):
    kept, sent = dp_sums(state, bit)
    return (kept, dp_hop(sent, bit))


def dp_total(state):
    return state[0].astype(f32) + state[1].astype(f32)


def dp_rest_from(state, start):
    for bit in range(start, dp_bits()):
        state = dp_next(state, bit)
    return dp_total(state)


def dp_rest(state):
    return dp_rest_from(state, 1)


def cap_axes(top):
    return (top - 1,) + tuple(range(top - 1)) + (top,)


def spread_rows(totals, own):
    count = lax.axis_size("fsdp")
    low = jnp.concatenate([total.astype(bf16) for total in totals], axis=1)
    rows = low.shape[0] // count
    pieces = trade_rel(
        [lax.dynamic_slice_in_dim(low, (own ^ m) * rows, rows, 0) for m in range(count)]
    )
    results, start = [], 0
    for total in totals:
        width = total.shape[1]
        part = [piece[:, start : start + width] for piece in pieces]
        results.append(jnp.concatenate(natural_order(part, own), axis=1).astype(f32))
        start += width
    return results


def to_owner(total):
    data_count, count = lax.axis_size("dp"), lax.axis_size("fsdp")
    pairs = [(d * count + f, f * data_count + d) for d in range(data_count) for f in range(count)]
    return lax.ppermute(total.astype(bf16), ("dp", "fsdp"), pairs).astype(f32)


def lane_of(shape):
    return lax.broadcasted_iota(jnp.int32, shape, len(shape) - 1)


def rotate_lanes(values, cosines, sines):
    lanes = lane_of(values.shape)
    even = lax.rem(lax.div(lanes, 16), 2) == 0
    width = values.shape[-1]
    partner = jnp.where(even, pltpu.roll(values, width - 16, 1), pltpu.roll(values, 16, 1))
    return values * cosines + partner * sines


def head_lanes(values, head, spare):
    lanes = lane_of(values.shape)
    mine = (lanes < 64) if head == 0 else (lanes >= 64)
    mark = 64 if head == 0 else 0
    return jnp.where(mine, values, jnp.where(lanes == mark, spare, jnp.zeros_like(values)))


def attend_body(
    q_ref, k_ref, v_ref, qinv_ref, kinv_ref, qg_ref, kg_ref, cosq_ref, sinq_ref, cosk_ref, sink_ref,
    ck_ref, cv_ref, live_ref, text_ref, tanh_ref,
    out_ref, qlow_ref, klow_ref, vlow_ref, lse_ref,
    km, vm, cm, cvm,
):
    @pl.when(pl.program_id(1) == 0)
    def _():
        key = rotate_lanes(
            k_ref[...] * kinv_ref[...] * kg_ref[...], cosk_ref[...], sink_ref[...]
        ).astype(bf16)
        value = v_ref[...].astype(bf16)
        klow_ref[...] = key
        vlow_ref[...] = value
        one = jnp.ones((), bf16)
        for head in range(2):
            km[head] = head_lanes(key, head, live_ref[...].astype(bf16))
            vm[head] = head_lanes(value, head, one)
            cm[head] = head_lanes(ck_ref[...], head, text_ref[...].astype(bf16))
            cvm[head] = head_lanes(cv_ref[...], head, one)

    query = rotate_lanes(
        q_ref[...] * qinv_ref[...] * qg_ref[...], cosq_ref[...], sinq_ref[...]
    ).astype(bf16)
    qlow_ref[...] = query
    scaled = query * jnp.asarray(0.125, bf16)
    lanes = lane_of(out_ref.shape)
    results, stats = [], []
    for head in range(2):
        part = head_lanes(scaled, head, jnp.ones((), bf16))
        mark = 64 if head == 0 else 0

        def one_side(keys, values):
            scores = mm_nt(part, keys)
            peak = jnp.max(scores, axis=-1, keepdims=True)
            weights = jnp.exp(scores - peak).astype(bf16)
            mixed = mm(weights, values)
            amount = mixed[:, mark : mark + 1]
            stats.append(peak + jnp.log(amount))
            return mixed / amount

        own = one_side(km[head], vm[head])
        text = one_side(cm[head], cvm[head])
        results.append(own + tanh_ref[...] * text)
    out_ref[...] = jnp.where(lanes < 64, results[0], results[1]).astype(bf16)
    table = jnp.where(lanes == 0, stats[0], stats[1])
    table = jnp.where(lanes == 2, stats[2], table)
    lse_ref[...] = jnp.where(lanes == 3, stats[3], table)


def attend_forward(qkv, inverses, gains, tables, capkey, capvalue, live_bias, text_bias, tanh_lane, rows):
    seq, width = qkv.shape[0], qkv.shape[1] // 3
    pairs, text = width // 128, capkey.shape[0]
    full = lambda p, i: (0, p)
    block = lambda p, i: (i, p)
    qrow = lambda p, i: (i, 0)
    whole = lambda p, i: (0, 0)
    return pl.pallas_call(
        attend_body,
        grid=(pairs, seq // rows),
        in_specs=[
            pl.BlockSpec((rows, 128), block),
            pl.BlockSpec((seq, 128), lambda p, i: (0, p + pairs)),
            pl.BlockSpec((seq, 128), lambda p, i: (0, p + 2 * pairs)),
            pl.BlockSpec((rows, 1), qrow),
            pl.BlockSpec((seq, 1), whole),
            pl.BlockSpec((1, 128), full),
            pl.BlockSpec((1, 128), full),
            pl.BlockSpec((rows, 128), qrow),
            pl.BlockSpec((rows, 128), qrow),
            pl.BlockSpec((seq, 128), whole),
            pl.BlockSpec((seq, 128), whole),
            pl.BlockSpec((text, 128), full),
            pl.BlockSpec((text, 128), full),
            pl.BlockSpec((seq, 1), whole),
            pl.BlockSpec((text, 1), whole),
            pl.BlockSpec((1, 128), full),
        ],
        out_specs=[
            pl.BlockSpec((rows, 128), block),
            pl.BlockSpec((rows, 128), block),
            pl.BlockSpec((seq, 128), full),
            pl.BlockSpec((seq, 128), full),
            pl.BlockSpec((rows, 128), block),
        ],
        out_shape=[
            jax.ShapeDtypeStruct((seq, width), bf16),
            jax.ShapeDtypeStruct((seq, width), bf16),
            jax.ShapeDtypeStruct((seq, width), bf16),
            jax.ShapeDtypeStruct((seq, width), bf16),
            jax.ShapeDtypeStruct((seq, width), f32),
        ],
        scratch_shapes=[
            pltpu.VMEM((2, seq, 128), bf16),
            pltpu.VMEM((2, seq, 128), bf16),
            pltpu.VMEM((2, text, 128), bf16),
            pltpu.VMEM((2, text, 128), bf16),
        ],
        compiler_params=pltpu.CompilerParams(
            dimension_semantics=("arbitrary", "arbitrary"), vmem_limit_bytes=40 << 20
        ),
        cost_estimate=pl.CostEstimate(
            flops=16 * seq * (seq + text) * width,
            transcendentals=seq * (seq + text) * width // 64,
            bytes_accessed=seq * width * 24,
        ),
        name="attend_forward",
    )(
        qkv, qkv, qkv, inverses[0], inverses[1], gains[0], gains[1], tables[0], tables[1],
        tables[0], tables[1], capkey, capvalue, live_bias, text_bias, tanh_lane,
    )


def text_back_body(
    q_ref, ck_ref, cv_ref, do_ref, lse_ref, text_ref, tanh_ref,
    dq_ref, dck_ref, dcv_ref, dtanh_ref,
    cm, dck, dcv,
):
    step = pl.program_id(1)

    @pl.when(step == 0)
    def _():
        for head in range(2):
            cm[head] = head_lanes(ck_ref[...], head, text_ref[...].astype(bf16))
        dck[...] = jnp.zeros_like(dck)
        dcv[...] = jnp.zeros_like(dcv)
        dtanh_ref[...] = jnp.zeros_like(dtanh_ref)

    scaled = q_ref[...] * jnp.asarray(0.125, bf16)
    grad = do_ref[...]
    lse = lse_ref[...]
    grads = []
    for head in range(2):
        part = head_lanes(scaled, head, jnp.ones((), bf16))
        grad_part = head_lanes(grad, head, jnp.zeros((), bf16))
        gate = tanh_ref[:, 64 * head : 64 * head + 1]
        probs = jnp.exp(mm_nt(part, cm[head]) - lse[:, 2 * head + 1 : 2 * head + 2])
        dprob = mm_nt(grad_part, cv_ref[...])
        total = jnp.sum(probs * dprob, axis=-1, keepdims=True)
        dscore = (probs * ((dprob - total) * gate)).astype(bf16)
        grads.append(mm(dscore, ck_ref[...]))

        def add(target, update):
            lanes = lane_of(target.shape)
            mine = (lanes < 64) if head == 0 else (lanes >= 64)
            target[...] += jnp.where(mine, update, jnp.zeros_like(update))

        add(dck, mm_tn(dscore, scaled))
        add(dcv, mm_tn(probs.astype(bf16), grad))
        add(dtanh_ref, jnp.broadcast_to(jnp.sum(total, axis=0, keepdims=True), dtanh_ref.shape))
    lanes = lane_of(dq_ref.shape)
    dq_ref[...] = jnp.where(lanes < 64, grads[0], grads[1])

    @pl.when(step == pl.num_programs(1) - 1)
    def _():
        dck_ref[...] = dck[...]
        dcv_ref[...] = (dcv[...] * tanh_ref[...]).astype(bf16)


def text_backward(query, capkey, capvalue, grad, lse, text_bias, tanh_lane, rows):
    seq, width = query.shape
    pairs, text = width // 128, capkey.shape[0]
    full = lambda p, i: (0, p)
    block = lambda p, i: (i, p)
    whole = lambda p, i: (0, 0)
    return pl.pallas_call(
        text_back_body,
        grid=(pairs, seq // rows),
        in_specs=[
            pl.BlockSpec((rows, 128), block),
            pl.BlockSpec((text, 128), full),
            pl.BlockSpec((text, 128), full),
            pl.BlockSpec((rows, 128), block),
            pl.BlockSpec((rows, 128), block),
            pl.BlockSpec((text, 1), whole),
            pl.BlockSpec((1, 128), full),
        ],
        out_specs=[
            pl.BlockSpec((rows, 128), block),
            pl.BlockSpec((text, 128), full),
            pl.BlockSpec((text, 128), full),
            pl.BlockSpec((8, 128), full),
        ],
        out_shape=[
            jax.ShapeDtypeStruct((seq, width), f32),
            jax.ShapeDtypeStruct((text, width), f32),
            jax.ShapeDtypeStruct((text, width), bf16),
            jax.ShapeDtypeStruct((8, width), f32),
        ],
        scratch_shapes=[
            pltpu.VMEM((2, text, 128), bf16),
            pltpu.VMEM((text, 128), f32),
            pltpu.VMEM((text, 128), f32),
        ],
        compiler_params=pltpu.CompilerParams(
            dimension_semantics=("arbitrary", "arbitrary"), vmem_limit_bytes=40 << 20
        ),
        cost_estimate=pl.CostEstimate(
            flops=40 * seq * text * width,
            transcendentals=seq * text * width // 64,
            bytes_accessed=seq * width * 16,
        ),
        name="text_backward",
    )(query, capkey, capvalue, grad, lse, text_bias, tanh_lane)


def self_back_body(
    q_ref, k_ref, v_ref, do_ref, lse_ref, dqt_ref, cosq_ref, sinq_ref, cosk_ref, sink_ref, live_ref,
    dq_ref, dk_ref, dv_ref,
    km, dk, dv,
):
    step = pl.program_id(1)

    @pl.when(step == 0)
    def _():
        for head in range(2):
            km[head] = head_lanes(k_ref[...], head, live_ref[...].astype(bf16))
        dk[...] = jnp.zeros_like(dk)
        dv[...] = jnp.zeros_like(dv)

    scaled = q_ref[...] * jnp.asarray(0.125, bf16)
    grad = do_ref[...]
    lse = lse_ref[...]
    grads = []
    for head in range(2):
        part = head_lanes(scaled, head, jnp.ones((), bf16))
        grad_part = head_lanes(grad, head, jnp.zeros((), bf16))
        probs = jnp.exp(mm_nt(part, km[head]) - lse[:, 2 * head : 2 * head + 1])
        dprob = mm_nt(grad_part, v_ref[...])
        total = jnp.sum(probs * dprob, axis=-1, keepdims=True)
        dscore = (probs * (dprob - total)).astype(bf16)
        grads.append(mm(dscore, k_ref[...]))

        def add(target, update):
            lanes = lane_of(target.shape)
            mine = (lanes < 64) if head == 0 else (lanes >= 64)
            target[...] += jnp.where(mine, update, jnp.zeros_like(update))

        add(dk, mm_tn(dscore, scaled))
        add(dv, mm_tn(probs.astype(bf16), grad))
    lanes = lane_of(dq_ref.shape)
    dq_ref[...] = rotate_lanes(
        (jnp.where(lanes < 64, grads[0], grads[1]) + dqt_ref[...]) * 0.125,
        cosq_ref[...],
        -sinq_ref[...],
    )

    @pl.when(step == pl.num_programs(1) - 1)
    def _():
        dk_ref[...] = rotate_lanes(dk[...], cosk_ref[...], -sink_ref[...])
        dv_ref[...] = dv[...].astype(bf16)


def self_backward(query, key, value, grad, lse, dquery_text, tables, live_bias, rows):
    seq, width = query.shape
    pairs = width // 128
    full = lambda p, i: (0, p)
    block = lambda p, i: (i, p)
    qrow = lambda p, i: (i, 0)
    whole = lambda p, i: (0, 0)
    return pl.pallas_call(
        self_back_body,
        grid=(pairs, seq // rows),
        in_specs=[
            pl.BlockSpec((rows, 128), block),
            pl.BlockSpec((seq, 128), full),
            pl.BlockSpec((seq, 128), full),
            pl.BlockSpec((rows, 128), block),
            pl.BlockSpec((rows, 128), block),
            pl.BlockSpec((rows, 128), block),
            pl.BlockSpec((rows, 128), qrow),
            pl.BlockSpec((rows, 128), qrow),
            pl.BlockSpec((seq, 128), whole),
            pl.BlockSpec((seq, 128), whole),
            pl.BlockSpec((seq, 1), whole),
        ],
        out_specs=[
            pl.BlockSpec((rows, 128), block),
            pl.BlockSpec((seq, 128), full),
            pl.BlockSpec((seq, 128), full),
        ],
        out_shape=[
            jax.ShapeDtypeStruct((seq, width), f32),
            jax.ShapeDtypeStruct((seq, width), f32),
            jax.ShapeDtypeStruct((seq, width), bf16),
        ],
        scratch_shapes=[
            pltpu.VMEM((2, seq, 128), bf16),
            pltpu.VMEM((seq, 128), f32),
            pltpu.VMEM((seq, 128), f32),
        ],
        compiler_params=pltpu.CompilerParams(
            dimension_semantics=("arbitrary", "arbitrary"), vmem_limit_bytes=40 << 20
        ),
        cost_estimate=pl.CostEstimate(
            flops=40 * seq * seq * width,
            transcendentals=seq * seq * width // 64,
            bytes_accessed=seq * width * 28,
        ),
        name="self_backward",
    )(query, key, value, grad, lse, dquery_text, tables[0], tables[1], tables[0], tables[1], live_bias)


def feed_body(x0_ref, x1_ref, g0_ref, g1_ref, gate_ref, up_ref, down_ref, hidden_ref, grads_ref):
    step = pl.program_id(0)
    block = down_ref.shape[0]
    units = grads_ref.shape[1] // 2
    rows_in = jnp.concatenate([x0_ref[...], x1_ref[...]], axis=0)
    grads_in = jnp.concatenate([g0_ref[...], g1_ref[...]], axis=0)
    gate = mm(rows_in, gate_ref[...])
    up = mm(rows_in, up_ref[...])
    grad_hidden = mm_nt(grads_in, down_ref[...])
    sigmoid = 1.0 / (1.0 + jnp.exp(-gate))
    silu = gate * sigmoid
    hidden_ref[...] = (silu * up).astype(bf16)
    start = pl.multiple_of(step * block, block)
    grads_ref[:, pl.ds(start, block)] = (
        grad_hidden * up * (sigmoid * (1.0 + gate * (1.0 - sigmoid)))
    ).astype(bf16)
    grads_ref[:, pl.ds(pl.multiple_of(units + start, block), block)] = (grad_hidden * silu).astype(bf16)


def feed_forward(rows_in, grads_in, gateup, down, units_block):
    rows, width = rows_in[0].shape
    units = down.shape[0]
    steps = units // units_block
    whole = pl.BlockSpec((rows, width), lambda j: (0, 0))
    return pl.pallas_call(
        feed_body,
        grid=(steps,),
        in_specs=[whole] * 4
        + [
            pl.BlockSpec((width, units_block), lambda j: (0, j)),
            pl.BlockSpec((width, units_block), lambda j: (0, j + steps)),
            pl.BlockSpec((units_block, width), lambda j: (j, 0)),
        ],
        out_specs=[
            pl.BlockSpec((2 * rows, units_block), lambda j: (0, j)),
            pl.BlockSpec((2 * rows, 2 * units), lambda j: (0, 0)),
        ],
        out_shape=[
            jax.ShapeDtypeStruct((2 * rows, units), bf16),
            jax.ShapeDtypeStruct((2 * rows, 2 * units), bf16),
        ],
        compiler_params=pltpu.CompilerParams(
            dimension_semantics=("arbitrary",), vmem_limit_bytes=48 << 20
        ),
        cost_estimate=pl.CostEstimate(
            flops=12 * rows * width * units,
            transcendentals=2 * rows * units,
            bytes_accessed=6 * width * units + 8 * rows * width + 12 * rows * units,
        ),
        name="feed_forward",
    )(*rows_in, *grads_in, gateup, gateup, down)


def on_device(
    tokens,
    caption,
    caption_mask,
    item_lengths,
    item_band,
    positions,
    band_table,
    adaln_weight,
    adaln_bias,
    query_weight,
    key_weight,
    value_weight,
    outproj_weight,
    capkey_weight,
    capvalue_weight,
    norm_gains,
    head_gate,
    gate_weight,
    up_weight,
    down_weight,
    cotangent,
):
    own = lax.axis_index("fsdp")
    place = lax.axis_index("dp")
    count = lax.axis_size("fsdp")
    data_count = lax.axis_size("dp")
    near = dp_place(0)
    rows, width = tokens.shape[1:]
    seq = rows * count
    part = width // count
    head_count = head_gate.shape[0]
    head_size = width // head_count
    own_heads = head_count // count
    units = down_weight.shape[0]
    text_rows = caption.shape[1]
    text = text_rows * count
    cap_depth = capkey_weight.shape[0]
    masks = (0, 1, 2, 3)

    def split_rel(values):
        return [values[m * rows : (m + 1) * rows] for m in masks]

    band_onehot = item_band[:, None] == jnp.arange(band_table.shape[0], dtype=jnp.int32)[None, :]
    band_vector = jnp.dot(band_onehot.astype(bf16), band_table, preferred_element_type=f32)
    silu_low = jax.nn.silu(band_vector).astype(bf16)
    slice_depth = adaln_weight.shape[0]
    modulation_part = mm(
        lax.dynamic_slice_in_dim(silu_low, own * slice_depth, slice_depth, 1), adaln_weight
    )[0]
    modulation_part = modulation_part + lax.dynamic_update_slice(
        jnp.zeros_like(modulation_part), adaln_bias.astype(f32), (own * adaln_bias.shape[0],)
    )
    gains_part = lax.dynamic_update_slice(
        jnp.zeros((2, width), f32), norm_gains[0::4].astype(f32), (0, own * part)
    )
    places_part = lax.dynamic_update_slice(
        jnp.zeros((2, seq), f32), positions[0].astype(f32), (0, own * rows)
    )
    small = jnp.concatenate([modulation_part, gains_part.reshape(-1), places_part.reshape(-1)])
    small = small + hop(small, 1)
    small = small + hop(small, 2)

    token_own = tokens[0]
    token_all = jnp.concatenate(gather_rel(token_own), axis=0)

    def cap_slice(mask):
        return lax.dynamic_slice_in_dim(caption[0], (own ^ mask) * cap_depth, cap_depth, 1)

    caption_rel = trade_rel([cap_slice(m) for m in masks])

    thin = gate_weight.shape[0] // data_count
    units_block = 256 if units % 256 == 0 else units

    def unit_columns(mask):
        return jnp.concatenate(
            [
                lax.dynamic_slice(w, (place * thin, (own ^ mask) * units), (thin, units))
                for w in (gate_weight, up_weight)
            ],
            axis=1,
        )

    thin_rel = trade_rel([unit_columns(m) for m in masks])

    depth = query_weight.shape[0]
    half_depth = depth // 2

    def head_columns(mask, start, length):
        return jnp.concatenate(
            [
                lax.dynamic_slice(w, (start, (own ^ mask) * part), (length, part))
                for w in (query_weight, key_weight, value_weight)
            ],
            axis=1,
        )

    fetched = hop(jnp.stack([head_columns(m, near * half_depth, half_depth) for m in (2, 3)]), 2)

    cap_items = caption[0][None]
    for bit in reversed(range(dp_bits())):
        half = cap_items.shape[2] // 2
        kept, sent = [
            lax.dynamic_slice_in_dim(cap_items, side * half, half, 2)
            for side in (dp_place(bit), 1 - dp_place(bit))
        ]
        cap_items = jnp.concatenate([kept, dp_hop(sent, bit)], axis=0)

    modulation = small[: 6 * width].reshape(6, 1, width)
    shift_mix, scale_mix, gate_mix, shift_feed, scale_feed, gate_feed = [modulation[i] for i in range(6)]
    gain_mix = small[6 * width : 7 * width][None]
    gain_feed = small[7 * width : 8 * width][None]
    places = small[8 * width :].reshape(2, count, rows)
    order = own ^ jnp.arange(count, dtype=jnp.int32)
    places_rel = jnp.concatenate(natural_order([places[:, m] for m in masks], own), axis=1)
    slots_rel = (order[:, None] * rows + jnp.arange(rows, dtype=jnp.int32)[None]).reshape(seq)
    live_bias = jnp.where(slots_rel < item_lengths[0], 0.0, masked_score).astype(f32)[:, None]
    text_live = (
        jnp.concatenate(
            natural_order(
                [caption_mask[0, m * text_rows : (m + 1) * text_rows] for m in masks], own
            )
        )
        > 0
    )
    text_bias = jnp.where(text_live, 0.0, masked_score).astype(f32)[:, None]
    quarter = head_size // 4
    lane = jnp.arange(128, dtype=jnp.int32)
    frequency = jnp.exp(-jnp.log(rope_base) * (lane % quarter).astype(f32) / quarter)[None]
    by_row = (lane % head_size < 2 * quarter)[None]
    angles = jnp.where(by_row, places_rel[0][:, None], places_rel[1][:, None]) * frequency
    sign = jnp.where((lane // quarter) % 2 == 0, -1.0, 1.0).astype(f32)[None]
    tables = (jnp.cos(angles), jnp.sin(angles) * sign)

    unit_all, _ = rms_parts(token_all.astype(f32))
    normed_all = (unit_all * gain_mix * (1.0 + scale_mix) + shift_mix).astype(bf16)

    joined = join(*thin_rel, normed_all)
    thin_rel, normed_all = joined[:count], joined[count]
    thin_all = jnp.stack(natural_order(thin_rel, own))
    gateup_weight = lax.all_gather(thin_all, "dp", axis=1, tiled=True).reshape(width, 2 * units)

    joined = join(*caption_rel, thin_all)
    caption_part = jnp.concatenate(joined[:count], axis=0)
    cap_partial = jnp.concatenate(
        [mm(caption_part, capkey_weight).astype(bf16), mm(caption_part, capvalue_weight).astype(bf16)],
        axis=0,
    )

    fetched, cap_partial = join(fetched, cap_partial)

    def cap_columns(mask):
        return lax.dynamic_slice_in_dim(cap_partial, (own ^ mask) * part, part, 1)

    def align(values, mask):
        return jnp.concatenate(
            [swap_blocks(values[:text], mask, count), swap_blocks(values[text:], mask, count)], axis=0
        )

    cap_inner = hop(jnp.stack([cap_columns(3), cap_columns(1)]), 1)
    cap_passed = (cap_columns(2).astype(f32) + align(cap_inner[0], 1).astype(f32)).astype(bf16)
    cap_kept = cap_columns(0).astype(f32) + align(cap_inner[1], 1).astype(f32)
    cap_raw = cap_kept + align(hop(cap_passed, 2), 2).astype(f32)
    capkey_raw, capvalue_low = cap_raw[:text], cap_raw[text:].astype(bf16)
    (cap_square,) = sum_rows_rel([jnp.sum(capkey_raw * capkey_raw, axis=-1)], count)
    capkey_inverse = lax.rsqrt(cap_square / width + norm_eps)[:, None]
    own_gains = norm_gains.astype(f32)
    capkey_low = (capkey_raw * capkey_inverse * own_gains[3:4]).astype(bf16)

    fetched_beside = dp_hop(fetched, 0)
    fetched_far = jnp.concatenate(
        [jnp.where(near == 0, fetched, fetched_beside), jnp.where(near == 0, fetched_beside, fetched)],
        axis=1,
    )
    fetched_near = hop(jnp.stack([head_columns(1, 0, depth), fetched_far[1]]), 1)
    qkv_rel = [head_columns(0, 0, depth), fetched_near[0], fetched_far[0], fetched_near[1]]
    qkv_weight = jnp.concatenate(natural_order(qkv_rel, own), axis=0)
    qkv = mm(normed_all, qkv_weight)
    query_square, key_square = sum_rows_rel(
        [
            jnp.sum(jnp.square(qkv[:, :part]), axis=-1),
            jnp.sum(jnp.square(qkv[:, part : 2 * part]), axis=-1),
        ],
        count,
    )
    query_inverse = lax.rsqrt(query_square / width + norm_eps)[:, None]
    key_inverse = lax.rsqrt(key_square / width + norm_eps)[:, None]
    tanh_gate = jnp.tanh(head_gate.astype(f32))
    own_tanh = lax.dynamic_slice_in_dim(tanh_gate, own * own_heads, own_heads, 0)
    tanh_lane = jnp.repeat(own_tanh, head_size)[None]
    block_rows = 256 if seq % 256 == 0 else seq

    query_live = (own * rows + jnp.arange(rows, dtype=jnp.int32)) < item_lengths[0]
    grad_out = cotangent[0].astype(f32) * query_live[:, None].astype(f32)
    grad_ffn = (gate_feed * grad_out).astype(bf16)
    grad_ffn_far = hop(grad_ffn, 2)
    cap_items_far = hop(cap_items, 2)
    attended, query_low, key_low, value_low, lse = attend_forward(
        qkv, (query_inverse, key_inverse), (own_gains[1:2], own_gains[2:3]), tables,
        capkey_low, capvalue_low, live_bias, text_bias, tanh_lane, block_rows,
    )
    attended, grad_ffn_far, cap_items_far = join(attended, grad_ffn_far, cap_items_far)
    grad_ffn_two = jnp.stack([grad_ffn, grad_ffn_far])
    grad_ffn_near = hop(grad_ffn_two, 1)
    grad_ffn_rel = [grad_ffn, grad_ffn_near[0], grad_ffn_far, grad_ffn_near[1]]
    cap_items_two = jnp.stack([cap_items, cap_items_far], axis=1)
    cap_items_near = hop(cap_items_two, 1)
    cap_items_all = jnp.stack(
        [cap_items_two[:, 0], cap_items_near[:, 0], cap_items_two[:, 1], cap_items_near[:, 1]], axis=1
    ).reshape(data_count * text, -1)
    branch = scatter_rel(split_rel(mm(attended, outproj_weight).astype(bf16)))
    token_float = token_own.astype(f32)
    middle = token_float + gate_mix * branch

    unit_feed, inverse_feed = rms_parts(middle)
    normed_feed = (unit_feed * gain_feed * (1.0 + scale_feed) + shift_feed).astype(bf16)
    feed_far = hop(normed_feed, 2)
    feed_rel = [normed_feed, hop(normed_feed, 1), feed_far, hop(feed_far, 1)]
    hidden_early, grads_early = feed_forward(
        feed_rel[:2], grad_ffn_rel[:2], gateup_weight, down_weight, units_block
    )
    early = mm_nt(grads_early, gateup_weight).astype(bf16)
    hidden_late, grads_late = feed_forward(
        feed_rel[2:], grad_ffn_rel[2:], gateup_weight, down_weight, units_block
    )
    late = mm_nt(grads_late, gateup_weight).astype(bf16)
    passed = (late[:rows].astype(f32) + hop(late[rows:], 1).astype(f32)).astype(bf16)
    passed, hidden_late, grads_late = join(passed, hidden_late, grads_late)
    passed = hop(passed, 2)
    hidden = jnp.concatenate([hidden_early, hidden_late], axis=0)
    grad_units = jnp.concatenate([grads_early, grads_late], axis=0)
    feed_all = jnp.concatenate(feed_rel, axis=0)
    grad_ffn_all = jnp.concatenate(grad_ffn_rel, axis=0)
    down_state = dp_first(mm_tn(hidden, grad_ffn_all).astype(bf16))
    gate_part = mm_tn(feed_all, grad_units[:, :units]).astype(bf16)
    passed, early, down_kept, gate_part = join(passed, early, down_state[0], gate_part)
    down_state = (down_kept, down_state[1])
    grad_normfeed = (
        early[:rows].astype(f32) + hop(early[rows:], 1).astype(f32) + passed.astype(f32)
    )

    dshift_feed = jnp.sum(grad_normfeed, axis=0)
    dscale_feed = jnp.sum(grad_normfeed * (unit_feed * gain_feed), axis=0)
    grad_scaledfeed = grad_normfeed * (1.0 + scale_feed)
    gain_feed_grad = jnp.sum(grad_scaledfeed * unit_feed, axis=0)
    grad_middle = grad_out + rms_back(unit_feed, inverse_feed, grad_scaledfeed * gain_feed)
    dgate_mix = jnp.sum(grad_middle * branch, axis=0)

    grad_branch_rel = gather_rel((gate_mix * grad_middle).astype(bf16))
    gate_state = dp_first(gate_part)
    up_part = mm_tn(feed_all, grad_units[:, units:]).astype(bf16)
    up_state = dp_first(up_part)
    joined = join(*grad_branch_rel, gate_state[0], up_state[0])
    grad_branch_rel = joined[:count]
    gate_state, up_state = (joined[count], gate_state[1]), (joined[count + 1], up_state[1])
    grad_branch_all = jnp.concatenate(grad_branch_rel, axis=0)
    grad_attended = mm_nt(grad_branch_all, outproj_weight).astype(bf16)
    dquery_text, dcapkey, grad_capvalue, dtanh = text_backward(
        query_low, capkey_low, capvalue_low, grad_attended, lse, text_bias, tanh_lane, seq
    )
    outproj_part = mm_tn(attended, grad_branch_all).astype(bf16)
    outproj_state = dp_first(outproj_part)
    capkey_unit = capkey_raw * capkey_inverse
    capkey_scaled = dcapkey * own_gains[3:4]
    (cap_dot,) = sum_rows_rel([jnp.sum(capkey_scaled * capkey_unit, axis=-1)], count)
    grad_capkey = (
        capkey_inverse * (capkey_scaled - capkey_unit * (cap_dot[:, None] / width))
    ).astype(bf16)
    gain_capkey_grad = jnp.sum(dcapkey * capkey_unit, axis=0)
    grad_cap = jnp.concatenate([grad_capkey, grad_capvalue], axis=1)
    ffn_part = mm(hidden, down_weight).astype(bf16)
    ffn_passed = (
        ffn_part[2 * rows : 3 * rows].astype(f32) + hop(ffn_part[3 * rows :], 1).astype(f32)
    ).astype(bf16)

    down_arrived, dtanh = join(down_state[1], dtanh)
    down_kept, down_sent = dp_sums((down_state[0], down_arrived), 1)
    dquery_text, grad_cap, ffn_passed, outproj_part, down_kept, down_sent = join(
        dquery_text, grad_cap, ffn_passed, outproj_part, down_kept, down_sent
    )
    down_state = (down_kept, dp_hop(down_sent, 1))
    ffn_passed = hop(ffn_passed, 2)
    top = dp_bits() - 1
    cap_items_grad = jnp.stack([grad_cap, dp_hop(grad_cap, top)])
    query_unrot, key_unrot, grad_value = self_backward(
        query_low, key_low, value_low, grad_attended, lse, dquery_text, tables, live_bias, block_rows
    )
    query_unrot, key_unrot, grad_value, ffn_passed, down_arrived, gate_arrived, cap_items_grad = join(
        query_unrot, key_unrot, grad_value, ffn_passed, down_state[1], gate_state[1], cap_items_grad
    )
    down_state = (down_state[0], down_arrived)
    gate_state = (gate_state[0], gate_arrived)

    query_unit = qkv[:, :part] * query_inverse
    key_unit = qkv[:, part : 2 * part] * key_inverse
    query_scaled = query_unrot * own_gains[1:2]
    key_scaled = key_unrot * own_gains[2:3]
    query_dot, key_dot = sum_rows_rel(
        [
            jnp.sum(query_scaled * query_unit, axis=-1),
            jnp.sum(key_scaled * key_unit, axis=-1),
        ],
        count,
    )
    gain_query_grad = jnp.sum(query_unrot * query_unit, axis=0)
    gain_key_grad = jnp.sum(key_unrot * key_unit, axis=0)
    grad_qk = jnp.concatenate(
        [
            (query_inverse * (query_scaled - query_unit * (query_dot[:, None] / width))).astype(bf16),
            (key_inverse * (key_scaled - key_unit * (key_dot[:, None] / width))).astype(bf16),
        ],
        axis=1,
    )
    grad_qkv = jnp.concatenate([grad_qk, grad_value], axis=1)
    qkv_state = dp_first(mm_tn(normed_all, grad_qkv).astype(bf16))
    normmix_part = mm_nt(grad_qkv, qkv_weight).astype(bf16)
    grad_normmix = scatter_rel(split_rel(normmix_part))

    gate_state = dp_next(gate_state, 1)
    down_sum = dp_rest_from(down_state, 2)
    up_arrived, qkv_kept = join(up_state[1], qkv_state[0])
    qkv_state = (qkv_kept, qkv_state[1])
    up_state = dp_next((up_state[0], up_arrived), 1)
    gate_sum = dp_rest_from(gate_state, 2)
    for bit in [0] + list(reversed(range(1, top))):
        cap_items_grad = jnp.concatenate(
            [cap_items_grad, dp_hop(cap_items_grad, bit)], axis=0
        )
    outproj_sum = dp_rest(outproj_state)
    up_sum = dp_rest_from(up_state, 2)
    qkv_sum = dp_rest(qkv_state)
    cap_shape = (2,) * top + (2,)
    order_axes = cap_axes(top)
    cap_grads = cap_items_grad.reshape(cap_shape + cap_items_grad.shape[1:])
    cap_grads = cap_grads.transpose(order_axes + (top + 1, top + 2)).reshape(data_count * text, -1)
    cap_sum = mm_tn(cap_items_all, cap_grads)

    ffn_kept = ffn_part[:rows].astype(f32) + hop(ffn_part[rows : 2 * rows], 1).astype(f32)
    ffn_out = ffn_kept + ffn_passed.astype(f32)
    block_out = (middle + gate_feed * ffn_out).astype(bf16)
    dgate_feed = jnp.sum(grad_out * ffn_out, axis=0)

    unit_mix, inverse_mix = rms_parts(token_float)
    dshift_mix = jnp.sum(grad_normmix, axis=0)
    dscale_mix = jnp.sum(grad_normmix * (unit_mix * gain_mix), axis=0)
    grad_scaledmix = grad_normmix * (1.0 + scale_mix)
    gain_mix_grad = jnp.sum(grad_scaledmix * unit_mix, axis=0)
    tokens_grad = (
        grad_middle + rms_back(unit_mix, inverse_mix, grad_scaledmix * gain_mix)
    ).astype(bf16)

    own_rows = jnp.zeros((3, width), f32)
    own_rows = lax.dynamic_update_slice(
        own_rows, jnp.stack([gain_query_grad, gain_key_grad, gain_capkey_grad]), (0, own * part)
    )
    gate_sums = lax.dynamic_update_slice(
        jnp.zeros((head_count,), f32), dtanh[0, ::head_size], (own * own_heads,)
    )
    sums = jnp.concatenate([gain_mix_grad, own_rows.reshape(-1), gain_feed_grad, gate_sums])
    grad_modulation = jnp.concatenate(
        [dshift_mix, dscale_mix, dgate_mix, dshift_feed, dscale_feed, dgate_feed]
    )
    message = jnp.concatenate([grad_modulation, sums])
    message = message + hop(message, 1)
    message = message + hop(message, 2)
    gathered = jnp.concatenate([message, silu_low[0].astype(f32)])[None]
    for bit in range(dp_bits()):
        gathered = jnp.concatenate([gathered, dp_hop(gathered, bit)], axis=0)
    mod_width = 6 * width
    modulation_rows = gathered[:, :mod_width]
    totals = jnp.sum(gathered[:, mod_width : mod_width + sums.shape[0]], axis=0)
    silu_rows = gathered[:, mod_width + sums.shape[0] :]
    owner = place * count + own
    devices = count * data_count
    cd_rows = silu_rows.shape[1] // devices
    adaln_wgrad = lax.dot_general(
        lax.dynamic_slice_in_dim(silu_rows, owner * cd_rows, cd_rows, 1),
        modulation_rows,
        (((0,), (0,)), ((), ())),
        precision=lax.Precision.HIGHEST,
        preferred_element_type=f32,
    )
    bias_rows = mod_width // devices
    adaln_bgrad = lax.dynamic_slice_in_dim(
        jnp.sum(modulation_rows, axis=0), owner * bias_rows, bias_rows, 0
    )
    gains_grad = lax.dynamic_slice_in_dim(
        totals[: 5 * width].reshape(5, width), owner * (width // devices), width // devices, 1
    )
    headgate_grad = totals[5 * width :] * (1.0 - tanh_gate * tanh_gate)

    gate_grad, up_grad = spread_rows([gate_sum, up_sum], own)
    capkey_grad, capvalue_grad = spread_rows([cap_sum[:, :part], cap_sum[:, part:]], own)
    query_grad, key_grad, value_grad = spread_rows(
        [qkv_sum[:, i * part : (i + 1) * part] for i in range(3)], own
    )
    owned = to_owner(jnp.concatenate([down_sum, outproj_sum], axis=0))
    down_grad, outproj_grad = owned[: down_sum.shape[0]], owned[down_sum.shape[0] :]
    return (
        block_out[None],
        tokens_grad[None],
        adaln_wgrad,
        adaln_bgrad,
        query_grad,
        key_grad,
        value_grad,
        outproj_grad,
        capkey_grad,
        capvalue_grad,
        gains_grad,
        headgate_grad,
        gate_grad,
        up_grad,
        down_grad,
    )


def solution(mesh):
    return jax.shard_map(
        on_device,
        mesh=mesh,
        in_specs=(
            P("dp", "fsdp", None),
            P("dp", "fsdp", None),
            P("dp", None),
            P("dp"),
            P("dp"),
            P("dp", None, "fsdp"),
            P(),
            P("fsdp", None),
            P("fsdp"),
            P("fsdp", None),
            P("fsdp", None),
            P("fsdp", None),
            P("fsdp", None),
            P("fsdp", None),
            P("fsdp", None),
            P(None, "fsdp"),
            P(),
            P("fsdp", None),
            P("fsdp", None),
            P("fsdp", None),
            P("dp", "fsdp", None),
        ),
        out_specs=(
            P("dp", "fsdp", None),
            P("dp", "fsdp", None),
            P(("dp", "fsdp"), None),
            P(("dp", "fsdp")),
            P(("dp", "fsdp"), None),
            P(("dp", "fsdp"), None),
            P(("dp", "fsdp"), None),
            P(("dp", "fsdp"), None),
            P(("dp", "fsdp"), None),
            P(("dp", "fsdp"), None),
            P(None, ("dp", "fsdp")),
            P(),
            P(("dp", "fsdp"), None),
            P(("dp", "fsdp"), None),
            P(("dp", "fsdp"), None),
        ),
        check_vma=False,
    )
```

```python
import jax
import jax.numpy as jnp
from jax import lax
from jax.experimental import pallas as pl
from jax.experimental.pallas import tpu as pltpu
from jax.sharding import PartitionSpec as P

norm_eps = 1e-06
rope_base = 10000.0
masked_score = -1e30
f32 = jnp.float32
bf16 = jnp.bfloat16


def mm(left_side, right_side):
    return lax.dot_general(
        left_side, right_side, (((1,), (0,)), ((), ())), preferred_element_type=f32
    )


def mm_nt(left_side, right_side):
    return lax.dot_general(
        left_side, right_side, (((1,), (1,)), ((), ())), preferred_element_type=f32
    )


def mm_tn(left_side, right_side):
    return lax.dot_general(
        left_side, right_side, (((0,), (0,)), ((), ())), preferred_element_type=f32
    )


def rms_parts(values):
    inverse = lax.rsqrt(jnp.mean(values * values, axis=-1, keepdims=True) + norm_eps)
    return (values * inverse, inverse)


def rms_back(unit_rows, inverse, grad_unit):
    return inverse * (
        grad_unit - unit_rows * jnp.mean(grad_unit * unit_rows, axis=-1, keepdims=True)
    )


def hop(values, mask):
    count = lax.axis_size("fsdp")
    return lax.ppermute(values, "fsdp", [(i, i ^ mask) for i in range(count)])


def gather_rel(values):
    two = jnp.stack([values, hop(values, 2)])
    other = hop(two, 1)
    return [values, other[0], two[1], other[1]]


def scatter_rel(blocks):
    arrived = hop(jnp.stack([blocks[3], blocks[1]]), 1)
    passed = hop((blocks[2].astype(f32) + arrived[0].astype(f32)).astype(bf16), 2)
    return blocks[0].astype(f32) + arrived[1].astype(f32) + passed.astype(f32)


def trade_rel(blocks, middle=None):
    far = hop(jnp.stack([blocks[2], blocks[3]]), 2)
    if middle is not None:
        far = middle(far)
    beside = hop(jnp.stack([blocks[1], far[1]]), 1)
    return [blocks[0], beside[0], far[0], beside[1]]


def swap_blocks(values, mask, count):
    rows = values.shape[0] // count
    return jnp.concatenate(
        [values[(m ^ mask) * rows : ((m ^ mask) + 1) * rows] for m in range(count)], axis=0
    )


def sum_rows_rel(columns, count):
    ends = [0]
    for column in columns:
        ends.append(ends[-1] + column.shape[0])
    total = jnp.concatenate(columns)
    for mask in (1, 2):
        arrived = hop(total, mask)
        total = total + jnp.concatenate(
            [swap_blocks(arrived[i:j], mask, count) for i, j in zip(ends, ends[1:])]
        )
    return [total[i:j] for i, j in zip(ends, ends[1:])]


def natural_order(pieces, own):
    far, near = own // 2, own % 2
    mixed = [[jnp.where(near == 0, pieces[2 * i + j], pieces[2 * i + 1 - j]) for j in range(2)] for i in range(2)]
    return [jnp.where(far == 0, mixed[i][j], mixed[1 - i][j]) for i in range(2) for j in range(2)]


def join(*values):
    return lax.optimization_barrier(values)


def dp_bits():
    return lax.axis_size("dp").bit_length() - 1


def dp_hop(values, bit):
    count = lax.axis_size("dp")
    return lax.ppermute(values, "dp", [(i, i ^ (1 << bit)) for i in range(count)])


def dp_place(bit):
    return (lax.axis_index("dp") >> bit) & 1


def pick(values, axis, index):
    return lax.dynamic_index_in_dim(values, index, axis, keepdims=False)


def dp_blocks(partial):
    return partial.reshape(lax.axis_size("dp"), -1, partial.shape[1])


def dp_half(blocks, bit, other):
    pairs = blocks.reshape((-1, 2) + blocks.shape[1:])
    return pick(pairs, 1, 1 - dp_place(bit) if other else dp_place(bit))


def dp_sent(blocks, start, stop):
    return dp_half(blocks[..., start:stop], 0, True)


def dp_joined(blocks, arrived, start, stop):
    return dp_sums((dp_half(blocks[..., start:stop], 0, False), arrived), 1)


def dp_sums(state, bit):
    kept, arrived = state

    def half(other):
        return (
            dp_half(kept, bit, other).astype(f32) + dp_half(arrived, bit, other).astype(f32)
        ).astype(bf16)

    return (half(False), half(True))


def dp_next(state, bit):
    kept, sent = dp_sums(state, bit)
    return (kept, dp_hop(sent, bit))


def dp_total(state):
    return state[0][0].astype(f32) + state[1][0].astype(f32)


def dp_rest_from(state, start):
    for bit in range(start, dp_bits()):
        state = dp_next(state, bit)
    return dp_total(state)


def dp_rest(state):
    return dp_rest_from(state, 1)


def cap_order(values, top):
    return values.reshape(-1, values.shape[-1])


def spread_pieces(totals, own):
    count = lax.axis_size("fsdp")
    low = jnp.concatenate([total.astype(bf16) for total in totals], axis=1)
    rows = low.shape[0] // count
    pieces = [lax.dynamic_slice_in_dim(low, (own ^ m) * rows, rows, 0) for m in range(count)]
    return (jnp.stack(pieces[:2]), jnp.stack(pieces[2:]))


def spread_near(pieces, far):
    return hop(jnp.stack([pieces[1], far[1]]), 1)


def spread_result(pieces, far, near, widths, own):
    results, start = [], 0
    for width in widths:
        part = [
            piece[:, start : start + width] for piece in (pieces[0], near[0], far[0], near[1])
        ]
        results.append(jnp.concatenate(natural_order(part, own), axis=1).astype(f32))
        start += width
    return results


def to_owner(total):
    data_count, count = lax.axis_size("dp"), lax.axis_size("fsdp")
    pairs = [(d * count + f, f * data_count + d) for d in range(data_count) for f in range(count)]
    return lax.ppermute(total.astype(bf16), ("dp", "fsdp"), pairs).astype(f32)


def lane_of(shape):
    return lax.broadcasted_iota(jnp.int32, shape, len(shape) - 1)


def rotate_lanes(values, cosines, sines):
    lanes = lane_of(values.shape)
    even = lax.rem(lax.div(lanes, 16), 2) == 0
    width = values.shape[-1]
    partner = jnp.where(even, pltpu.roll(values, width - 16, 1), pltpu.roll(values, 16, 1))
    return values * cosines + partner * sines


def head_lanes(values, head, spare):
    lanes = lane_of(values.shape)
    mine = (lanes < 64) if head == 0 else (lanes >= 64)
    mark = 64 if head == 0 else 0
    return jnp.where(mine, values, jnp.where(lanes == mark, spare, jnp.zeros_like(values)))


def attend_body(
    q_ref, k_ref, v_ref, qinv_ref, kinv_ref, qg_ref, kg_ref, cosq_ref, sinq_ref, cosk_ref, sink_ref,
    ck_ref, cv_ref, live_ref, text_ref, tanh_ref,
    out_ref, qlow_ref, klow_ref, vlow_ref, lse_ref,
    km, vm, cm, cvm,
):
    @pl.when(pl.program_id(1) == 0)
    def _():
        key = rotate_lanes(
            k_ref[...] * kinv_ref[...] * kg_ref[...], cosk_ref[...], sink_ref[...]
        ).astype(bf16)
        value = v_ref[...].astype(bf16)
        klow_ref[...] = key
        vlow_ref[...] = value
        one = jnp.ones((), bf16)
        for head in range(2):
            km[head] = head_lanes(key, head, live_ref[...].astype(bf16))
            vm[head] = head_lanes(value, head, one)
            cm[head] = head_lanes(ck_ref[...], head, text_ref[...].astype(bf16))
            cvm[head] = head_lanes(cv_ref[...], head, one)

    query = rotate_lanes(
        q_ref[...] * qinv_ref[...] * qg_ref[...], cosq_ref[...], sinq_ref[...]
    ).astype(bf16)
    qlow_ref[...] = query
    scaled = query * jnp.asarray(0.125, bf16)
    lanes = lane_of(out_ref.shape)
    results, stats = [], []
    for head in range(2):
        part = head_lanes(scaled, head, jnp.ones((), bf16))
        mark = 64 if head == 0 else 0

        def one_side(keys, values):
            scores = mm_nt(part, keys)
            peak = jnp.max(scores, axis=-1, keepdims=True)
            weights = jnp.exp(scores - peak).astype(bf16)
            mixed = mm(weights, values)
            amount = mixed[:, mark : mark + 1]
            stats.append(peak + jnp.log(amount))
            return mixed / amount

        own = one_side(km[head], vm[head])
        text = one_side(cm[head], cvm[head])
        results.append(own + tanh_ref[...] * text)
    out_ref[...] = jnp.where(lanes < 64, results[0], results[1]).astype(bf16)
    table = jnp.where(lanes == 0, stats[0], stats[1])
    table = jnp.where(lanes == 2, stats[2], table)
    lse_ref[...] = jnp.where(lanes == 3, stats[3], table)


def attend_forward(qkv, inverses, gains, tables, capkey, capvalue, live_bias, text_bias, tanh_lane, rows):
    seq, width = qkv.shape[0], qkv.shape[1] // 3
    pairs, text = width // 128, capkey.shape[0]
    full = lambda p, i: (0, p)
    block = lambda p, i: (i, p)
    qrow = lambda p, i: (i, 0)
    whole = lambda p, i: (0, 0)
    return pl.pallas_call(
        attend_body,
        grid=(pairs, seq // rows),
        in_specs=[
            pl.BlockSpec((rows, 128), block),
            pl.BlockSpec((seq, 128), lambda p, i: (0, p + pairs)),
            pl.BlockSpec((seq, 128), lambda p, i: (0, p + 2 * pairs)),
            pl.BlockSpec((rows, 1), qrow),
            pl.BlockSpec((seq, 1), whole),
            pl.BlockSpec((1, 128), full),
            pl.BlockSpec((1, 128), full),
            pl.BlockSpec((rows, 128), qrow),
            pl.BlockSpec((rows, 128), qrow),
            pl.BlockSpec((seq, 128), whole),
            pl.BlockSpec((seq, 128), whole),
            pl.BlockSpec((text, 128), full),
            pl.BlockSpec((text, 128), full),
            pl.BlockSpec((seq, 1), whole),
            pl.BlockSpec((text, 1), whole),
            pl.BlockSpec((1, 128), full),
        ],
        out_specs=[
            pl.BlockSpec((rows, 128), block),
            pl.BlockSpec((rows, 128), block),
            pl.BlockSpec((seq, 128), full),
            pl.BlockSpec((seq, 128), full),
            pl.BlockSpec((rows, 128), block),
        ],
        out_shape=[
            jax.ShapeDtypeStruct((seq, width), bf16),
            jax.ShapeDtypeStruct((seq, width), bf16),
            jax.ShapeDtypeStruct((seq, width), bf16),
            jax.ShapeDtypeStruct((seq, width), bf16),
            jax.ShapeDtypeStruct((seq, width), f32),
        ],
        scratch_shapes=[
            pltpu.VMEM((2, seq, 128), bf16),
            pltpu.VMEM((2, seq, 128), bf16),
            pltpu.VMEM((2, text, 128), bf16),
            pltpu.VMEM((2, text, 128), bf16),
        ],
        compiler_params=pltpu.CompilerParams(
            dimension_semantics=("arbitrary", "arbitrary"), vmem_limit_bytes=20 << 20
        ),
        cost_estimate=pl.CostEstimate(
            flops=seq * width,
            transcendentals=0,
            bytes_accessed=seq * width,
        ),
        name="attend_forward",
    )(
        qkv, qkv, qkv, inverses[0], inverses[1], gains[0], gains[1], tables[0], tables[1],
        tables[0], tables[1], capkey, capvalue, live_bias, text_bias, tanh_lane,
    )


def text_back_body(
    q_ref, ck_ref, cv_ref, do_ref, lse_ref, text_ref, tanh_ref,
    dq_ref, dck_ref, dcv_ref, dtanh_ref,
    cm, dck, dcv,
):
    step = pl.program_id(1)

    @pl.when(step == 0)
    def _():
        for head in range(2):
            cm[head] = head_lanes(ck_ref[...], head, text_ref[...].astype(bf16))
        dck[...] = jnp.zeros_like(dck)
        dcv[...] = jnp.zeros_like(dcv)
        dtanh_ref[...] = jnp.zeros_like(dtanh_ref)

    scaled = q_ref[...] * jnp.asarray(0.125, bf16)
    grad = do_ref[...]
    lse = lse_ref[...]
    grads = []
    for head in range(2):
        part = head_lanes(scaled, head, jnp.ones((), bf16))
        grad_part = head_lanes(grad, head, jnp.zeros((), bf16))
        gate = tanh_ref[:, 64 * head : 64 * head + 1]
        probs = jnp.exp(mm_nt(part, cm[head]) - lse[:, 2 * head + 1 : 2 * head + 2])
        dprob = mm_nt(grad_part, cv_ref[...])
        total = jnp.sum(probs * dprob, axis=-1, keepdims=True)
        dscore = (probs * ((dprob - total) * gate)).astype(bf16)
        grads.append(mm(dscore, ck_ref[...]))

        def add(target, update):
            lanes = lane_of(target.shape)
            mine = (lanes < 64) if head == 0 else (lanes >= 64)
            target[...] += jnp.where(mine, update, jnp.zeros_like(update))

        add(dck, mm_tn(dscore, scaled))
        add(dcv, mm_tn(probs.astype(bf16), grad))
        add(dtanh_ref, jnp.broadcast_to(jnp.sum(total, axis=0, keepdims=True), dtanh_ref.shape))
    lanes = lane_of(dq_ref.shape)
    dq_ref[...] = jnp.where(lanes < 64, grads[0], grads[1])

    @pl.when(step == pl.num_programs(1) - 1)
    def _():
        dck_ref[...] = dck[...]
        dcv_ref[...] = (dcv[...] * tanh_ref[...]).astype(bf16)


def text_backward(query, capkey, capvalue, grad, lse, text_bias, tanh_lane, rows):
    seq, width = query.shape
    pairs, text = width // 128, capkey.shape[0]
    full = lambda p, i: (0, p)
    block = lambda p, i: (i, p)
    whole = lambda p, i: (0, 0)
    return pl.pallas_call(
        text_back_body,
        grid=(pairs, seq // rows),
        in_specs=[
            pl.BlockSpec((rows, 128), block),
            pl.BlockSpec((text, 128), full),
            pl.BlockSpec((text, 128), full),
            pl.BlockSpec((rows, 128), block),
            pl.BlockSpec((rows, 128), block),
            pl.BlockSpec((text, 1), whole),
            pl.BlockSpec((1, 128), full),
        ],
        out_specs=[
            pl.BlockSpec((rows, 128), block),
            pl.BlockSpec((text, 128), full),
            pl.BlockSpec((text, 128), full),
            pl.BlockSpec((8, 128), full),
        ],
        out_shape=[
            jax.ShapeDtypeStruct((seq, width), f32),
            jax.ShapeDtypeStruct((text, width), f32),
            jax.ShapeDtypeStruct((text, width), bf16),
            jax.ShapeDtypeStruct((8, width), f32),
        ],
        scratch_shapes=[
            pltpu.VMEM((2, text, 128), bf16),
            pltpu.VMEM((text, 128), f32),
            pltpu.VMEM((text, 128), f32),
        ],
        compiler_params=pltpu.CompilerParams(
            dimension_semantics=("arbitrary", "arbitrary"), vmem_limit_bytes=20 << 20
        ),
        cost_estimate=pl.CostEstimate(
            flops=40 * seq * text * width,
            transcendentals=seq * text * width // 64,
            bytes_accessed=seq * width * 16,
        ),
        name="text_backward",
    )(query, capkey, capvalue, grad, lse, text_bias, tanh_lane)


def self_back_body(
    q_ref, k_ref, v_ref, do_ref, lse_ref, dqt_ref, cosq_ref, sinq_ref, cosk_ref, sink_ref, live_ref,
    dq_ref, dk_ref, dv_ref,
    km, dk, dv,
):
    step = pl.program_id(1)

    @pl.when(step == 0)
    def _():
        for head in range(2):
            km[head] = head_lanes(k_ref[...], head, live_ref[...].astype(bf16))
        dk[...] = jnp.zeros_like(dk)
        dv[...] = jnp.zeros_like(dv)

    scaled = q_ref[...] * jnp.asarray(0.125, bf16)
    grad = do_ref[...]
    lse = lse_ref[...]
    grads = []
    for head in range(2):
        part = head_lanes(scaled, head, jnp.ones((), bf16))
        grad_part = head_lanes(grad, head, jnp.zeros((), bf16))
        probs = jnp.exp(mm_nt(part, km[head]) - lse[:, 2 * head : 2 * head + 1])
        dprob = mm_nt(grad_part, v_ref[...])
        total = jnp.sum(probs * dprob, axis=-1, keepdims=True)
        dscore = (probs * (dprob - total)).astype(bf16)
        grads.append(mm(dscore, k_ref[...]))

        def add(target, update):
            lanes = lane_of(target.shape)
            mine = (lanes < 64) if head == 0 else (lanes >= 64)
            target[...] += jnp.where(mine, update, jnp.zeros_like(update))

        add(dk, mm_tn(dscore, scaled))
        add(dv, mm_tn(probs.astype(bf16), grad))
    lanes = lane_of(dq_ref.shape)
    dq_ref[...] = rotate_lanes(
        (jnp.where(lanes < 64, grads[0], grads[1]) + dqt_ref[...]) * 0.125,
        cosq_ref[...],
        -sinq_ref[...],
    )

    @pl.when(step == pl.num_programs(1) - 1)
    def _():
        dk_ref[...] = rotate_lanes(dk[...], cosk_ref[...], -sink_ref[...])
        dv_ref[...] = dv[...].astype(bf16)


def self_backward(query, key, value, grad, lse, dquery_text, tables, live_bias, rows):
    seq, width = query.shape
    pairs = width // 128
    full = lambda p, i: (0, p)
    block = lambda p, i: (i, p)
    qrow = lambda p, i: (i, 0)
    whole = lambda p, i: (0, 0)
    return pl.pallas_call(
        self_back_body,
        grid=(pairs, seq // rows),
        in_specs=[
            pl.BlockSpec((rows, 128), block),
            pl.BlockSpec((seq, 128), full),
            pl.BlockSpec((seq, 128), full),
            pl.BlockSpec((rows, 128), block),
            pl.BlockSpec((rows, 128), block),
            pl.BlockSpec((rows, 128), block),
            pl.BlockSpec((rows, 128), qrow),
            pl.BlockSpec((rows, 128), qrow),
            pl.BlockSpec((seq, 128), whole),
            pl.BlockSpec((seq, 128), whole),
            pl.BlockSpec((seq, 1), whole),
        ],
        out_specs=[
            pl.BlockSpec((rows, 128), block),
            pl.BlockSpec((seq, 128), full),
            pl.BlockSpec((seq, 128), full),
        ],
        out_shape=[
            jax.ShapeDtypeStruct((seq, width), f32),
            jax.ShapeDtypeStruct((seq, width), f32),
            jax.ShapeDtypeStruct((seq, width), bf16),
        ],
        scratch_shapes=[
            pltpu.VMEM((2, seq, 128), bf16),
            pltpu.VMEM((seq, 128), f32),
            pltpu.VMEM((seq, 128), f32),
        ],
        compiler_params=pltpu.CompilerParams(
            dimension_semantics=("arbitrary", "arbitrary"), vmem_limit_bytes=20 << 20
        ),
        cost_estimate=pl.CostEstimate(
            flops=40 * seq * seq * width,
            transcendentals=seq * seq * width // 64,
            bytes_accessed=seq * width * 28,
        ),
        name="self_backward",
    )(query, key, value, grad, lse, dquery_text, tables[0], tables[1], tables[0], tables[1], live_bias)


def feed_body(x0_ref, x1_ref, g0_ref, g1_ref, gate_ref, up_ref, down_ref, hidden_ref, grads_ref):
    step = pl.program_id(0)
    block = down_ref.shape[0]
    units = grads_ref.shape[1] // 2
    rows_in = jnp.concatenate([x0_ref[...], x1_ref[...]], axis=0)
    grads_in = jnp.concatenate([g0_ref[...], g1_ref[...]], axis=0)
    gate = mm(rows_in, gate_ref[...])
    up = mm(rows_in, up_ref[...])
    grad_hidden = mm_nt(grads_in, down_ref[...])
    sigmoid = 1.0 / (1.0 + jnp.exp(-gate))
    silu = gate * sigmoid
    hidden_ref[...] = (silu * up).astype(bf16)
    start = pl.multiple_of(step * block, block)
    grads_ref[:, pl.ds(start, block)] = (
        grad_hidden * up * (sigmoid * (1.0 + gate * (1.0 - sigmoid)))
    ).astype(bf16)
    grads_ref[:, pl.ds(pl.multiple_of(units + start, block), block)] = (grad_hidden * silu).astype(bf16)


def feed_forward(rows_in, grads_in, gateup, down, units_block):
    rows, width = rows_in[0].shape
    units = down.shape[0]
    steps = units // units_block
    whole = pl.BlockSpec((rows, width), lambda j: (0, 0))
    return pl.pallas_call(
        feed_body,
        grid=(steps,),
        in_specs=[whole] * 4
        + [
            pl.BlockSpec((width, units_block), lambda j: (0, j)),
            pl.BlockSpec((width, units_block), lambda j: (0, j + steps)),
            pl.BlockSpec((units_block, width), lambda j: (j, 0)),
        ],
        out_specs=[
            pl.BlockSpec((2 * rows, units_block), lambda j: (0, j)),
            pl.BlockSpec((2 * rows, 2 * units), lambda j: (0, 0)),
        ],
        out_shape=[
            jax.ShapeDtypeStruct((2 * rows, units), bf16),
            jax.ShapeDtypeStruct((2 * rows, 2 * units), bf16),
        ],
        compiler_params=pltpu.CompilerParams(
            dimension_semantics=("arbitrary",), vmem_limit_bytes=32 << 20
        ),
        cost_estimate=pl.CostEstimate(
            flops=12 * rows * width * units,
            transcendentals=2 * rows * units,
            bytes_accessed=6 * width * units + 8 * rows * width + 12 * rows * units,
        ),
        name="feed_forward",
    )(*rows_in, *grads_in, gateup, gateup, down)


def on_device(
    tokens,
    caption,
    caption_mask,
    item_lengths,
    item_band,
    positions,
    band_table,
    adaln_weight,
    adaln_bias,
    query_weight,
    key_weight,
    value_weight,
    outproj_weight,
    capkey_weight,
    capvalue_weight,
    norm_gains,
    head_gate,
    gate_weight,
    up_weight,
    down_weight,
    cotangent,
):
    own = lax.axis_index("fsdp")
    place = lax.axis_index("dp")
    count = lax.axis_size("fsdp")
    data_count = lax.axis_size("dp")
    near = dp_place(0)
    rows, width = tokens.shape[1:]
    seq = rows * count
    part = width // count
    head_count = head_gate.shape[0]
    head_size = width // head_count
    own_heads = head_count // count
    units = down_weight.shape[0]
    text_rows = caption.shape[1]
    text = text_rows * count
    cap_depth = capkey_weight.shape[0]
    masks = (0, 1, 2, 3)

    def split_rel(values):
        return [values[m * rows : (m + 1) * rows] for m in masks]

    band_onehot = item_band[:, None] == jnp.arange(band_table.shape[0], dtype=jnp.int32)[None, :]
    band_vector = jnp.dot(band_onehot.astype(bf16), band_table, preferred_element_type=f32)
    silu_low = jax.nn.silu(band_vector).astype(bf16)
    slice_depth = adaln_weight.shape[0]
    modulation_part = mm(
        lax.dynamic_slice_in_dim(silu_low, own * slice_depth, slice_depth, 1), adaln_weight
    )[0]
    modulation_part = modulation_part + lax.dynamic_update_slice(
        jnp.zeros_like(modulation_part), adaln_bias.astype(f32), (own * adaln_bias.shape[0],)
    )
    gains_part = lax.dynamic_update_slice(
        jnp.zeros((2, width), f32), norm_gains[0::4].astype(f32), (0, own * part)
    )
    places_part = lax.dynamic_update_slice(
        jnp.zeros((2, seq), f32), positions[0].astype(f32), (0, own * rows)
    )
    small = jnp.concatenate([modulation_part, gains_part.reshape(-1), places_part.reshape(-1)])

    def cap_slice(mask):
        return lax.dynamic_slice_in_dim(caption[0], (own ^ mask) * cap_depth, cap_depth, 1)

    depth = query_weight.shape[0]
    half_depth = depth // 2

    def head_columns(mask, start, length):
        return jnp.concatenate(
            [
                lax.dynamic_slice(w, (start, (own ^ mask) * part), (length, part))
                for w in (query_weight, key_weight, value_weight)
            ],
            axis=1,
        )

    thin = gate_weight.shape[0] // data_count
    units_block = 256 if units % 256 == 0 else units

    def unit_columns(mask):
        return jnp.concatenate(
            [
                lax.dynamic_slice(w, (place * thin, (own ^ mask) * units), (thin, units))
                for w in (gate_weight, up_weight)
            ],
            axis=1,
        )

    small_far = hop(small, 2)
    cap_far = hop(jnp.stack([cap_slice(2), cap_slice(3)]), 2)
    fetched = hop(jnp.stack([head_columns(m, near * half_depth, half_depth) for m in (2, 3)]), 2)
    thin_far = hop(jnp.stack([unit_columns(2), unit_columns(3)]), 2)
    token_own = tokens[0]
    small, small_far, cap_far, fetched, token_own, thin_far = join(
        small, small_far, cap_far, fetched, token_own, thin_far
    )

    token_far = hop(token_own, 2)
    thin_near = hop(jnp.stack([unit_columns(1), thin_far[1]]), 1)
    thin_all = jnp.stack(natural_order([unit_columns(0), thin_near[0], thin_far[0], thin_near[1]], own))
    gateup_weight = lax.all_gather(thin_all, "dp", axis=1, tiled=True).reshape(width, 2 * units)
    fetched_beside = dp_hop(fetched, 0)
    small = small + small_far
    small_near = hop(small, 1)
    cap_near = hop(jnp.stack([cap_slice(1), cap_far[1]]), 1)
    caption_part = jnp.concatenate([cap_slice(0), cap_near[0], cap_far[0], cap_near[1]], axis=0)
    cap_partial = jnp.concatenate(
        [mm(caption_part, capkey_weight).astype(bf16), mm(caption_part, capvalue_weight).astype(bf16)],
        axis=0,
    )

    def cap_columns(mask):
        return lax.dynamic_slice_in_dim(cap_partial, (own ^ mask) * part, part, 1)

    cap_sent = jnp.stack([cap_columns(3), cap_columns(1)])
    cap_kept = jnp.stack([cap_columns(2), cap_columns(0)])
    token_two = jnp.stack([token_own, token_far])
    (
        token_two, thin_all, fetched_beside, small_near, cap_sent, cap_kept
    ) = join(token_two, thin_all, fetched_beside, small_near, cap_sent, cap_kept)

    token_near = hop(token_two, 1)
    token_all = jnp.concatenate([token_two[0], token_near[0], token_two[1], token_near[1]], axis=0)
    fetched_all = jnp.concatenate(
        [jnp.where(near == 0, fetched, fetched_beside), jnp.where(near == 0, fetched_beside, fetched)],
        axis=1,
    )
    fetched_near = hop(jnp.stack([head_columns(1, 0, depth), fetched_all[1]]), 1)
    cap_inner = hop(cap_sent, 1)
    top = dp_bits() - 1

    def cap_split(values, bit):
        half = values.shape[2] // 2
        return [
            lax.dynamic_slice_in_dim(values, side * half, half, 2)
            for side in (dp_place(bit), 1 - dp_place(bit))
        ]

    token_all, fetched_near, cap_inner = join(token_all, fetched_near, cap_inner)

    small = small + small_near
    modulation = small[: 6 * width].reshape(6, 1, width)
    shift_mix, scale_mix, gate_mix, shift_feed, scale_feed, gate_feed = [modulation[i] for i in range(6)]
    gain_mix = small[6 * width : 7 * width][None]
    gain_feed = small[7 * width : 8 * width][None]
    places = small[8 * width :].reshape(2, count, rows)
    order = own ^ jnp.arange(count, dtype=jnp.int32)
    places_rel = jnp.concatenate(natural_order([places[:, m] for m in masks], own), axis=1)
    slots_rel = (order[:, None] * rows + jnp.arange(rows, dtype=jnp.int32)[None]).reshape(seq)
    live_bias = jnp.where(slots_rel < item_lengths[0], 0.0, masked_score).astype(f32)[:, None]
    text_live = (
        jnp.concatenate(
            natural_order(
                [caption_mask[0, m * text_rows : (m + 1) * text_rows] for m in masks], own
            )
        )
        > 0
    )
    text_bias = jnp.where(text_live, 0.0, masked_score).astype(f32)[:, None]
    quarter = head_size // 4
    lane = jnp.arange(128, dtype=jnp.int32)
    frequency = jnp.exp(-jnp.log(rope_base) * (lane % quarter).astype(f32) / quarter)[None]
    by_row = (lane % head_size < 2 * quarter)[None]
    angles = jnp.where(by_row, places_rel[0][:, None], places_rel[1][:, None]) * frequency
    sign = jnp.where((lane // quarter) % 2 == 0, -1.0, 1.0).astype(f32)[None]
    tables = (jnp.cos(angles), jnp.sin(angles) * sign)

    def align(values, mask):
        return jnp.concatenate(
            [swap_blocks(values[:text], mask, count), swap_blocks(values[text:], mask, count)], axis=0
        )

    cap_passed = hop((cap_kept[0].astype(f32) + align(cap_inner[0], 1).astype(f32)).astype(bf16), 2)
    unit_all, _ = rms_parts(token_all.astype(f32))
    normed_all = (unit_all * gain_mix * (1.0 + scale_mix) + shift_mix).astype(bf16)
    qkv_rel = [head_columns(0, 0, depth), fetched_near[0], fetched_all[0], fetched_near[1]]
    qkv_weight = jnp.concatenate(natural_order(qkv_rel, own), axis=0)
    qkv = mm(normed_all, qkv_weight)
    cap_passed, qkv, tables = join(cap_passed, qkv, tables)
    cap_raw = (
        cap_kept[1].astype(f32)
        + align(cap_inner[1], 1).astype(f32)
        + align(cap_passed, 2).astype(f32)
    )
    capkey_raw, capvalue_low = cap_raw[:text], cap_raw[text:].astype(bf16)

    query_square, key_square, cap_square = sum_rows_rel(
        [
            jnp.sum(jnp.square(qkv[:, :part]), axis=-1),
            jnp.sum(jnp.square(qkv[:, part : 2 * part]), axis=-1),
            jnp.sum(capkey_raw * capkey_raw, axis=-1),
        ],
        count,
    )
    query_inverse = lax.rsqrt(query_square / width + norm_eps)[:, None]
    key_inverse = lax.rsqrt(key_square / width + norm_eps)[:, None]
    capkey_inverse = lax.rsqrt(cap_square / width + norm_eps)[:, None]
    own_gains = norm_gains.astype(f32)
    capkey_low = (capkey_raw * capkey_inverse * own_gains[3:4]).astype(bf16)
    tanh_gate = jnp.tanh(head_gate.astype(f32))
    own_tanh = lax.dynamic_slice_in_dim(tanh_gate, own * own_heads, own_heads, 0)
    tanh_lane = jnp.repeat(own_tanh, head_size)[None]
    block_rows = 256 if seq % 256 == 0 else seq

    query_live = (own * rows + jnp.arange(rows, dtype=jnp.int32)) < item_lengths[0]
    grad_out = cotangent[0].astype(f32) * query_live[:, None].astype(f32)
    grad_ffn = (gate_feed * grad_out).astype(bf16)
    cap_items, cap_items_sent = cap_split(caption[0][None], top)
    grad_ffn, cap_items_sent, query_inverse, key_inverse, capkey_low = join(
        grad_ffn, cap_items_sent, query_inverse, key_inverse, capkey_low
    )
    grad_ffn_far = hop(grad_ffn, 2)
    cap_items = jnp.concatenate([cap_items, dp_hop(cap_items_sent, top)], axis=0)
    attended, query_low, key_low, value_low, lse = attend_forward(
        qkv, (query_inverse, key_inverse), (own_gains[1:2], own_gains[2:3]), tables,
        capkey_low, capvalue_low, live_bias, text_bias, tanh_lane, block_rows,
    )
    attended, grad_ffn_far, cap_items = join(attended, grad_ffn_far, cap_items)

    branch_part = mm(attended, outproj_weight).astype(bf16)
    branch_near = hop(
        jnp.stack([branch_part[3 * rows :], branch_part[rows : 2 * rows]]), 1
    )
    branch_passed = (
        branch_part[2 * rows : 3 * rows].astype(f32) + branch_near[0].astype(f32)
    ).astype(bf16)
    branch_kept = branch_part[:rows].astype(f32) + branch_near[1].astype(f32)
    branch_passed, branch_kept, grad_ffn_far = join(branch_passed, branch_kept, grad_ffn_far)
    branch_passed = hop(branch_passed, 2)
    grad_ffn_near = hop(jnp.stack([grad_ffn, grad_ffn_far]), 1)
    grad_ffn_rel = [grad_ffn, grad_ffn_near[0], grad_ffn_far, grad_ffn_near[1]]
    grad_ffn_all = jnp.concatenate(grad_ffn_rel, axis=0)
    branch_passed, gateup_weight, grad_ffn_all, *grad_ffn_rel = join(
        branch_passed, gateup_weight, grad_ffn_all, *grad_ffn_rel
    )
    branch = branch_kept + branch_passed.astype(f32)
    token_float = token_own.astype(f32)
    middle = token_float + gate_mix * branch

    unit_feed, inverse_feed = rms_parts(middle)
    normed_feed = (unit_feed * gain_feed * (1.0 + scale_feed) + shift_feed).astype(bf16)
    feed_far = hop(normed_feed, 2)
    feed_near = hop(normed_feed, 1)
    hidden_early, grads_early = feed_forward(
        [normed_feed, feed_near], grad_ffn_rel[:2], gateup_weight, down_weight, units_block
    )
    early = mm_nt(grads_early, gateup_weight).astype(bf16)
    for bit in reversed(range(1, top)):
        cap_items, cap_items_sent = cap_split(cap_items, bit)
        cap_items = jnp.concatenate([cap_items, dp_hop(cap_items_sent, bit)], axis=0)
    cap_items, cap_items_sent = cap_split(cap_items, 0)
    feed_far, hidden_early, early, cap_items_sent = join(feed_far, hidden_early, early, cap_items_sent)
    feed_rel = [normed_feed, feed_near, feed_far, hop(feed_far, 1)]
    hidden_late, grads_late = feed_forward(
        feed_rel[2:], grad_ffn_rel[2:], gateup_weight, down_weight, units_block
    )
    late = mm_nt(grads_late, gateup_weight).astype(bf16)
    late_near = hop(late[rows:], 1)
    passed = (late[:rows].astype(f32) + late_near.astype(f32)).astype(bf16)
    passed, early, hidden_late, grads_late, cap_items_sent = join(
        passed, early, hidden_late, grads_late, cap_items_sent
    )

    passed = hop(passed, 2)
    early_near = hop(early[rows:], 1)
    cap_items = jnp.concatenate([cap_items, dp_hop(cap_items_sent, 0)], axis=0)
    hidden = jnp.concatenate([hidden_early, hidden_late], axis=0)
    down_blocks = dp_blocks(mm_tn(hidden, grad_ffn_all).astype(bf16))
    down_cut = width // 2
    down_first = dp_hop(dp_sent(down_blocks, 0, down_cut), 0)
    feed_all = jnp.concatenate(feed_rel, axis=0)
    grad_units = jnp.concatenate([grads_early, grads_late], axis=0)
    gateup_blocks = dp_blocks(mm_tn(feed_all, grad_units).astype(bf16))
    down_sent = dp_sent(down_blocks, down_cut, width)
    passed, early_near, down_first, gateup_blocks, down_sent, cap_items = join(
        passed, early_near, down_first, gateup_blocks, down_sent, cap_items
    )
    down_second = dp_hop(down_sent, 0)
    grad_normfeed = early[:rows].astype(f32) + early_near.astype(f32) + passed.astype(f32)

    dshift_feed = jnp.sum(grad_normfeed, axis=0)
    dscale_feed = jnp.sum(grad_normfeed * (unit_feed * gain_feed), axis=0)
    grad_scaledfeed = grad_normfeed * (1.0 + scale_feed)
    gain_feed_grad = jnp.sum(grad_scaledfeed * unit_feed, axis=0)
    grad_middle = grad_out + rms_back(unit_feed, inverse_feed, grad_scaledfeed * gain_feed)
    dgate_mix = jnp.sum(grad_middle * branch, axis=0)

    grad_branch = (gate_mix * grad_middle).astype(bf16)
    grad_branch, gateup_blocks = join(grad_branch, gateup_blocks)
    grad_branch_far = hop(grad_branch, 2)
    ffn_part = mm(hidden, down_weight).astype(bf16)
    first_cut, second_cut = 2 * units * 2 // 8, 2 * units * 5 // 8
    gateup_sent = dp_sent(gateup_blocks, 0, first_cut)
    grad_branch_far, down_second, ffn_part, gateup_sent, cap_items = join(
        grad_branch_far, down_second, ffn_part, gateup_sent, cap_items
    )
    gateup_first = dp_hop(gateup_sent, 0)
    cap_items_far = hop(cap_items, 2)
    grad_branch_two = jnp.stack([grad_branch, grad_branch_far])
    grad_branch_near = hop(grad_branch_two, 1)
    ffn_near = hop(jnp.stack([ffn_part[3 * rows :], ffn_part[rows : 2 * rows]]), 1)
    grad_branch_all = jnp.concatenate(
        [grad_branch, grad_branch_near[0], grad_branch_far, grad_branch_near[1]], axis=0
    )
    down_joined = [
        dp_joined(down_blocks, down_first, 0, down_cut),
        dp_joined(down_blocks, down_second, down_cut, width),
    ]
    down_kept = jnp.concatenate([kept for kept, _ in down_joined], axis=-1)
    down_line = dp_hop(jnp.concatenate([sent for _, sent in down_joined], axis=-1), 1)
    grad_attended = mm_nt(grad_branch_all, outproj_weight).astype(bf16)
    dquery_text, dcapkey, grad_capvalue, dtanh = text_backward(
        query_low, capkey_low, capvalue_low, grad_attended, lse, text_bias, tanh_lane, seq
    )
    outproj_blocks = dp_blocks(mm_tn(attended, grad_branch_all).astype(bf16))
    outproj_sent = dp_sent(outproj_blocks, 0, width)
    (
        dquery_text, dcapkey, grad_capvalue, dtanh, gateup_first, down_line, ffn_near, cap_items_far,
        outproj_sent,
    ) = join(
        dquery_text, dcapkey, grad_capvalue, dtanh, gateup_first, down_line, ffn_near, cap_items_far,
        outproj_sent,
    )
    outproj_beside = dp_hop(outproj_sent, 0)
    capkey_unit = capkey_raw * capkey_inverse
    capkey_scaled = dcapkey * own_gains[3:4]
    (cap_dot,) = sum_rows_rel([jnp.sum(capkey_scaled * capkey_unit, axis=-1)], count)
    grad_capkey = (
        capkey_inverse * (capkey_scaled - capkey_unit * (cap_dot[:, None] / width))
    ).astype(bf16)
    gain_capkey_grad = jnp.sum(dcapkey * capkey_unit, axis=0)
    grad_cap = jnp.concatenate([grad_capkey, grad_capvalue], axis=1)
    ffn_passed = (
        ffn_part[2 * rows : 3 * rows].astype(f32) + ffn_near[0].astype(f32)
    ).astype(bf16)
    gateup_sent = dp_sent(gateup_blocks, first_cut, second_cut)
    dquery_text, grad_cap, ffn_passed, gateup_sent, outproj_beside = join(
        dquery_text, grad_cap, ffn_passed, gateup_sent, outproj_beside
    )

    ffn_passed = hop(ffn_passed, 2)
    gateup_second = dp_hop(gateup_sent, 0)
    down_state = dp_next((down_kept, down_line), 2) if top >= 2 else (down_kept, down_line)
    gateup_kept, gateup_line = dp_joined(gateup_blocks, gateup_first, 0, first_cut)
    gateup_line = dp_hop(gateup_line, 1)
    cap_grads = jnp.stack([grad_cap, dp_hop(grad_cap, top)])
    query_unrot, key_unrot, grad_value = self_backward(
        query_low, key_low, value_low, grad_attended, lse, dquery_text, tables, live_bias, block_rows
    )
    gateup_sent = dp_sent(gateup_blocks, second_cut, 2 * units)
    (
        query_unrot, key_unrot, grad_value, ffn_passed, gateup_second, down_arrived, gateup_line,
        cap_grads, gateup_sent,
    ) = join(
        query_unrot, key_unrot, grad_value, ffn_passed, gateup_second, down_state[1], gateup_line,
        cap_grads, gateup_sent,
    )
    down_state = (down_state[0], down_arrived)
    cap_items_two = jnp.stack([cap_items, cap_items_far], axis=1)

    gateup_third = dp_hop(gateup_sent, 0)
    second_kept, second_line = dp_joined(gateup_blocks, gateup_second, first_cut, second_cut)
    second_line = dp_hop(second_line, 1)
    down_sum = dp_total(down_state) if top <= 2 else dp_rest_from(down_state, 3)
    outproj_kept, outproj_line = dp_joined(outproj_blocks, outproj_beside, 0, width)
    outproj_line = dp_hop(outproj_line, 1)
    first_state = dp_next((gateup_kept, gateup_line), 2) if top >= 2 else (gateup_kept, gateup_line)
    query_unit = qkv[:, :part] * query_inverse
    key_unit = qkv[:, part : 2 * part] * key_inverse
    query_scaled = query_unrot * own_gains[1:2]
    key_scaled = key_unrot * own_gains[2:3]
    query_dot, key_dot = sum_rows_rel(
        [
            jnp.sum(query_scaled * query_unit, axis=-1),
            jnp.sum(key_scaled * key_unit, axis=-1),
        ],
        count,
    )
    gain_query_grad = jnp.sum(query_unrot * query_unit, axis=0)
    gain_key_grad = jnp.sum(key_unrot * key_unit, axis=0)
    grad_qkv = jnp.concatenate(
        [
            (query_inverse * (query_scaled - query_unit * (query_dot[:, None] / width))).astype(bf16),
            (key_inverse * (key_scaled - key_unit * (key_dot[:, None] / width))).astype(bf16),
            grad_value,
        ],
        axis=1,
    )
    qkv_blocks = dp_blocks(mm_tn(normed_all, grad_qkv).astype(bf16))
    qkv_sent = dp_sent(qkv_blocks, 0, 3 * part)
    qkv_sent, gateup_third, first_arrived, second_line, outproj_line = join(
        qkv_sent, gateup_third, first_state[1], second_line, outproj_line
    )
    first_state = (first_state[0], first_arrived)

    qkv_beside = dp_hop(qkv_sent, 0)
    third_kept, third_line = dp_joined(gateup_blocks, gateup_third, second_cut, 2 * units)
    third_line = dp_hop(third_line, 1)
    second_state = dp_next((second_kept, second_line), 2) if top >= 2 else (second_kept, second_line)
    for bit in reversed(range(1, top)):
        cap_grads = jnp.concatenate([cap_grads, dp_hop(cap_grads, bit)], axis=0)
    normmix_part = mm_nt(grad_qkv, qkv_weight).astype(bf16)
    normmix_near = hop(jnp.stack([normmix_part[3 * rows :], normmix_part[rows : 2 * rows]]), 1)
    normmix_passed = hop(
        (normmix_part[2 * rows : 3 * rows].astype(f32) + normmix_near[0].astype(f32)).astype(bf16), 2
    )
    (
        qkv_beside, third_line, normmix_passed, cap_grads, second_arrived, cap_items_two, outproj_line
    ) = join(
        qkv_beside, third_line, normmix_passed, cap_grads, second_state[1], cap_items_two, outproj_line
    )
    second_state = (second_state[0], second_arrived)
    outproj_state = (outproj_kept, outproj_line)
    if top >= 2:
        outproj_state = dp_next(outproj_state, 2)
    cap_items_near = hop(cap_items_two, 1)
    cap_items_all = jnp.stack(
        [cap_items_two[:, 0], cap_items_near[:, 0], cap_items_two[:, 1], cap_items_near[:, 1]], axis=1
    ).reshape(data_count * text, -1)

    qkv_kept, qkv_line = dp_joined(qkv_blocks, qkv_beside, 0, 3 * part)
    qkv_line = dp_hop(qkv_line, 1)
    third_state = dp_next((third_kept, third_line), 2) if top >= 2 else (third_kept, third_line)
    cap_grads = jnp.concatenate([cap_grads, dp_hop(cap_grads, 0)], axis=0)
    grad_normmix = (
        normmix_part[:rows].astype(f32) + normmix_near[1].astype(f32) + normmix_passed.astype(f32)
    )
    ffn_out = ffn_part[:rows].astype(f32) + ffn_near[1].astype(f32) + ffn_passed.astype(f32)
    block_out = (middle + gate_feed * ffn_out).astype(bf16)
    dgate_feed = jnp.sum(grad_out * ffn_out, axis=0)
    unit_mix, inverse_mix = rms_parts(token_float)
    dshift_mix = jnp.sum(grad_normmix, axis=0)
    dscale_mix = jnp.sum(grad_normmix * (unit_mix * gain_mix), axis=0)
    grad_scaledmix = grad_normmix * (1.0 + scale_mix)
    gain_mix_grad = jnp.sum(grad_scaledmix * unit_mix, axis=0)
    tokens_grad = (
        grad_middle + rms_back(unit_mix, inverse_mix, grad_scaledmix * gain_mix)
    ).astype(bf16)

    own_rows = jnp.zeros((3, width), f32)
    own_rows = lax.dynamic_update_slice(
        own_rows, jnp.stack([gain_query_grad, gain_key_grad, gain_capkey_grad]), (0, own * part)
    )
    gate_sums = lax.dynamic_update_slice(
        jnp.zeros((head_count,), f32), dtanh[0, ::head_size], (own * own_heads,)
    )
    sums = jnp.concatenate([gain_mix_grad, own_rows.reshape(-1), gain_feed_grad, gate_sums])
    grad_modulation = jnp.concatenate(
        [dshift_mix, dscale_mix, dgate_mix, dshift_feed, dscale_feed, dgate_feed]
    )
    message = jnp.concatenate([grad_modulation, sums])
    message = message + hop(message, 1)
    message = message + hop(message, 2)
    mod_width = 6 * width
    item_rows = jnp.concatenate([message[:mod_width], silu_low[0].astype(f32)]).astype(bf16)[None]
    totals = message[mod_width:]

    def wider(item_rows, totals, bit):
        flat = jnp.concatenate([item_rows.reshape(-1), totals.astype(bf16)])
        arrived = dp_hop(flat, bit)
        return (
            jnp.concatenate([item_rows, arrived[: item_rows.size].reshape(item_rows.shape)], axis=0),
            totals + arrived[item_rows.size :].astype(f32),
        )

    first_sum = dp_total(first_state) if top <= 2 else dp_rest_from(first_state, 3)
    second_sum = dp_total(second_state) if top <= 2 else dp_rest_from(second_state, 3)
    qkv_line, item_rows, totals, third_arrived, first_sum, second_sum, outproj_arrived = join(
        qkv_line, item_rows, totals, third_state[1], first_sum, second_sum, outproj_state[1]
    )
    outproj_state = (outproj_state[0], outproj_arrived)

    qkv_state = dp_next((qkv_kept, qkv_line), 2) if top >= 2 else (qkv_kept, qkv_line)
    third_state = (third_state[0], third_arrived)
    third_sum = dp_total(third_state) if top <= 2 else dp_rest_from(third_state, 3)
    gateup_pieces, gateup_sent = spread_pieces([first_sum, second_sum, third_sum], own)
    gateup_far = hop(gateup_sent, 2)
    item_rows, totals = wider(item_rows, totals, 0)
    cap_sum = mm_tn(cap_items_all, cap_grads.reshape(-1, cap_grads.shape[-1]))
    cap_pieces, cap_sent_far = spread_pieces([cap_sum], own)
    outproj_sum = dp_total(outproj_state) if top <= 2 else dp_rest_from(outproj_state, 3)
    owned_sent = jnp.concatenate([down_sum, outproj_sum], axis=0).astype(bf16)
    qkv_arrived, gateup_far, item_rows, totals, cap_sent_far, owned_sent = join(
        qkv_state[1], gateup_far, item_rows, totals, cap_sent_far, owned_sent
    )
    qkv_state = (qkv_state[0], qkv_arrived)

    qkv_sum = dp_total(qkv_state) if top <= 2 else dp_rest_from(qkv_state, 3)
    qkv_pieces, qkv_sent_far = spread_pieces([qkv_sum], own)
    qkv_far = hop(qkv_sent_far, 2)
    cap_far_rows = hop(cap_sent_far, 2)
    gateup_near = spread_near(gateup_pieces, gateup_far)
    owned = to_owner(owned_sent)
    item_rows, totals = wider(item_rows, totals, 1)
    qkv_far, cap_far_rows, gateup_near, item_rows, totals, owned = join(
        qkv_far, cap_far_rows, gateup_near, item_rows, totals, owned
    )
    qkv_near = spread_near(qkv_pieces, qkv_far)
    cap_near_rows = spread_near(cap_pieces, cap_far_rows)
    for bit in range(2, top + 1):
        item_rows, totals = wider(item_rows, totals, bit)
    gate_grad, up_grad = spread_result(gateup_pieces, gateup_far, gateup_near, [units] * 2, own)
    query_grad, key_grad, value_grad = spread_result(qkv_pieces, qkv_far, qkv_near, [part] * 3, own)
    capkey_grad, capvalue_grad = spread_result(cap_pieces, cap_far_rows, cap_near_rows, [part] * 2, own)
    modulation_rows = item_rows[:, :mod_width].astype(f32)
    silu_rows = item_rows[:, mod_width:].astype(f32)
    owner = place * count + own
    devices = count * data_count
    cd_rows = silu_rows.shape[1] // devices
    adaln_wgrad = lax.dot_general(
        lax.dynamic_slice_in_dim(silu_rows, owner * cd_rows, cd_rows, 1),
        modulation_rows,
        (((0,), (0,)), ((), ())),
        precision=lax.Precision.HIGHEST,
        preferred_element_type=f32,
    )
    bias_rows = mod_width // devices
    adaln_bgrad = lax.dynamic_slice_in_dim(
        jnp.sum(modulation_rows, axis=0), owner * bias_rows, bias_rows, 0
    )
    gains_grad = lax.dynamic_slice_in_dim(
        totals[: 5 * width].reshape(5, width), owner * (width // devices), width // devices, 1
    )
    headgate_grad = totals[5 * width :] * (1.0 - tanh_gate * tanh_gate)

    down_grad, outproj_grad = owned[: down_sum.shape[0]], owned[down_sum.shape[0] :]
    return (
        block_out[None],
        tokens_grad[None],
        adaln_wgrad,
        adaln_bgrad,
        query_grad,
        key_grad,
        value_grad,
        outproj_grad,
        capkey_grad,
        capvalue_grad,
        gains_grad,
        headgate_grad,
        gate_grad,
        up_grad,
        down_grad,
    )


def solution(mesh):
    return jax.shard_map(
        on_device,
        mesh=mesh,
        in_specs=(
            P("dp", "fsdp", None),
            P("dp", "fsdp", None),
            P("dp", None),
            P("dp"),
            P("dp"),
            P("dp", None, "fsdp"),
            P(),
            P("fsdp", None),
            P("fsdp"),
            P("fsdp", None),
            P("fsdp", None),
            P("fsdp", None),
            P("fsdp", None),
            P("fsdp", None),
            P("fsdp", None),
            P(None, "fsdp"),
            P(),
            P("fsdp", None),
            P("fsdp", None),
            P("fsdp", None),
            P("dp", "fsdp", None),
        ),
        out_specs=(
            P("dp", "fsdp", None),
            P("dp", "fsdp", None),
            P(("dp", "fsdp"), None),
            P(("dp", "fsdp")),
            P(("dp", "fsdp"), None),
            P(("dp", "fsdp"), None),
            P(("dp", "fsdp"), None),
            P(("dp", "fsdp"), None),
            P(("dp", "fsdp"), None),
            P(("dp", "fsdp"), None),
            P(None, ("dp", "fsdp")),
            P(),
            P(("dp", "fsdp"), None),
            P(("dp", "fsdp"), None),
            P(("dp", "fsdp"), None),
        ),
        check_vma=False,
    )
```

```python
import jax
import jax.numpy as jnp
from jax import lax
from jax.experimental import pallas as pl
from jax.experimental.pallas import tpu as pltpu
from jax.sharding import PartitionSpec as P

norm_eps = 1e-06
rope_base = 10000.0
masked_score = -1e30
f32 = jnp.float32
bf16 = jnp.bfloat16


def mm(left_side, right_side):
    return lax.dot_general(
        left_side, right_side, (((1,), (0,)), ((), ())), preferred_element_type=f32
    )


def mm_nt(left_side, right_side):
    return lax.dot_general(
        left_side, right_side, (((1,), (1,)), ((), ())), preferred_element_type=f32
    )


def mm_tn(left_side, right_side):
    return lax.dot_general(
        left_side, right_side, (((0,), (0,)), ((), ())), preferred_element_type=f32
    )


def rms_parts(values):
    inverse = lax.rsqrt(jnp.mean(values * values, axis=-1, keepdims=True) + norm_eps)
    return (values * inverse, inverse)


def rms_back(unit_rows, inverse, grad_unit):
    return inverse * (
        grad_unit - unit_rows * jnp.mean(grad_unit * unit_rows, axis=-1, keepdims=True)
    )


def hop(values, mask):
    count = lax.axis_size("fsdp")
    return lax.ppermute(values, "fsdp", [(i, i ^ mask) for i in range(count)])


def gather_rel(values):
    two = jnp.stack([values, hop(values, 2)])
    other = hop(two, 1)
    return [values, other[0], two[1], other[1]]


def scatter_rel(blocks):
    arrived = hop(jnp.stack([blocks[3], blocks[1]]), 1)
    passed = hop((blocks[2].astype(f32) + arrived[0].astype(f32)).astype(bf16), 2)
    return blocks[0].astype(f32) + arrived[1].astype(f32) + passed.astype(f32)


def trade_rel(blocks, middle=None):
    far = hop(jnp.stack([blocks[2], blocks[3]]), 2)
    if middle is not None:
        far = middle(far)
    beside = hop(jnp.stack([blocks[1], far[1]]), 1)
    return [blocks[0], beside[0], far[0], beside[1]]


def swap_blocks(values, mask, count):
    rows = values.shape[0] // count
    return jnp.concatenate(
        [values[(m ^ mask) * rows : ((m ^ mask) + 1) * rows] for m in range(count)], axis=0
    )


def sum_rows_rel(columns, count, plain=()):
    swapped = len(columns)
    columns = list(columns) + list(plain)
    ends = [0]
    for column in columns:
        ends.append(ends[-1] + column.shape[0])
    total = jnp.concatenate(columns)
    for mask in (1, 2):
        arrived = hop(total, mask)
        total = total + jnp.concatenate(
            [swap_blocks(arrived[i:j], mask, count) for i, j in zip(ends, ends[1 : swapped + 1])]
            + [arrived[ends[swapped] :]]
        )
    return [total[i:j] for i, j in zip(ends, ends[1:])]


def natural_order(pieces, own):
    far, near = own // 2, own % 2
    mixed = [[jnp.where(near == 0, pieces[2 * i + j], pieces[2 * i + 1 - j]) for j in range(2)] for i in range(2)]
    return [jnp.where(far == 0, mixed[i][j], mixed[1 - i][j]) for i in range(2) for j in range(2)]


def join(*values):
    return lax.optimization_barrier(values)


def dp_bits():
    return lax.axis_size("dp").bit_length() - 1


def dp_hop(values, bit):
    count = lax.axis_size("dp")
    return lax.ppermute(values, "dp", [(i, i ^ (1 << bit)) for i in range(count)])


def dp_place(bit):
    return (lax.axis_index("dp") >> bit) & 1


def pick(values, axis, index):
    return lax.dynamic_index_in_dim(values, index, axis, keepdims=False)


def dp_blocks(partial):
    return partial.reshape(lax.axis_size("dp"), -1, partial.shape[1])


def dp_half(blocks, bit, other):
    pairs = blocks.reshape((-1, 2) + blocks.shape[1:])
    return pick(pairs, 1, 1 - dp_place(bit) if other else dp_place(bit))


def dp_sent(blocks, start, stop):
    return dp_half(blocks[..., start:stop], 0, True)


def dp_joined(blocks, arrived, start, stop):
    return dp_sums((dp_half(blocks[..., start:stop], 0, False), arrived), 1)


def dp_sums(state, bit):
    kept, arrived = state

    def half(other):
        return (
            dp_half(kept, bit, other).astype(f32) + dp_half(arrived, bit, other).astype(f32)
        ).astype(bf16)

    return (half(False), half(True))


def dp_next(state, bit):
    kept, sent = dp_sums(state, bit)
    return (kept, dp_hop(sent, bit))


def dp_total(state):
    return state[0][0].astype(f32) + state[1][0].astype(f32)


def dp_rest_from(state, start):
    for bit in range(start, dp_bits()):
        state = dp_next(state, bit)
    return dp_total(state)


def dp_rest(state):
    return dp_rest_from(state, 1)


def cap_order(values, top):
    return values.reshape(-1, values.shape[-1])


def spread_pieces(totals, own):
    count = lax.axis_size("fsdp")
    low = jnp.concatenate([total.astype(bf16) for total in totals], axis=1)
    rows = low.shape[0] // count
    pieces = [lax.dynamic_slice_in_dim(low, (own ^ m) * rows, rows, 0) for m in range(count)]
    return (jnp.stack(pieces[:2]), jnp.stack(pieces[2:]))


def spread_near(pieces, far):
    return hop(jnp.stack([pieces[1], far[1]]), 1)


def spread_result(pieces, far, near, widths, own):
    results, start = [], 0
    for width in widths:
        part = [
            piece[:, start : start + width] for piece in (pieces[0], near[0], far[0], near[1])
        ]
        results.append(jnp.concatenate(natural_order(part, own), axis=1).astype(f32))
        start += width
    return results


def to_owner(total):
    data_count, count = lax.axis_size("dp"), lax.axis_size("fsdp")
    pairs = [(d * count + f, f * data_count + d) for d in range(data_count) for f in range(count)]
    return lax.ppermute(total.astype(bf16), ("dp", "fsdp"), pairs).astype(f32)


def lane_of(shape):
    return lax.broadcasted_iota(jnp.int32, shape, len(shape) - 1)


def rotate_lanes(values, cosines, sines):
    lanes = lane_of(values.shape)
    even = lax.rem(lax.div(lanes, 16), 2) == 0
    width = values.shape[-1]
    partner = jnp.where(even, pltpu.roll(values, width - 16, 1), pltpu.roll(values, 16, 1))
    return values * cosines + partner * sines


def as_column(row):
    return jnp.transpose(jnp.broadcast_to(row, (8, row.shape[1])))[:, :1]


def head_lanes(values, head, spare):
    lanes = lane_of(values.shape)
    mine = (lanes < 64) if head == 0 else (lanes >= 64)
    mark = 64 if head == 0 else 0
    return jnp.where(mine, values, jnp.where(lanes == mark, spare, jnp.zeros_like(values)))


def attend_body(
    q_ref, k_ref, v_ref, qinv_ref, kinv_ref, qg_ref, kg_ref, cosq_ref, sinq_ref, cosk_ref, sink_ref,
    ck_ref, cv_ref, live_ref, text_ref, tanh_ref,
    out_ref, qlow_ref, klow_ref, vlow_ref, lse_ref,
    km, vm, cm, cvm,
):
    @pl.when(pl.program_id(1) == 0)
    def _():
        key = rotate_lanes(
            k_ref[...] * as_column(kinv_ref[...]) * kg_ref[...], cosk_ref[...], sink_ref[...]
        ).astype(bf16)
        value = v_ref[...].astype(bf16)
        klow_ref[...] = key
        vlow_ref[...] = value
        one = jnp.ones((), bf16)
        for head in range(2):
            km[head] = head_lanes(key, head, live_ref[...].astype(bf16))
            vm[head] = head_lanes(value, head, one)
            cm[head] = head_lanes(ck_ref[...], head, text_ref[...].astype(bf16))
            cvm[head] = head_lanes(cv_ref[...], head, one)

    query = rotate_lanes(
        q_ref[...] * as_column(qinv_ref[...]) * qg_ref[...], cosq_ref[...], sinq_ref[...]
    ).astype(bf16)
    qlow_ref[...] = query
    scaled = query * jnp.asarray(0.125, bf16)
    lanes = lane_of(out_ref.shape)
    results, stats = [], []
    for head in range(2):
        part = head_lanes(scaled, head, jnp.ones((), bf16))
        mark = 64 if head == 0 else 0

        def one_side(keys, values):
            scores = mm_nt(part, keys)
            peak = jnp.max(scores, axis=-1, keepdims=True)
            weights = jnp.exp(scores - peak).astype(bf16)
            mixed = mm(weights, values)
            amount = mixed[:, mark : mark + 1]
            stats.append(peak + jnp.log(amount))
            return mixed / amount

        own = one_side(km[head], vm[head])
        text = one_side(cm[head], cvm[head])
        results.append(own + tanh_ref[...] * text)
    out_ref[...] = jnp.where(lanes < 64, results[0], results[1]).astype(bf16)
    table = jnp.where(lanes == 0, stats[0], stats[1])
    table = jnp.where(lanes == 2, stats[2], table)
    lse_ref[...] = jnp.where(lanes == 3, stats[3], table)


def attend_forward(qkv, inverses, gains, tables, capkey, capvalue, live_bias, text_bias, tanh_lane, rows):
    seq, width = qkv.shape[0], qkv.shape[1] // 3
    pairs, text = width // 128, capkey.shape[0]
    full = lambda p, i: (0, p)
    block = lambda p, i: (i, p)
    qrow = lambda p, i: (i, 0)
    whole = lambda p, i: (0, 0)
    return pl.pallas_call(
        attend_body,
        grid=(pairs, seq // rows),
        in_specs=[
            pl.BlockSpec((rows, 128), block),
            pl.BlockSpec((seq, 128), lambda p, i: (0, p + pairs)),
            pl.BlockSpec((seq, 128), lambda p, i: (0, p + 2 * pairs)),
            pl.BlockSpec((1, rows), lambda p, i: (0, i)),
            pl.BlockSpec((1, seq), whole),
            pl.BlockSpec((1, 128), full),
            pl.BlockSpec((1, 128), full),
            pl.BlockSpec((rows, 128), qrow),
            pl.BlockSpec((rows, 128), qrow),
            pl.BlockSpec((seq, 128), whole),
            pl.BlockSpec((seq, 128), whole),
            pl.BlockSpec((text, 128), full),
            pl.BlockSpec((text, 128), full),
            pl.BlockSpec((seq, 1), whole),
            pl.BlockSpec((text, 1), whole),
            pl.BlockSpec((1, 128), full),
        ],
        out_specs=[
            pl.BlockSpec((rows, 128), block),
            pl.BlockSpec((rows, 128), block),
            pl.BlockSpec((seq, 128), full),
            pl.BlockSpec((seq, 128), full),
            pl.BlockSpec((rows, 128), block),
        ],
        out_shape=[
            jax.ShapeDtypeStruct((seq, width), bf16),
            jax.ShapeDtypeStruct((seq, width), bf16),
            jax.ShapeDtypeStruct((seq, width), bf16),
            jax.ShapeDtypeStruct((seq, width), bf16),
            jax.ShapeDtypeStruct((seq, width), f32),
        ],
        scratch_shapes=[
            pltpu.VMEM((2, seq, 128), bf16),
            pltpu.VMEM((2, seq, 128), bf16),
            pltpu.VMEM((2, text, 128), bf16),
            pltpu.VMEM((2, text, 128), bf16),
        ],
        compiler_params=pltpu.CompilerParams(
            dimension_semantics=("arbitrary", "arbitrary"), vmem_limit_bytes=20 << 20
        ),
        cost_estimate=pl.CostEstimate(
            flops=seq * width,
            transcendentals=0,
            bytes_accessed=seq * width,
        ),
        name="attend_forward",
    )(
        qkv, qkv, qkv, inverses[0], inverses[1], gains[0], gains[1], tables[0], tables[1],
        tables[0], tables[1], capkey, capvalue, live_bias, text_bias, tanh_lane,
    )


def text_back_body(
    q_ref, ck_ref, cv_ref, do_ref, lse_ref, text_ref, tanh_ref,
    dq_ref, dck_ref, dcv_ref, dtanh_ref,
    cm, dck, dcv,
):
    step = pl.program_id(1)

    @pl.when(step == 0)
    def _():
        for head in range(2):
            cm[head] = head_lanes(ck_ref[...], head, text_ref[...].astype(bf16))
        dck[...] = jnp.zeros_like(dck)
        dcv[...] = jnp.zeros_like(dcv)
        dtanh_ref[...] = jnp.zeros_like(dtanh_ref)

    scaled = q_ref[...] * jnp.asarray(0.125, bf16)
    grad = do_ref[...]
    lse = lse_ref[...]
    grads = []
    for head in range(2):
        part = head_lanes(scaled, head, jnp.ones((), bf16))
        grad_part = head_lanes(grad, head, jnp.zeros((), bf16))
        gate = tanh_ref[:, 64 * head : 64 * head + 1]
        probs = jnp.exp(mm_nt(part, cm[head]) - lse[:, 2 * head + 1 : 2 * head + 2])
        dprob = mm_nt(grad_part, cv_ref[...])
        total = jnp.sum(probs * dprob, axis=-1, keepdims=True)
        dscore = (probs * ((dprob - total) * gate)).astype(bf16)
        grads.append(mm(dscore, ck_ref[...]))

        def add(target, update):
            lanes = lane_of(target.shape)
            mine = (lanes < 64) if head == 0 else (lanes >= 64)
            target[...] += jnp.where(mine, update, jnp.zeros_like(update))

        add(dck, mm_tn(dscore, scaled))
        add(dcv, mm_tn(probs.astype(bf16), grad))
        add(dtanh_ref, jnp.broadcast_to(jnp.sum(total, axis=0, keepdims=True), dtanh_ref.shape))
    lanes = lane_of(dq_ref.shape)
    dq_ref[...] = jnp.where(lanes < 64, grads[0], grads[1])

    @pl.when(step == pl.num_programs(1) - 1)
    def _():
        dck_ref[...] = dck[...]
        dcv_ref[...] = (dcv[...] * tanh_ref[...]).astype(bf16)


def text_backward(query, capkey, capvalue, grad, lse, text_bias, tanh_lane, rows):
    seq, width = query.shape
    pairs, text = width // 128, capkey.shape[0]
    full = lambda p, i: (0, p)
    block = lambda p, i: (i, p)
    whole = lambda p, i: (0, 0)
    return pl.pallas_call(
        text_back_body,
        grid=(pairs, seq // rows),
        in_specs=[
            pl.BlockSpec((rows, 128), block),
            pl.BlockSpec((text, 128), full),
            pl.BlockSpec((text, 128), full),
            pl.BlockSpec((rows, 128), block),
            pl.BlockSpec((rows, 128), block),
            pl.BlockSpec((text, 1), whole),
            pl.BlockSpec((1, 128), full),
        ],
        out_specs=[
            pl.BlockSpec((rows, 128), block),
            pl.BlockSpec((text, 128), full),
            pl.BlockSpec((text, 128), full),
            pl.BlockSpec((8, 128), full),
        ],
        out_shape=[
            jax.ShapeDtypeStruct((seq, width), f32),
            jax.ShapeDtypeStruct((text, width), f32),
            jax.ShapeDtypeStruct((text, width), bf16),
            jax.ShapeDtypeStruct((8, width), f32),
        ],
        scratch_shapes=[
            pltpu.VMEM((2, text, 128), bf16),
            pltpu.VMEM((text, 128), f32),
            pltpu.VMEM((text, 128), f32),
        ],
        compiler_params=pltpu.CompilerParams(
            dimension_semantics=("arbitrary", "arbitrary"), vmem_limit_bytes=20 << 20
        ),
        cost_estimate=pl.CostEstimate(
            flops=40 * seq * text * width,
            transcendentals=seq * text * width // 64,
            bytes_accessed=seq * width * 16,
        ),
        name="text_backward",
    )(query, capkey, capvalue, grad, lse, text_bias, tanh_lane)


def self_back_body(
    q_ref, k_ref, v_ref, do_ref, lse_ref, dqt_ref, cosq_ref, sinq_ref, cosk_ref, sink_ref, live_ref,
    dq_ref, dk_ref, dv_ref,
    km, dk, dv,
):
    step = pl.program_id(1)

    @pl.when(step == 0)
    def _():
        for head in range(2):
            km[head] = head_lanes(k_ref[...], head, live_ref[...].astype(bf16))
        dk[...] = jnp.zeros_like(dk)
        dv[...] = jnp.zeros_like(dv)

    scaled = q_ref[...] * jnp.asarray(0.125, bf16)
    grad = do_ref[...]
    lse = lse_ref[...]
    grads = []
    for head in range(2):
        part = head_lanes(scaled, head, jnp.ones((), bf16))
        grad_part = head_lanes(grad, head, jnp.zeros((), bf16))
        probs = jnp.exp(mm_nt(part, km[head]) - lse[:, 2 * head : 2 * head + 1])
        dprob = mm_nt(grad_part, v_ref[...])
        total = jnp.sum(probs * dprob, axis=-1, keepdims=True)
        dscore = (probs * (dprob - total)).astype(bf16)
        grads.append(mm(dscore, k_ref[...]))

        def add(target, update):
            lanes = lane_of(target.shape)
            mine = (lanes < 64) if head == 0 else (lanes >= 64)
            target[...] += jnp.where(mine, update, jnp.zeros_like(update))

        add(dk, mm_tn(dscore, scaled))
        add(dv, mm_tn(probs.astype(bf16), grad))
    lanes = lane_of(dq_ref.shape)
    dq_ref[...] = rotate_lanes(
        (jnp.where(lanes < 64, grads[0], grads[1]) + dqt_ref[...]) * 0.125,
        cosq_ref[...],
        -sinq_ref[...],
    )

    @pl.when(step == pl.num_programs(1) - 1)
    def _():
        dk_ref[...] = rotate_lanes(dk[...], cosk_ref[...], -sink_ref[...])
        dv_ref[...] = dv[...].astype(bf16)


def self_backward(query, key, value, grad, lse, dquery_text, tables, live_bias, rows):
    seq, width = query.shape
    pairs = width // 128
    full = lambda p, i: (0, p)
    block = lambda p, i: (i, p)
    qrow = lambda p, i: (i, 0)
    whole = lambda p, i: (0, 0)
    return pl.pallas_call(
        self_back_body,
        grid=(pairs, seq // rows),
        in_specs=[
            pl.BlockSpec((rows, 128), block),
            pl.BlockSpec((seq, 128), full),
            pl.BlockSpec((seq, 128), full),
            pl.BlockSpec((rows, 128), block),
            pl.BlockSpec((rows, 128), block),
            pl.BlockSpec((rows, 128), block),
            pl.BlockSpec((rows, 128), qrow),
            pl.BlockSpec((rows, 128), qrow),
            pl.BlockSpec((seq, 128), whole),
            pl.BlockSpec((seq, 128), whole),
            pl.BlockSpec((seq, 1), whole),
        ],
        out_specs=[
            pl.BlockSpec((rows, 128), block),
            pl.BlockSpec((seq, 128), full),
            pl.BlockSpec((seq, 128), full),
        ],
        out_shape=[
            jax.ShapeDtypeStruct((seq, width), f32),
            jax.ShapeDtypeStruct((seq, width), f32),
            jax.ShapeDtypeStruct((seq, width), bf16),
        ],
        scratch_shapes=[
            pltpu.VMEM((2, seq, 128), bf16),
            pltpu.VMEM((seq, 128), f32),
            pltpu.VMEM((seq, 128), f32),
        ],
        compiler_params=pltpu.CompilerParams(
            dimension_semantics=("arbitrary", "arbitrary"), vmem_limit_bytes=20 << 20
        ),
        cost_estimate=pl.CostEstimate(
            flops=40 * seq * seq * width,
            transcendentals=seq * seq * width // 64,
            bytes_accessed=seq * width * 28,
        ),
        name="self_backward",
    )(query, key, value, grad, lse, dquery_text, tables[0], tables[1], tables[0], tables[1], live_bias)


def feed_body(x0_ref, x1_ref, g0_ref, g1_ref, gate_ref, up_ref, down_ref, hidden_ref, grads_ref):
    step = pl.program_id(0)
    block = down_ref.shape[0]
    units = grads_ref.shape[1] // 2
    rows_in = jnp.concatenate([x0_ref[...], x1_ref[...]], axis=0)
    grads_in = jnp.concatenate([g0_ref[...], g1_ref[...]], axis=0)
    gate = mm(rows_in, gate_ref[...])
    up = mm(rows_in, up_ref[...])
    grad_hidden = mm_nt(grads_in, down_ref[...])
    sigmoid = 1.0 / (1.0 + jnp.exp(-gate))
    silu = gate * sigmoid
    hidden_ref[...] = (silu * up).astype(bf16)
    start = pl.multiple_of(step * block, block)
    grads_ref[:, pl.ds(start, block)] = (
        grad_hidden * up * (sigmoid * (1.0 + gate * (1.0 - sigmoid)))
    ).astype(bf16)
    grads_ref[:, pl.ds(pl.multiple_of(units + start, block), block)] = (grad_hidden * silu).astype(bf16)


def feed_forward(rows_in, grads_in, gateup, down, units_block):
    rows, width = rows_in[0].shape
    units = down.shape[0]
    steps = units // units_block
    whole = pl.BlockSpec((rows, width), lambda j: (0, 0))
    return pl.pallas_call(
        feed_body,
        grid=(steps,),
        in_specs=[whole] * 4
        + [
            pl.BlockSpec((width, units_block), lambda j: (0, j)),
            pl.BlockSpec((width, units_block), lambda j: (0, j + steps)),
            pl.BlockSpec((units_block, width), lambda j: (j, 0)),
        ],
        out_specs=[
            pl.BlockSpec((2 * rows, units_block), lambda j: (0, j)),
            pl.BlockSpec((2 * rows, 2 * units), lambda j: (0, 0)),
        ],
        out_shape=[
            jax.ShapeDtypeStruct((2 * rows, units), bf16),
            jax.ShapeDtypeStruct((2 * rows, 2 * units), bf16),
        ],
        compiler_params=pltpu.CompilerParams(
            dimension_semantics=("arbitrary",), vmem_limit_bytes=32 << 20
        ),
        cost_estimate=pl.CostEstimate(
            flops=12 * rows * width * units,
            transcendentals=2 * rows * units,
            bytes_accessed=6 * width * units + 8 * rows * width + 12 * rows * units,
        ),
        name="feed_forward",
    )(*rows_in, *grads_in, gateup, gateup, down)


def project_body(
    own_ref, x_ref, gain_ref, scale_ref, shift_ref, w0_ref, w1_ref, w2_ref, w3_ref,
    normed_ref, out_ref, query_ref, key_ref,
):
    values = x_ref[...].astype(f32)
    inverse = lax.rsqrt(jnp.mean(values * values, axis=-1, keepdims=True) + norm_eps)
    normed_ref[...] = (
        values * inverse * gain_ref[...] * (1.0 + scale_ref[...]) + shift_ref[...]
    ).astype(bf16)
    depth = w0_ref.shape[0]
    total = None
    for m, w_ref in enumerate((w0_ref, w1_ref, w2_ref, w3_ref)):
        start = pl.multiple_of((own_ref[0] ^ m) * depth, depth)
        term = mm(normed_ref[:, pl.ds(start, depth)], w_ref[...])
        total = term if total is None else total + term
    out_ref[...] = total
    part = out_ref.shape[1] // 3
    ones = jnp.ones((8, part), f32)

    def squares(rows):
        return lax.dot_general(
            ones,
            rows * rows,
            (((1,), (1,)), ((), ())),
            precision=lax.Precision.HIGHEST,
            preferred_element_type=f32,
        )

    query_ref[...] = squares(total[:, :part])
    key_ref[...] = squares(total[:, part : 2 * part])


def project(own, tokens, gain, scale, shift, weights):
    seq, width = tokens.shape
    columns = weights[0].shape[1]
    rows = 256 if seq % 256 == 0 else seq
    row = lambda i, own: (0, 0)
    block = lambda i, own: (i, 0)
    flat = lambda i, own: (0, i)
    return pl.pallas_call(
        project_body,
        grid_spec=pltpu.PrefetchScalarGridSpec(
            num_scalar_prefetch=1,
            grid=(seq // rows,),
            in_specs=[pl.BlockSpec((rows, width), block)]
            + [pl.BlockSpec((1, width), row)] * 3
            + [pl.BlockSpec(weights[0].shape, row)] * 4,
            out_specs=[
                pl.BlockSpec((rows, width), block),
                pl.BlockSpec((rows, columns), block),
                pl.BlockSpec((8, rows), flat),
                pl.BlockSpec((8, rows), flat),
            ],
        ),
        out_shape=[
            jax.ShapeDtypeStruct((seq, width), bf16),
            jax.ShapeDtypeStruct((seq, columns), f32),
            jax.ShapeDtypeStruct((8, seq), f32),
            jax.ShapeDtypeStruct((8, seq), f32),
        ],
        compiler_params=pltpu.CompilerParams(
            dimension_semantics=("arbitrary",), vmem_limit_bytes=24 << 20
        ),
        cost_estimate=pl.CostEstimate(
            flops=seq * width, transcendentals=0, bytes_accessed=seq * width
        ),
        name="project",
    )(own[None], tokens, gain, scale, shift, *weights)


def project_back_body(own_ref, d_ref, w0_ref, w1_ref, w2_ref, w3_ref, out_ref):
    depth = w0_ref.shape[0]
    for m, w_ref in enumerate((w0_ref, w1_ref, w2_ref, w3_ref)):
        start = pl.multiple_of((own_ref[0] ^ m) * depth, depth)
        out_ref[:, pl.ds(start, depth)] = mm_nt(d_ref[...], w_ref[...]).astype(bf16)


def project_back(own, grads, weights):
    seq, columns = grads.shape
    width = weights[0].shape[0] * 4
    rows = 256 if seq % 256 == 0 else seq
    block = lambda i, own: (i, 0)
    return pl.pallas_call(
        project_back_body,
        grid_spec=pltpu.PrefetchScalarGridSpec(
            num_scalar_prefetch=1,
            grid=(seq // rows,),
            in_specs=[pl.BlockSpec((rows, columns), block)]
            + [pl.BlockSpec(weights[0].shape, lambda i, own: (0, 0))] * 4,
            out_specs=pl.BlockSpec((rows, width), block),
        ),
        out_shape=jax.ShapeDtypeStruct((seq, width), bf16),
        compiler_params=pltpu.CompilerParams(
            dimension_semantics=("arbitrary",), vmem_limit_bytes=24 << 20
        ),
        cost_estimate=pl.CostEstimate(
            flops=seq * width, transcendentals=0, bytes_accessed=seq * width
        ),
        name="project_back",
    )(own[None], grads, *weights)


def on_device(
    tokens,
    caption,
    caption_mask,
    item_lengths,
    item_band,
    positions,
    band_table,
    adaln_weight,
    adaln_bias,
    query_weight,
    key_weight,
    value_weight,
    outproj_weight,
    capkey_weight,
    capvalue_weight,
    norm_gains,
    head_gate,
    gate_weight,
    up_weight,
    down_weight,
    cotangent,
):
    own = lax.axis_index("fsdp")
    place = lax.axis_index("dp")
    count = lax.axis_size("fsdp")
    data_count = lax.axis_size("dp")
    near = dp_place(0)
    rows, width = tokens.shape[1:]
    seq = rows * count
    part = width // count
    head_count = head_gate.shape[0]
    head_size = width // head_count
    own_heads = head_count // count
    units = down_weight.shape[0]
    text_rows = caption.shape[1]
    text = text_rows * count
    cap_depth = capkey_weight.shape[0]
    masks = (0, 1, 2, 3)

    def split_rel(values):
        return [values[m * rows : (m + 1) * rows] for m in masks]

    band_onehot = item_band[:, None] == jnp.arange(band_table.shape[0], dtype=jnp.int32)[None, :]
    band_vector = jnp.dot(band_onehot.astype(bf16), band_table, preferred_element_type=f32)
    silu_low = jax.nn.silu(band_vector).astype(bf16)
    slice_depth = adaln_weight.shape[0]
    modulation_part = mm(
        lax.dynamic_slice_in_dim(silu_low, own * slice_depth, slice_depth, 1), adaln_weight
    )[0]
    modulation_part = modulation_part + lax.dynamic_update_slice(
        jnp.zeros_like(modulation_part), adaln_bias.astype(f32), (own * adaln_bias.shape[0],)
    )
    gains_part = lax.dynamic_update_slice(
        jnp.zeros((2, width), f32), norm_gains[0::4].astype(f32), (0, own * part)
    )
    places_part = lax.dynamic_update_slice(
        jnp.zeros((2, seq), f32), positions[0].astype(f32), (0, own * rows)
    )
    small = jnp.concatenate([modulation_part, gains_part.reshape(-1), places_part.reshape(-1)])

    def cap_slice(mask):
        return lax.dynamic_slice_in_dim(caption[0], (own ^ mask) * cap_depth, cap_depth, 1)

    depth = query_weight.shape[0]
    half_depth = depth // 2

    def head_columns(mask, start, length):
        return jnp.concatenate(
            [
                lax.dynamic_slice(w, (start, (own ^ mask) * part), (length, part))
                for w in (query_weight, key_weight, value_weight)
            ],
            axis=1,
        )

    thin = gate_weight.shape[0] // data_count
    units_block = 256 if units % 256 == 0 else units

    def unit_columns(mask):
        return jnp.concatenate(
            [
                lax.dynamic_slice(w, (place * thin, (own ^ mask) * units), (thin, units))
                for w in (gate_weight, up_weight)
            ],
            axis=1,
        )

    small_far = hop(small, 2)
    cap_far = hop(jnp.stack([cap_slice(2), cap_slice(3)]), 2)
    fetched = hop(jnp.stack([head_columns(m, near * half_depth, half_depth) for m in (2, 3)]), 2)
    thin_far = hop(jnp.stack([unit_columns(2), unit_columns(3)]), 2)
    token_own = tokens[0]
    small, small_far, cap_far, fetched, token_own, thin_far = join(
        small, small_far, cap_far, fetched, token_own, thin_far
    )

    token_far = hop(token_own, 2)
    thin_near = hop(jnp.stack([unit_columns(1), thin_far[1]]), 1)
    thin_all = jnp.stack(natural_order([unit_columns(0), thin_near[0], thin_far[0], thin_near[1]], own))
    gateup_weight = lax.all_gather(thin_all, "dp", axis=1, tiled=True).reshape(width, 2 * units)
    fetched_beside = dp_hop(fetched, 0)
    small = small + small_far
    small_near = hop(small, 1)
    cap_near = hop(jnp.stack([cap_slice(1), cap_far[1]]), 1)
    caption_part = jnp.concatenate(
        natural_order([cap_slice(0), cap_near[0], cap_far[0], cap_near[1]], own), axis=0
    )
    cap_partial = jnp.concatenate(
        [mm(caption_part, capkey_weight).astype(bf16), mm(caption_part, capvalue_weight).astype(bf16)],
        axis=0,
    )

    def cap_columns(mask):
        return lax.dynamic_slice_in_dim(cap_partial, (own ^ mask) * part, part, 1)

    cap_sent = jnp.stack([cap_columns(3), cap_columns(1)])
    cap_kept = jnp.stack([cap_columns(2), cap_columns(0)])
    cap_inner = hop(cap_sent, 1)
    cap_passed = (cap_kept[0].astype(f32) + cap_inner[0].astype(f32)).astype(bf16)
    token_two = jnp.stack([token_own, token_far])
    (
        token_two, thin_all, fetched_beside, small_near, cap_inner, cap_kept, cap_passed
    ) = join(token_two, thin_all, fetched_beside, small_near, cap_inner, cap_kept, cap_passed)
    cap_passed = hop(cap_passed, 2)

    token_near = hop(token_two, 1)
    token_all = jnp.concatenate([token_two[0], token_near[0], token_two[1], token_near[1]], axis=0)
    fetched_all = jnp.concatenate(
        [jnp.where(near == 0, fetched, fetched_beside), jnp.where(near == 0, fetched_beside, fetched)],
        axis=1,
    )
    fetched_near = hop(jnp.stack([head_columns(1, 0, depth), fetched_all[1]]), 1)
    top = dp_bits() - 1

    def cap_split(values, bit):
        half = values.shape[2] // 2
        return [
            lax.dynamic_slice_in_dim(values, side * half, half, 2)
            for side in (dp_place(bit), 1 - dp_place(bit))
        ]

    token_all, fetched_near = join(token_all, fetched_near)

    small = small + small_near
    modulation = small[: 6 * width].reshape(6, 1, width)
    shift_mix, scale_mix, gate_mix, shift_feed, scale_feed, gate_feed = [modulation[i] for i in range(6)]
    gain_mix = small[6 * width : 7 * width][None]
    gain_feed = small[7 * width : 8 * width][None]
    places = small[8 * width :].reshape(2, count, rows)
    order = own ^ jnp.arange(count, dtype=jnp.int32)
    places_rel = jnp.concatenate(natural_order([places[:, m] for m in masks], own), axis=1)
    slots_rel = (order[:, None] * rows + jnp.arange(rows, dtype=jnp.int32)[None]).reshape(seq)
    live_bias = jnp.where(slots_rel < item_lengths[0], 0.0, masked_score).astype(f32)[:, None]
    text_live = caption_mask[0] > 0
    text_bias = jnp.where(text_live, 0.0, masked_score).astype(f32)[:, None]
    quarter = head_size // 4
    lane = jnp.arange(128, dtype=jnp.int32)
    frequency = jnp.exp(-jnp.log(rope_base) * (lane % quarter).astype(f32) / quarter)[None]
    by_row = (lane % head_size < 2 * quarter)[None]
    angles = jnp.where(by_row, places_rel[0][:, None], places_rel[1][:, None]) * frequency
    sign = jnp.where((lane // quarter) % 2 == 0, -1.0, 1.0).astype(f32)[None]
    tables = (jnp.cos(angles), jnp.sin(angles) * sign)

    qkv_rel = [head_columns(0, 0, depth), fetched_near[0], fetched_all[0], fetched_near[1]]
    normed_all, qkv, query_square, key_square = project(
        own, token_all, gain_mix, scale_mix, shift_mix, qkv_rel
    )
    cap_passed, query_square, key_square = join(cap_passed, query_square, key_square)
    cap_raw = cap_kept[1].astype(f32) + cap_inner[1].astype(f32) + cap_passed.astype(f32)
    capkey_raw, capvalue_low = cap_raw[:text], cap_raw[text:].astype(bf16)

    query_square, key_square, cap_square = sum_rows_rel(
        [
            query_square[0],
            key_square[0],
        ],
        count,
        [jnp.sum(capkey_raw * capkey_raw, axis=-1)],
    )
    query_inverse = lax.rsqrt(query_square / width + norm_eps)[None]
    key_inverse = lax.rsqrt(key_square / width + norm_eps)[None]
    capkey_inverse = lax.rsqrt(cap_square / width + norm_eps)[:, None]
    own_gains = norm_gains.astype(f32)
    capkey_low = (capkey_raw * capkey_inverse * own_gains[3:4]).astype(bf16)
    tanh_gate = jnp.tanh(head_gate.astype(f32))
    own_tanh = lax.dynamic_slice_in_dim(tanh_gate, own * own_heads, own_heads, 0)
    tanh_lane = jnp.repeat(own_tanh, head_size)[None]
    block_rows = 256 if seq % 256 == 0 else seq

    query_live = (own * rows + jnp.arange(rows, dtype=jnp.int32)) < item_lengths[0]
    grad_out = cotangent[0].astype(f32) * query_live[:, None].astype(f32)
    grad_ffn = (gate_feed * grad_out).astype(bf16)
    cap_items, cap_items_sent = cap_split(caption[0][None], top)
    grad_ffn, cap_items_sent, query_inverse, key_inverse, capkey_low = join(
        grad_ffn, cap_items_sent, query_inverse, key_inverse, capkey_low
    )
    grad_ffn_far = hop(grad_ffn, 2)
    cap_items = jnp.concatenate([cap_items, dp_hop(cap_items_sent, top)], axis=0)
    attended, query_low, key_low, value_low, lse = attend_forward(
        qkv, (query_inverse, key_inverse), (own_gains[1:2], own_gains[2:3]), tables,
        capkey_low, capvalue_low, live_bias, text_bias, tanh_lane, block_rows,
    )
    attended, grad_ffn_far, cap_items = join(attended, grad_ffn_far, cap_items)

    branch_part = mm(attended, outproj_weight).astype(bf16)
    branch_near = hop(
        jnp.stack([branch_part[3 * rows :], branch_part[rows : 2 * rows]]), 1
    )
    branch_passed = (
        branch_part[2 * rows : 3 * rows].astype(f32) + branch_near[0].astype(f32)
    ).astype(bf16)
    branch_kept = branch_part[:rows].astype(f32) + branch_near[1].astype(f32)
    branch_passed, branch_kept, grad_ffn_far = join(branch_passed, branch_kept, grad_ffn_far)
    branch_passed = hop(branch_passed, 2)
    grad_ffn_near = hop(jnp.stack([grad_ffn, grad_ffn_far]), 1)
    grad_ffn_rel = [grad_ffn, grad_ffn_near[0], grad_ffn_far, grad_ffn_near[1]]
    grad_ffn_all = jnp.concatenate(grad_ffn_rel, axis=0)
    branch_passed, gateup_weight, grad_ffn_all, *grad_ffn_rel = join(
        branch_passed, gateup_weight, grad_ffn_all, *grad_ffn_rel
    )
    branch = branch_kept + branch_passed.astype(f32)
    token_float = token_own.astype(f32)
    middle = token_float + gate_mix * branch

    unit_feed, inverse_feed = rms_parts(middle)
    normed_feed = (unit_feed * gain_feed * (1.0 + scale_feed) + shift_feed).astype(bf16)
    feed_far = hop(normed_feed, 2)
    feed_near = hop(normed_feed, 1)
    hidden_early, grads_early = feed_forward(
        [normed_feed, feed_near], grad_ffn_rel[:2], gateup_weight, down_weight, units_block
    )
    early = mm_nt(grads_early, gateup_weight).astype(bf16)
    feed_far, hidden_early, early = join(feed_far, hidden_early, early)
    feed_rel = [normed_feed, feed_near, feed_far, hop(feed_far, 1)]
    hidden_late, grads_late = feed_forward(
        feed_rel[2:], grad_ffn_rel[2:], gateup_weight, down_weight, units_block
    )
    late = mm_nt(grads_late, gateup_weight).astype(bf16)
    late_near = hop(late[rows:], 1)
    passed = (late[:rows].astype(f32) + late_near.astype(f32)).astype(bf16)
    passed, early, hidden_late, grads_late, cap_items = join(
        passed, early, hidden_late, grads_late, cap_items
    )

    passed = hop(passed, 2)
    early_near = hop(early[rows:], 1)
    for bit in reversed(range(1, top)):
        cap_items, cap_items_sent = cap_split(cap_items, bit)
        cap_items = jnp.concatenate([cap_items, dp_hop(cap_items_sent, bit)], axis=0)
    hidden = jnp.concatenate([hidden_early, hidden_late], axis=0)
    down_blocks = dp_blocks(mm_tn(hidden, grad_ffn_all).astype(bf16))
    down_cut = width // 3
    down_first = dp_hop(dp_sent(down_blocks, 0, down_cut), 0)
    feed_all = jnp.concatenate(feed_rel, axis=0)
    grad_units = jnp.concatenate([grads_early, grads_late], axis=0)
    gateup_blocks = dp_blocks(mm_tn(feed_all, grad_units).astype(bf16))
    down_sent = dp_sent(down_blocks, down_cut, width)
    passed, early_near, down_first, gateup_blocks, down_sent, cap_items = join(
        passed, early_near, down_first, gateup_blocks, down_sent, cap_items
    )
    down_second = dp_hop(down_sent, 0)
    grad_normfeed = early[:rows].astype(f32) + early_near.astype(f32) + passed.astype(f32)

    dshift_feed = jnp.sum(grad_normfeed, axis=0)
    dscale_feed = jnp.sum(grad_normfeed * (unit_feed * gain_feed), axis=0)
    grad_scaledfeed = grad_normfeed * (1.0 + scale_feed)
    gain_feed_grad = jnp.sum(grad_scaledfeed * unit_feed, axis=0)
    grad_middle = grad_out + rms_back(unit_feed, inverse_feed, grad_scaledfeed * gain_feed)
    dgate_mix = jnp.sum(grad_middle * branch, axis=0)

    grad_branch = (gate_mix * grad_middle).astype(bf16)
    grad_branch, gateup_blocks = join(grad_branch, gateup_blocks)
    grad_branch_far = hop(grad_branch, 2)
    ffn_part = mm(hidden, down_weight).astype(bf16)
    cuts = [2 * units * i // 16 for i in (0, 4, 7, 11, 16)]
    gateup_sent = dp_sent(gateup_blocks, cuts[0], cuts[1])
    cap_items, cap_items_sent = cap_split(cap_items, 0)
    grad_branch_far, down_second, ffn_part, gateup_sent, cap_items_sent = join(
        grad_branch_far, down_second, ffn_part, gateup_sent, cap_items_sent
    )
    gateup_first = dp_hop(gateup_sent, 0)
    cap_items = jnp.concatenate([cap_items, dp_hop(cap_items_sent, 0)], axis=0)
    grad_branch_two = jnp.stack([grad_branch, grad_branch_far])
    grad_branch_near = hop(grad_branch_two, 1)
    ffn_near = hop(jnp.stack([ffn_part[3 * rows :], ffn_part[rows : 2 * rows]]), 1)
    grad_branch_all = jnp.concatenate(
        [grad_branch, grad_branch_near[0], grad_branch_far, grad_branch_near[1]], axis=0
    )
    down_joined = [
        dp_joined(down_blocks, down_first, 0, down_cut),
        dp_joined(down_blocks, down_second, down_cut, width),
    ]
    down_kept = jnp.concatenate([kept for kept, _ in down_joined], axis=-1)
    down_line = dp_hop(jnp.concatenate([sent for _, sent in down_joined], axis=-1), 1)
    grad_attended = mm_nt(grad_branch_all, outproj_weight).astype(bf16)
    dquery_text, dcapkey, grad_capvalue, dtanh = text_backward(
        query_low, capkey_low, capvalue_low, grad_attended, lse, text_bias, tanh_lane, seq
    )
    outproj_part = mm_tn(attended, grad_branch_all).astype(bf16)
    outproj_blocks = (
        outproj_part.reshape(data_count, -1, count, part)
        .transpose(0, 2, 1, 3)
        .reshape(data_count, width // data_count, part)
    )
    gateup_sent = dp_sent(gateup_blocks, cuts[1], cuts[2])
    (
        dquery_text, dcapkey, grad_capvalue, dtanh, gateup_first, down_line, ffn_near, cap_items,
        outproj_blocks, gateup_sent,
    ) = join(
        dquery_text, dcapkey, grad_capvalue, dtanh, gateup_first, down_line, ffn_near, cap_items,
        outproj_blocks, gateup_sent,
    )
    gateup_more = dp_hop(gateup_sent, 0)
    cap_items_far = hop(cap_items, 2)
    capkey_unit = capkey_raw * capkey_inverse
    capkey_scaled = dcapkey * own_gains[3:4]
    (cap_dot,) = sum_rows_rel([], count, [jnp.sum(capkey_scaled * capkey_unit, axis=-1)])
    grad_capkey = (
        capkey_inverse * (capkey_scaled - capkey_unit * (cap_dot[:, None] / width))
    ).astype(bf16)
    gain_capkey_grad = jnp.sum(dcapkey * capkey_unit, axis=0)
    grad_cap = jnp.concatenate([grad_capkey, grad_capvalue], axis=1)
    ffn_passed = (
        ffn_part[2 * rows : 3 * rows].astype(f32) + ffn_near[0].astype(f32)
    ).astype(bf16)
    gateup_sent = jnp.concatenate(
        [dp_sent(gateup_blocks, cuts[2], cuts[3]), dp_sent(outproj_blocks, 0, part)], axis=-1
    )
    dquery_text, grad_cap, ffn_passed, gateup_sent, gateup_more, cap_items_far = join(
        dquery_text, grad_cap, ffn_passed, gateup_sent, gateup_more, cap_items_far
    )

    ffn_passed = hop(ffn_passed, 2)
    gateup_second = dp_hop(gateup_sent, 0)
    down_state = dp_next((down_kept, down_line), 2) if top >= 2 else (down_kept, down_line)
    gateup_joined = [
        dp_joined(gateup_blocks, gateup_first, cuts[0], cuts[1]),
        dp_joined(gateup_blocks, gateup_more, cuts[1], cuts[2]),
    ]
    gateup_kept = jnp.concatenate([kept for kept, _ in gateup_joined], axis=-1)
    gateup_line = dp_hop(jnp.concatenate([sent for _, sent in gateup_joined], axis=-1), 1)
    cap_grads = jnp.stack([grad_cap, dp_hop(grad_cap, top)])
    query_unrot, key_unrot, grad_value = self_backward(
        query_low, key_low, value_low, grad_attended, lse, dquery_text, tables, live_bias, block_rows
    )
    gateup_sent = dp_sent(gateup_blocks, cuts[3], cuts[4])
    (
        query_unrot, key_unrot, grad_value, ffn_passed, gateup_second, down_arrived, gateup_line,
        cap_grads, gateup_sent,
    ) = join(
        query_unrot, key_unrot, grad_value, ffn_passed, gateup_second, down_state[1], gateup_line,
        cap_grads, gateup_sent,
    )
    down_state = (down_state[0], down_arrived)
    cap_items_two = jnp.stack([cap_items, cap_items_far], axis=1)

    gateup_third = dp_hop(gateup_sent, 0)
    second_width = cuts[3] - cuts[2]
    second_joined = [
        dp_joined(gateup_blocks, gateup_second[..., :second_width], cuts[2], cuts[3]),
        dp_joined(outproj_blocks, gateup_second[..., second_width:], 0, part),
    ]
    second_kept = jnp.concatenate([kept for kept, _ in second_joined], axis=-1)
    second_line = dp_hop(jnp.concatenate([sent for _, sent in second_joined], axis=-1), 1)
    down_sum = dp_total(down_state) if top <= 2 else dp_rest_from(down_state, 3)
    owned_down = to_owner(down_sum)
    first_state = dp_next((gateup_kept, gateup_line), 2) if top >= 2 else (gateup_kept, gateup_line)
    query_inverse, key_inverse = query_inverse[0][:, None], key_inverse[0][:, None]
    query_unit = qkv[:, :part] * query_inverse
    key_unit = qkv[:, part : 2 * part] * key_inverse
    query_scaled = query_unrot * own_gains[1:2]
    key_scaled = key_unrot * own_gains[2:3]
    query_dot, key_dot = sum_rows_rel(
        [
            jnp.sum(query_scaled * query_unit, axis=-1),
            jnp.sum(key_scaled * key_unit, axis=-1),
        ],
        count,
    )
    gain_query_grad = jnp.sum(query_unrot * query_unit, axis=0)
    gain_key_grad = jnp.sum(key_unrot * key_unit, axis=0)
    grad_qkv = jnp.concatenate(
        [
            (query_inverse * (query_scaled - query_unit * (query_dot[:, None] / width))).astype(bf16),
            (key_inverse * (key_scaled - key_unit * (key_dot[:, None] / width))).astype(bf16),
            grad_value,
        ],
        axis=1,
    )
    qkv_blocks = dp_blocks(mm_tn(normed_all, grad_qkv).astype(bf16))
    qkv_sent = dp_sent(qkv_blocks, 0, 3 * part)
    qkv_sent, gateup_third, first_arrived, second_line, owned_down = join(
        qkv_sent, gateup_third, first_state[1], second_line, owned_down
    )
    first_state = (first_state[0], first_arrived)

    qkv_beside = dp_hop(qkv_sent, 0)
    third_kept, third_line = dp_joined(gateup_blocks, gateup_third, cuts[3], cuts[4])
    third_line = dp_hop(third_line, 1)
    second_state = dp_next((second_kept, second_line), 2) if top >= 2 else (second_kept, second_line)
    for bit in reversed(range(1, top)):
        cap_grads = jnp.concatenate([cap_grads, dp_hop(cap_grads, bit)], axis=0)
    normmix_part = project_back(own, grad_qkv, qkv_rel)
    normmix_near = hop(jnp.stack([normmix_part[3 * rows :], normmix_part[rows : 2 * rows]]), 1)
    normmix_passed = hop(
        (normmix_part[2 * rows : 3 * rows].astype(f32) + normmix_near[0].astype(f32)).astype(bf16), 2
    )
    qkv_beside, third_line, normmix_passed, cap_grads, second_arrived, cap_items_two = join(
        qkv_beside, third_line, normmix_passed, cap_grads, second_state[1], cap_items_two
    )
    second_state = (second_state[0], second_arrived)
    cap_items_near = hop(cap_items_two, 1)
    cap_items_all = jnp.stack(
        natural_order(
            [cap_items_two[:, 0], cap_items_near[:, 0], cap_items_two[:, 1], cap_items_near[:, 1]], own
        ),
        axis=1,
    ).reshape(data_count * text, -1)

    qkv_kept, qkv_line = dp_joined(qkv_blocks, qkv_beside, 0, 3 * part)
    qkv_line = dp_hop(qkv_line, 1)
    third_state = dp_next((third_kept, third_line), 2) if top >= 2 else (third_kept, third_line)
    cap_grads = jnp.concatenate([cap_grads, dp_hop(cap_grads, 0)], axis=0)
    grad_normmix = (
        normmix_part[:rows].astype(f32) + normmix_near[1].astype(f32) + normmix_passed.astype(f32)
    )
    ffn_out = ffn_part[:rows].astype(f32) + ffn_near[1].astype(f32) + ffn_passed.astype(f32)
    block_out = (middle + gate_feed * ffn_out).astype(bf16)
    dgate_feed = jnp.sum(grad_out * ffn_out, axis=0)
    unit_mix, inverse_mix = rms_parts(token_float)
    dshift_mix = jnp.sum(grad_normmix, axis=0)
    dscale_mix = jnp.sum(grad_normmix * (unit_mix * gain_mix), axis=0)
    grad_scaledmix = grad_normmix * (1.0 + scale_mix)
    gain_mix_grad = jnp.sum(grad_scaledmix * unit_mix, axis=0)
    tokens_grad = (
        grad_middle + rms_back(unit_mix, inverse_mix, grad_scaledmix * gain_mix)
    ).astype(bf16)

    own_rows = jnp.zeros((3, width), f32)
    own_rows = lax.dynamic_update_slice(
        own_rows, jnp.stack([gain_query_grad, gain_key_grad, gain_capkey_grad]), (0, own * part)
    )
    gate_sums = lax.dynamic_update_slice(
        jnp.zeros((head_count,), f32), dtanh[0, ::head_size], (own * own_heads,)
    )
    sums = jnp.concatenate([gain_mix_grad, own_rows.reshape(-1), gain_feed_grad, gate_sums])
    grad_modulation = jnp.concatenate(
        [dshift_mix, dscale_mix, dgate_mix, dshift_feed, dscale_feed, dgate_feed]
    )
    message = jnp.concatenate([grad_modulation, sums])
    message = message + hop(message, 1)
    message = message + hop(message, 2)
    mod_width = 6 * width
    item_rows = jnp.concatenate([message[:mod_width], silu_low[0].astype(f32)]).astype(bf16)[None]
    totals = message[mod_width:]

    def wider(item_rows, totals, bit):
        high = totals.astype(bf16)
        low = (totals - high.astype(f32)).astype(bf16)
        arrived = dp_hop(jnp.concatenate([item_rows.reshape(-1), high, low]), bit)
        rest = arrived[item_rows.size :].astype(f32)
        return (
            jnp.concatenate([item_rows, arrived[: item_rows.size].reshape(item_rows.shape)], axis=0),
            totals + (rest[: totals.size] + rest[totals.size :]),
        )

    first_sum = dp_total(first_state) if top <= 2 else dp_rest_from(first_state, 3)
    second_sum = dp_total(second_state) if top <= 2 else dp_rest_from(second_state, 3)
    outproj_sum = (
        second_sum[:, second_width:].reshape(count, -1, part).transpose(1, 0, 2).reshape(-1, width)
    )
    owned_outproj = to_owner(outproj_sum)
    second_sum = second_sum[:, :second_width]
    qkv_line, item_rows, totals, third_arrived, first_sum, second_sum, owned_outproj = join(
        qkv_line, item_rows, totals, third_state[1], first_sum, second_sum, owned_outproj
    )

    qkv_state = dp_next((qkv_kept, qkv_line), 2) if top >= 2 else (qkv_kept, qkv_line)
    third_state = (third_state[0], third_arrived)
    third_sum = dp_total(third_state) if top <= 2 else dp_rest_from(third_state, 3)
    gateup_pieces, gateup_sent = spread_pieces([first_sum, second_sum, third_sum], own)
    gateup_far = hop(gateup_sent, 2)
    item_rows, totals = wider(item_rows, totals, 0)
    cap_sum = mm_tn(cap_items_all, cap_grads.reshape(-1, cap_grads.shape[-1]))
    cap_pieces, cap_sent_far = spread_pieces([cap_sum], own)
    qkv_arrived, gateup_far, item_rows, totals, cap_sent_far = join(
        qkv_state[1], gateup_far, item_rows, totals, cap_sent_far
    )
    qkv_state = (qkv_state[0], qkv_arrived)

    qkv_sum = dp_total(qkv_state) if top <= 2 else dp_rest_from(qkv_state, 3)
    qkv_pieces, qkv_sent_far = spread_pieces([qkv_sum], own)
    qkv_far = hop(qkv_sent_far, 2)
    cap_far_rows = hop(cap_sent_far, 2)
    gateup_near = spread_near(gateup_pieces, gateup_far)
    item_rows, totals = wider(item_rows, totals, 1)
    qkv_far, cap_far_rows, gateup_near, item_rows, totals = join(
        qkv_far, cap_far_rows, gateup_near, item_rows, totals
    )
    qkv_near = spread_near(qkv_pieces, qkv_far)
    cap_near_rows = spread_near(cap_pieces, cap_far_rows)
    for bit in range(2, top + 1):
        item_rows, totals = wider(item_rows, totals, bit)
    gate_grad, up_grad = spread_result(gateup_pieces, gateup_far, gateup_near, [units] * 2, own)
    query_grad, key_grad, value_grad = spread_result(qkv_pieces, qkv_far, qkv_near, [part] * 3, own)
    capkey_grad, capvalue_grad = spread_result(cap_pieces, cap_far_rows, cap_near_rows, [part] * 2, own)
    modulation_rows = item_rows[:, :mod_width].astype(f32)
    silu_rows = item_rows[:, mod_width:].astype(f32)
    owner = place * count + own
    devices = count * data_count
    cd_rows = silu_rows.shape[1] // devices
    adaln_wgrad = lax.dot_general(
        lax.dynamic_slice_in_dim(silu_rows, owner * cd_rows, cd_rows, 1),
        modulation_rows,
        (((0,), (0,)), ((), ())),
        precision=lax.Precision.HIGHEST,
        preferred_element_type=f32,
    )
    bias_rows = mod_width // devices
    adaln_bgrad = lax.dynamic_slice_in_dim(
        jnp.sum(modulation_rows, axis=0), owner * bias_rows, bias_rows, 0
    )
    gains_grad = lax.dynamic_slice_in_dim(
        totals[: 5 * width].reshape(5, width), owner * (width // devices), width // devices, 1
    )
    headgate_grad = totals[5 * width :] * (1.0 - tanh_gate * tanh_gate)

    down_grad, outproj_grad = owned_down, owned_outproj
    return (
        block_out[None],
        tokens_grad[None],
        adaln_wgrad,
        adaln_bgrad,
        query_grad,
        key_grad,
        value_grad,
        outproj_grad,
        capkey_grad,
        capvalue_grad,
        gains_grad,
        headgate_grad,
        gate_grad,
        up_grad,
        down_grad,
    )


def solution(mesh):
    return jax.shard_map(
        on_device,
        mesh=mesh,
        in_specs=(
            P("dp", "fsdp", None),
            P("dp", "fsdp", None),
            P("dp", None),
            P("dp"),
            P("dp"),
            P("dp", None, "fsdp"),
            P(),
            P("fsdp", None),
            P("fsdp"),
            P("fsdp", None),
            P("fsdp", None),
            P("fsdp", None),
            P("fsdp", None),
            P("fsdp", None),
            P("fsdp", None),
            P(None, "fsdp"),
            P(),
            P("fsdp", None),
            P("fsdp", None),
            P("fsdp", None),
            P("dp", "fsdp", None),
        ),
        out_specs=(
            P("dp", "fsdp", None),
            P("dp", "fsdp", None),
            P(("dp", "fsdp"), None),
            P(("dp", "fsdp")),
            P(("dp", "fsdp"), None),
            P(("dp", "fsdp"), None),
            P(("dp", "fsdp"), None),
            P(("dp", "fsdp"), None),
            P(("dp", "fsdp"), None),
            P(("dp", "fsdp"), None),
            P(None, ("dp", "fsdp")),
            P(),
            P(("dp", "fsdp"), None),
            P(("dp", "fsdp"), None),
            P(("dp", "fsdp"), None),
        ),
        check_vma=False,
    )
```

```python
import jax
import jax.numpy as jnp
from jax import lax
from jax.experimental import pallas as pl
from jax.experimental.pallas import tpu as pltpu
from jax.sharding import PartitionSpec as P

norm_eps = 1e-06
rope_base = 10000.0
masked_score = -1e30
f32 = jnp.float32
bf16 = jnp.bfloat16


def mm(left_side, right_side):
    return lax.dot_general(
        left_side, right_side, (((1,), (0,)), ((), ())), preferred_element_type=f32
    )


def mm_nt(left_side, right_side):
    return lax.dot_general(
        left_side, right_side, (((1,), (1,)), ((), ())), preferred_element_type=f32
    )


def mm_tn(left_side, right_side):
    return lax.dot_general(
        left_side, right_side, (((0,), (0,)), ((), ())), preferred_element_type=f32
    )


def rms_parts(values):
    inverse = lax.rsqrt(jnp.mean(values * values, axis=-1, keepdims=True) + norm_eps)
    return (values * inverse, inverse)


def rms_back(unit_rows, inverse, grad_unit):
    return inverse * (
        grad_unit - unit_rows * jnp.mean(grad_unit * unit_rows, axis=-1, keepdims=True)
    )


def hop(values, mask):
    count = lax.axis_size("fsdp")
    return lax.ppermute(values, "fsdp", [(i, i ^ mask) for i in range(count)])


def gather_rel(values):
    two = jnp.stack([values, hop(values, 2)])
    other = hop(two, 1)
    return [values, other[0], two[1], other[1]]


def scatter_rel(blocks):
    arrived = hop(jnp.stack([blocks[3], blocks[1]]), 1)
    passed = hop((blocks[2].astype(f32) + arrived[0].astype(f32)).astype(bf16), 2)
    return blocks[0].astype(f32) + arrived[1].astype(f32) + passed.astype(f32)


def trade_rel(blocks, middle=None):
    far = hop(jnp.stack([blocks[2], blocks[3]]), 2)
    if middle is not None:
        far = middle(far)
    beside = hop(jnp.stack([blocks[1], far[1]]), 1)
    return [blocks[0], beside[0], far[0], beside[1]]


def swap_blocks(values, mask, count):
    rows = values.shape[0] // count
    return jnp.concatenate(
        [values[(m ^ mask) * rows : ((m ^ mask) + 1) * rows] for m in range(count)], axis=0
    )


def sum_rows_rel(columns, count, plain=()):
    swapped = len(columns)
    columns = list(columns) + list(plain)
    ends = [0]
    for column in columns:
        ends.append(ends[-1] + column.shape[0])
    total = jnp.concatenate(columns)
    for mask in (1, 2):
        arrived = hop(total, mask)
        total = total + jnp.concatenate(
            [swap_blocks(arrived[i:j], mask, count) for i, j in zip(ends, ends[1 : swapped + 1])]
            + [arrived[ends[swapped] :]]
        )
    return [total[i:j] for i, j in zip(ends, ends[1:])]


def natural_order(pieces, own):
    far, near = own // 2, own % 2
    mixed = [[jnp.where(near == 0, pieces[2 * i + j], pieces[2 * i + 1 - j]) for j in range(2)] for i in range(2)]
    return [jnp.where(far == 0, mixed[i][j], mixed[1 - i][j]) for i in range(2) for j in range(2)]


def join(*values):
    return lax.optimization_barrier(values)


def dp_bits():
    return lax.axis_size("dp").bit_length() - 1


def dp_hop(values, bit):
    count = lax.axis_size("dp")
    return lax.ppermute(values, "dp", [(i, i ^ (1 << bit)) for i in range(count)])


def dp_place(bit):
    return (lax.axis_index("dp") >> bit) & 1


def pick(values, axis, index):
    return lax.dynamic_index_in_dim(values, index, axis, keepdims=False)


def dp_blocks(partial):
    return partial.reshape(lax.axis_size("dp"), -1, partial.shape[1])


def dp_half(blocks, bit, other):
    pairs = blocks.reshape((-1, 2) + blocks.shape[1:])
    return pick(pairs, 1, 1 - dp_place(bit) if other else dp_place(bit))


def dp_sent(blocks, start, stop):
    return dp_half(blocks[..., start:stop], 0, True)


def dp_joined(blocks, arrived, start, stop):
    return dp_sums((dp_half(blocks[..., start:stop], 0, False), arrived), 1)


def dp_sums(state, bit):
    kept, arrived = state

    def half(other):
        return (
            dp_half(kept, bit, other).astype(f32) + dp_half(arrived, bit, other).astype(f32)
        ).astype(bf16)

    return (half(False), half(True))


def dp_next(state, bit):
    kept, sent = dp_sums(state, bit)
    return (kept, dp_hop(sent, bit))


def dp_total(state):
    return state[0][0].astype(f32) + state[1][0].astype(f32)


def dp_rest_from(state, start):
    for bit in range(start, dp_bits()):
        state = dp_next(state, bit)
    return dp_total(state)


def dp_rest(state):
    return dp_rest_from(state, 1)


def cap_order(values, top):
    return values.reshape(-1, values.shape[-1])


def spread_pieces(totals, own):
    count = lax.axis_size("fsdp")
    low = jnp.concatenate([total.astype(bf16) for total in totals], axis=1)
    rows = low.shape[0] // count
    pieces = [lax.dynamic_slice_in_dim(low, (own ^ m) * rows, rows, 0) for m in range(count)]
    return (jnp.stack(pieces[:2]), jnp.stack(pieces[2:]))


def spread_near(pieces, far):
    return hop(jnp.stack([pieces[1], far[1]]), 1)


def spread_result(pieces, far, near, widths, own):
    results, start = [], 0
    for width in widths:
        part = [
            piece[:, start : start + width] for piece in (pieces[0], near[0], far[0], near[1])
        ]
        results.append(jnp.concatenate(natural_order(part, own), axis=1).astype(f32))
        start += width
    return results


def to_owner(total):
    data_count, count = lax.axis_size("dp"), lax.axis_size("fsdp")
    pairs = [(d * count + f, f * data_count + d) for d in range(data_count) for f in range(count)]
    return lax.ppermute(total.astype(bf16), ("dp", "fsdp"), pairs).astype(f32)


def lane_of(shape):
    return lax.broadcasted_iota(jnp.int32, shape, len(shape) - 1)


def rotate_lanes(values, cosines, sines):
    lanes = lane_of(values.shape)
    even = lax.rem(lax.div(lanes, 16), 2) == 0
    width = values.shape[-1]
    partner = jnp.where(even, pltpu.roll(values, width - 16, 1), pltpu.roll(values, 16, 1))
    return values * cosines + partner * sines


def as_column(row):
    return jnp.transpose(jnp.broadcast_to(row, (8, row.shape[1])))[:, :1]


def head_lanes(values, head, spare):
    lanes = lane_of(values.shape)
    mine = (lanes < 64) if head == 0 else (lanes >= 64)
    mark = 64 if head == 0 else 0
    return jnp.where(mine, values, jnp.where(lanes == mark, spare, jnp.zeros_like(values)))


def attend_body(
    q_ref, k_ref, v_ref, qinv_ref, kinv_ref, qg_ref, kg_ref, cosq_ref, sinq_ref, cosk_ref, sink_ref,
    ck_ref, cv_ref, live_ref, text_ref, tanh_ref,
    out_ref, qlow_ref, klow_ref, vlow_ref, lse_ref,
    km, vm, cm, cvm,
):
    @pl.when(pl.program_id(1) == 0)
    def _():
        key = rotate_lanes(
            k_ref[...] * as_column(kinv_ref[...]) * kg_ref[...], cosk_ref[...], sink_ref[...]
        ).astype(bf16)
        value = v_ref[...].astype(bf16)
        klow_ref[...] = key
        vlow_ref[...] = value
        one = jnp.ones((), bf16)
        for head in range(2):
            km[head] = head_lanes(key, head, live_ref[...].astype(bf16))
            vm[head] = head_lanes(value, head, one)
            cm[head] = head_lanes(ck_ref[...], head, text_ref[...].astype(bf16))
            cvm[head] = head_lanes(cv_ref[...], head, one)

    query = rotate_lanes(
        q_ref[...] * as_column(qinv_ref[...]) * qg_ref[...], cosq_ref[...], sinq_ref[...]
    ).astype(bf16)
    qlow_ref[...] = query
    scaled = query * jnp.asarray(0.125, bf16)
    lanes = lane_of(out_ref.shape)
    results, stats = [], []
    for head in range(2):
        part = head_lanes(scaled, head, jnp.ones((), bf16))
        mark = 64 if head == 0 else 0

        def one_side(keys, values):
            scores = mm_nt(part, keys)
            peak = jnp.max(scores, axis=-1, keepdims=True)
            weights = jnp.exp(scores - peak).astype(bf16)
            mixed = mm(weights, values)
            amount = mixed[:, mark : mark + 1]
            stats.append(peak + jnp.log(amount))
            return mixed / amount

        own = one_side(km[head], vm[head])
        text = one_side(cm[head], cvm[head])
        results.append(own + tanh_ref[...] * text)
    out_ref[...] = jnp.where(lanes < 64, results[0], results[1]).astype(bf16)
    table = jnp.where(lanes == 0, stats[0], stats[1])
    table = jnp.where(lanes == 2, stats[2], table)
    lse_ref[...] = jnp.where(lanes == 3, stats[3], table)


def attend_forward(qkv, inverses, gains, tables, capkey, capvalue, live_bias, text_bias, tanh_lane, rows):
    seq, width = qkv.shape[0], qkv.shape[1] // 3
    pairs, text = width // 128, capkey.shape[0]
    full = lambda p, i: (0, p)
    block = lambda p, i: (i, p)
    qrow = lambda p, i: (i, 0)
    whole = lambda p, i: (0, 0)
    return pl.pallas_call(
        attend_body,
        grid=(pairs, seq // rows),
        in_specs=[
            pl.BlockSpec((rows, 128), block),
            pl.BlockSpec((seq, 128), lambda p, i: (0, p + pairs)),
            pl.BlockSpec((seq, 128), lambda p, i: (0, p + 2 * pairs)),
            pl.BlockSpec((1, rows), lambda p, i: (0, i)),
            pl.BlockSpec((1, seq), whole),
            pl.BlockSpec((1, 128), full),
            pl.BlockSpec((1, 128), full),
            pl.BlockSpec((rows, 128), qrow),
            pl.BlockSpec((rows, 128), qrow),
            pl.BlockSpec((seq, 128), whole),
            pl.BlockSpec((seq, 128), whole),
            pl.BlockSpec((text, 128), full),
            pl.BlockSpec((text, 128), full),
            pl.BlockSpec((seq, 1), whole),
            pl.BlockSpec((text, 1), whole),
            pl.BlockSpec((1, 128), full),
        ],
        out_specs=[
            pl.BlockSpec((rows, 128), block),
            pl.BlockSpec((rows, 128), block),
            pl.BlockSpec((seq, 128), full),
            pl.BlockSpec((seq, 128), full),
            pl.BlockSpec((rows, 128), block),
        ],
        out_shape=[
            jax.ShapeDtypeStruct((seq, width), bf16),
            jax.ShapeDtypeStruct((seq, width), bf16),
            jax.ShapeDtypeStruct((seq, width), bf16),
            jax.ShapeDtypeStruct((seq, width), bf16),
            jax.ShapeDtypeStruct((seq, width), f32),
        ],
        scratch_shapes=[
            pltpu.VMEM((2, seq, 128), bf16),
            pltpu.VMEM((2, seq, 128), bf16),
            pltpu.VMEM((2, text, 128), bf16),
            pltpu.VMEM((2, text, 128), bf16),
        ],
        compiler_params=pltpu.CompilerParams(
            dimension_semantics=("arbitrary", "arbitrary"), vmem_limit_bytes=20 << 20
        ),
        cost_estimate=pl.CostEstimate(
            flops=seq * width,
            transcendentals=0,
            bytes_accessed=seq * width,
        ),
        name="attend_forward",
    )(
        qkv, qkv, qkv, inverses[0], inverses[1], gains[0], gains[1], tables[0], tables[1],
        tables[0], tables[1], capkey, capvalue, live_bias, text_bias, tanh_lane,
    )


def text_back_body(
    q_ref, ck_ref, cv_ref, do_ref, lse_ref, text_ref, tanh_ref,
    dq_ref, dck_ref, dcv_ref, dtanh_ref,
    cm, dck, dcv,
):
    step = pl.program_id(1)

    @pl.when(step == 0)
    def _():
        for head in range(2):
            cm[head] = head_lanes(ck_ref[...], head, text_ref[...].astype(bf16))
        dck[...] = jnp.zeros_like(dck)
        dcv[...] = jnp.zeros_like(dcv)
        dtanh_ref[...] = jnp.zeros_like(dtanh_ref)

    scaled = q_ref[...] * jnp.asarray(0.125, bf16)
    grad = do_ref[...]
    lse = lse_ref[...]
    grads = []
    for head in range(2):
        part = head_lanes(scaled, head, jnp.ones((), bf16))
        grad_part = head_lanes(grad, head, jnp.zeros((), bf16))
        gate = tanh_ref[:, 64 * head : 64 * head + 1]
        probs = jnp.exp(mm_nt(part, cm[head]) - lse[:, 2 * head + 1 : 2 * head + 2])
        dprob = mm_nt(grad_part, cv_ref[...])
        total = jnp.sum(probs * dprob, axis=-1, keepdims=True)
        dscore = (probs * ((dprob - total) * gate)).astype(bf16)
        grads.append(mm(dscore, ck_ref[...]))

        def add(target, update):
            lanes = lane_of(target.shape)
            mine = (lanes < 64) if head == 0 else (lanes >= 64)
            target[...] += jnp.where(mine, update, jnp.zeros_like(update))

        add(dck, mm_tn(dscore, scaled))
        add(dcv, mm_tn(probs.astype(bf16), grad))
        add(dtanh_ref, jnp.broadcast_to(jnp.sum(total, axis=0, keepdims=True), dtanh_ref.shape))
    lanes = lane_of(dq_ref.shape)
    dq_ref[...] = jnp.where(lanes < 64, grads[0], grads[1])

    @pl.when(step == pl.num_programs(1) - 1)
    def _():
        dck_ref[...] = dck[...]
        dcv_ref[...] = (dcv[...] * tanh_ref[...]).astype(bf16)


def text_backward(query, capkey, capvalue, grad, lse, text_bias, tanh_lane, rows):
    seq, width = query.shape
    pairs, text = width // 128, capkey.shape[0]
    full = lambda p, i: (0, p)
    block = lambda p, i: (i, p)
    whole = lambda p, i: (0, 0)
    return pl.pallas_call(
        text_back_body,
        grid=(pairs, seq // rows),
        in_specs=[
            pl.BlockSpec((rows, 128), block),
            pl.BlockSpec((text, 128), full),
            pl.BlockSpec((text, 128), full),
            pl.BlockSpec((rows, 128), block),
            pl.BlockSpec((rows, 128), block),
            pl.BlockSpec((text, 1), whole),
            pl.BlockSpec((1, 128), full),
        ],
        out_specs=[
            pl.BlockSpec((rows, 128), block),
            pl.BlockSpec((text, 128), full),
            pl.BlockSpec((text, 128), full),
            pl.BlockSpec((8, 128), full),
        ],
        out_shape=[
            jax.ShapeDtypeStruct((seq, width), f32),
            jax.ShapeDtypeStruct((text, width), f32),
            jax.ShapeDtypeStruct((text, width), bf16),
            jax.ShapeDtypeStruct((8, width), f32),
        ],
        scratch_shapes=[
            pltpu.VMEM((2, text, 128), bf16),
            pltpu.VMEM((text, 128), f32),
            pltpu.VMEM((text, 128), f32),
        ],
        compiler_params=pltpu.CompilerParams(
            dimension_semantics=("arbitrary", "arbitrary"), vmem_limit_bytes=20 << 20
        ),
        cost_estimate=pl.CostEstimate(
            flops=40 * seq * text * width,
            transcendentals=seq * text * width // 64,
            bytes_accessed=seq * width * 16,
        ),
        name="text_backward",
    )(query, capkey, capvalue, grad, lse, text_bias, tanh_lane)


def self_back_body(
    q_ref, k_ref, v_ref, do_ref, lse_ref, dqt_ref, cosq_ref, sinq_ref, cosk_ref, sink_ref, live_ref,
    dq_ref, dk_ref, dv_ref,
    km, dk, dv,
):
    step = pl.program_id(1)

    @pl.when(step == 0)
    def _():
        for head in range(2):
            km[head] = head_lanes(k_ref[...], head, live_ref[...].astype(bf16))
        dk[...] = jnp.zeros_like(dk)
        dv[...] = jnp.zeros_like(dv)

    scaled = q_ref[...] * jnp.asarray(0.125, bf16)
    grad = do_ref[...]
    lse = lse_ref[...]
    grads = []
    for head in range(2):
        part = head_lanes(scaled, head, jnp.ones((), bf16))
        grad_part = head_lanes(grad, head, jnp.zeros((), bf16))
        probs = jnp.exp(mm_nt(part, km[head]) - lse[:, 2 * head : 2 * head + 1])
        dprob = mm_nt(grad_part, v_ref[...])
        total = jnp.sum(probs * dprob, axis=-1, keepdims=True)
        dscore = (probs * (dprob - total)).astype(bf16)
        grads.append(mm(dscore, k_ref[...]))

        def add(target, update):
            lanes = lane_of(target.shape)
            mine = (lanes < 64) if head == 0 else (lanes >= 64)
            target[...] += jnp.where(mine, update, jnp.zeros_like(update))

        add(dk, mm_tn(dscore, scaled))
        add(dv, mm_tn(probs.astype(bf16), grad))
    lanes = lane_of(dq_ref.shape)
    dq_ref[...] = rotate_lanes(
        (jnp.where(lanes < 64, grads[0], grads[1]) + dqt_ref[...]) * 0.125,
        cosq_ref[...],
        -sinq_ref[...],
    )

    @pl.when(step == pl.num_programs(1) - 1)
    def _():
        dk_ref[...] = rotate_lanes(dk[...], cosk_ref[...], -sink_ref[...])
        dv_ref[...] = dv[...].astype(bf16)


def self_backward(query, key, value, grad, lse, dquery_text, tables, live_bias, rows):
    seq, width = query.shape
    pairs = width // 128
    full = lambda p, i: (0, p)
    block = lambda p, i: (i, p)
    qrow = lambda p, i: (i, 0)
    whole = lambda p, i: (0, 0)
    return pl.pallas_call(
        self_back_body,
        grid=(pairs, seq // rows),
        in_specs=[
            pl.BlockSpec((rows, 128), block),
            pl.BlockSpec((seq, 128), full),
            pl.BlockSpec((seq, 128), full),
            pl.BlockSpec((rows, 128), block),
            pl.BlockSpec((rows, 128), block),
            pl.BlockSpec((rows, 128), block),
            pl.BlockSpec((rows, 128), qrow),
            pl.BlockSpec((rows, 128), qrow),
            pl.BlockSpec((seq, 128), whole),
            pl.BlockSpec((seq, 128), whole),
            pl.BlockSpec((seq, 1), whole),
        ],
        out_specs=[
            pl.BlockSpec((rows, 128), block),
            pl.BlockSpec((seq, 128), full),
            pl.BlockSpec((seq, 128), full),
        ],
        out_shape=[
            jax.ShapeDtypeStruct((seq, width), f32),
            jax.ShapeDtypeStruct((seq, width), f32),
            jax.ShapeDtypeStruct((seq, width), bf16),
        ],
        scratch_shapes=[
            pltpu.VMEM((2, seq, 128), bf16),
            pltpu.VMEM((seq, 128), f32),
            pltpu.VMEM((seq, 128), f32),
        ],
        compiler_params=pltpu.CompilerParams(
            dimension_semantics=("arbitrary", "arbitrary"), vmem_limit_bytes=20 << 20
        ),
        cost_estimate=pl.CostEstimate(
            flops=40 * seq * seq * width,
            transcendentals=seq * seq * width // 64,
            bytes_accessed=seq * width * 28,
        ),
        name="self_backward",
    )(query, key, value, grad, lse, dquery_text, tables[0], tables[1], tables[0], tables[1], live_bias)


def feed_body(x0_ref, x1_ref, g0_ref, g1_ref, gate_ref, up_ref, down_ref, hidden_ref, grads_ref):
    step = pl.program_id(0)
    block = down_ref.shape[0]
    units = grads_ref.shape[1] // 2
    rows_in = jnp.concatenate([x0_ref[...], x1_ref[...]], axis=0)
    grads_in = jnp.concatenate([g0_ref[...], g1_ref[...]], axis=0)
    gate = mm(rows_in, gate_ref[...])
    up = mm(rows_in, up_ref[...])
    grad_hidden = mm_nt(grads_in, down_ref[...])
    sigmoid = 1.0 / (1.0 + jnp.exp(-gate))
    silu = gate * sigmoid
    hidden_ref[...] = (silu * up).astype(bf16)
    start = pl.multiple_of(step * block, block)
    grads_ref[:, pl.ds(start, block)] = (
        grad_hidden * up * (sigmoid * (1.0 + gate * (1.0 - sigmoid)))
    ).astype(bf16)
    grads_ref[:, pl.ds(pl.multiple_of(units + start, block), block)] = (grad_hidden * silu).astype(bf16)


def feed_forward(rows_in, grads_in, gateup, down, units_block):
    rows, width = rows_in[0].shape
    units = down.shape[0]
    steps = units // units_block
    whole = pl.BlockSpec((rows, width), lambda j: (0, 0))
    return pl.pallas_call(
        feed_body,
        grid=(steps,),
        in_specs=[whole] * 4
        + [
            pl.BlockSpec((width, units_block), lambda j: (0, j)),
            pl.BlockSpec((width, units_block), lambda j: (0, j + steps)),
            pl.BlockSpec((units_block, width), lambda j: (j, 0)),
        ],
        out_specs=[
            pl.BlockSpec((2 * rows, units_block), lambda j: (0, j)),
            pl.BlockSpec((2 * rows, 2 * units), lambda j: (0, 0)),
        ],
        out_shape=[
            jax.ShapeDtypeStruct((2 * rows, units), bf16),
            jax.ShapeDtypeStruct((2 * rows, 2 * units), bf16),
        ],
        compiler_params=pltpu.CompilerParams(
            dimension_semantics=("arbitrary",), vmem_limit_bytes=32 << 20
        ),
        cost_estimate=pl.CostEstimate(
            flops=12 * rows * width * units,
            transcendentals=2 * rows * units,
            bytes_accessed=6 * width * units + 8 * rows * width + 12 * rows * units,
        ),
        name="feed_forward",
    )(*rows_in, *grads_in, gateup, gateup, down)


def project_body(
    own_ref, x_ref, gain_ref, scale_ref, shift_ref, w0_ref, w1_ref, w2_ref, w3_ref,
    normed_ref, out_ref, query_ref, key_ref,
):
    values = x_ref[...].astype(f32)
    inverse = lax.rsqrt(jnp.mean(values * values, axis=-1, keepdims=True) + norm_eps)
    normed_ref[...] = (
        values * inverse * gain_ref[...] * (1.0 + scale_ref[...]) + shift_ref[...]
    ).astype(bf16)
    depth = w0_ref.shape[0]
    total = None
    for m, w_ref in enumerate((w0_ref, w1_ref, w2_ref, w3_ref)):
        start = pl.multiple_of((own_ref[0] ^ m) * depth, depth)
        term = mm(normed_ref[:, pl.ds(start, depth)], w_ref[...])
        total = term if total is None else total + term
    out_ref[...] = total
    part = out_ref.shape[1] // 3
    ones = jnp.ones((8, part), f32)

    def squares(rows):
        return lax.dot_general(
            ones,
            rows * rows,
            (((1,), (1,)), ((), ())),
            precision=lax.Precision.HIGHEST,
            preferred_element_type=f32,
        )

    query_ref[...] = squares(total[:, :part])
    key_ref[...] = squares(total[:, part : 2 * part])


def project(own, tokens, gain, scale, shift, weights):
    seq, width = tokens.shape
    columns = weights[0].shape[1]
    rows = 512 if seq % 512 == 0 else seq
    row = lambda i, own: (0, 0)
    block = lambda i, own: (i, 0)
    flat = lambda i, own: (0, i)
    return pl.pallas_call(
        project_body,
        grid_spec=pltpu.PrefetchScalarGridSpec(
            num_scalar_prefetch=1,
            grid=(seq // rows,),
            in_specs=[pl.BlockSpec((rows, width), block)]
            + [pl.BlockSpec((1, width), row)] * 3
            + [pl.BlockSpec(weights[0].shape, row)] * 4,
            out_specs=[
                pl.BlockSpec((rows, width), block),
                pl.BlockSpec((rows, columns), block),
                pl.BlockSpec((8, rows), flat),
                pl.BlockSpec((8, rows), flat),
            ],
        ),
        out_shape=[
            jax.ShapeDtypeStruct((seq, width), bf16),
            jax.ShapeDtypeStruct((seq, columns), f32),
            jax.ShapeDtypeStruct((8, seq), f32),
            jax.ShapeDtypeStruct((8, seq), f32),
        ],
        compiler_params=pltpu.CompilerParams(
            dimension_semantics=("arbitrary",), vmem_limit_bytes=24 << 20
        ),
        cost_estimate=pl.CostEstimate(
            flops=seq * width, transcendentals=0, bytes_accessed=seq * width
        ),
        name="project",
    )(own[None], tokens, gain, scale, shift, *weights)


def project_back_body(own_ref, d_ref, w0_ref, w1_ref, w2_ref, w3_ref, out_ref):
    depth = w0_ref.shape[0]
    for m, w_ref in enumerate((w0_ref, w1_ref, w2_ref, w3_ref)):
        start = pl.multiple_of((own_ref[0] ^ m) * depth, depth)
        out_ref[:, pl.ds(start, depth)] = mm_nt(d_ref[...], w_ref[...]).astype(bf16)


def project_back(own, grads, weights):
    seq, columns = grads.shape
    width = weights[0].shape[0] * 4
    rows = 512 if seq % 512 == 0 else seq
    block = lambda i, own: (i, 0)
    return pl.pallas_call(
        project_back_body,
        grid_spec=pltpu.PrefetchScalarGridSpec(
            num_scalar_prefetch=1,
            grid=(seq // rows,),
            in_specs=[pl.BlockSpec((rows, columns), block)]
            + [pl.BlockSpec(weights[0].shape, lambda i, own: (0, 0))] * 4,
            out_specs=pl.BlockSpec((rows, width), block),
        ),
        out_shape=jax.ShapeDtypeStruct((seq, width), bf16),
        compiler_params=pltpu.CompilerParams(
            dimension_semantics=("arbitrary",), vmem_limit_bytes=24 << 20
        ),
        cost_estimate=pl.CostEstimate(
            flops=seq * width, transcendentals=0, bytes_accessed=seq * width
        ),
        name="project_back",
    )(own[None], grads, *weights)


def on_device(
    tokens,
    caption,
    caption_mask,
    item_lengths,
    item_band,
    positions,
    band_table,
    adaln_weight,
    adaln_bias,
    query_weight,
    key_weight,
    value_weight,
    outproj_weight,
    capkey_weight,
    capvalue_weight,
    norm_gains,
    head_gate,
    gate_weight,
    up_weight,
    down_weight,
    cotangent,
):
    own = lax.axis_index("fsdp")
    place = lax.axis_index("dp")
    count = lax.axis_size("fsdp")
    data_count = lax.axis_size("dp")
    near = dp_place(0)
    rows, width = tokens.shape[1:]
    seq = rows * count
    part = width // count
    head_count = head_gate.shape[0]
    head_size = width // head_count
    own_heads = head_count // count
    units = down_weight.shape[0]
    text_rows = caption.shape[1]
    text = text_rows * count
    cap_depth = capkey_weight.shape[0]
    masks = (0, 1, 2, 3)

    def split_rel(values):
        return [values[m * rows : (m + 1) * rows] for m in masks]

    band_onehot = item_band[:, None] == jnp.arange(band_table.shape[0], dtype=jnp.int32)[None, :]
    band_vector = jnp.dot(band_onehot.astype(bf16), band_table, preferred_element_type=f32)
    silu_low = jax.nn.silu(band_vector).astype(bf16)
    slice_depth = adaln_weight.shape[0]
    modulation_part = mm(
        lax.dynamic_slice_in_dim(silu_low, own * slice_depth, slice_depth, 1), adaln_weight
    )[0]
    modulation_part = modulation_part + lax.dynamic_update_slice(
        jnp.zeros_like(modulation_part), adaln_bias.astype(f32), (own * adaln_bias.shape[0],)
    )
    gains_part = lax.dynamic_update_slice(
        jnp.zeros((2, width), f32), norm_gains[0::4].astype(f32), (0, own * part)
    )
    places_part = lax.dynamic_update_slice(
        jnp.zeros((2, seq), f32), positions[0].astype(f32), (0, own * rows)
    )
    small = jnp.concatenate([modulation_part, gains_part.reshape(-1), places_part.reshape(-1)])

    def cap_slice(mask):
        return lax.dynamic_slice_in_dim(caption[0], (own ^ mask) * cap_depth, cap_depth, 1)

    depth = query_weight.shape[0]
    half_depth = depth // 2

    def head_columns(mask, start, length):
        return jnp.concatenate(
            [
                lax.dynamic_slice(w, (start, (own ^ mask) * part), (length, part))
                for w in (query_weight, key_weight, value_weight)
            ],
            axis=1,
        )

    thin = gate_weight.shape[0] // data_count
    units_block = 256 if units % 256 == 0 else units

    def unit_columns(mask):
        return jnp.concatenate(
            [
                lax.dynamic_slice(w, (place * thin, (own ^ mask) * units), (thin, units))
                for w in (gate_weight, up_weight)
            ],
            axis=1,
        )

    small_far = hop(small, 2)
    cap_far = hop(jnp.stack([cap_slice(2), cap_slice(3)]), 2)
    fetched = hop(jnp.stack([head_columns(m, near * half_depth, half_depth) for m in (2, 3)]), 2)
    thin_far = hop(jnp.stack([unit_columns(2), unit_columns(3)]), 2)
    token_own = tokens[0]
    thin_near = hop(jnp.stack([unit_columns(1), thin_far[1]]), 1)
    thin_all = jnp.stack(natural_order([unit_columns(0), thin_near[0], thin_far[0], thin_near[1]], own))
    gateup_weight = lax.all_gather(thin_all, "dp", axis=1, tiled=True).reshape(width, 2 * units)
    small, small_far, cap_far, fetched, token_own, thin_all = join(
        small, small_far, cap_far, fetched, token_own, thin_all
    )

    token_far = hop(token_own, 2)
    fetched_beside = dp_hop(fetched, 0)
    small = small + small_far
    small_near = hop(small, 1)
    cap_near = hop(jnp.stack([cap_slice(1), cap_far[1]]), 1)
    caption_part = jnp.concatenate(
        natural_order([cap_slice(0), cap_near[0], cap_far[0], cap_near[1]], own), axis=0
    )
    cap_partial = jnp.concatenate(
        [mm(caption_part, capkey_weight).astype(bf16), mm(caption_part, capvalue_weight).astype(bf16)],
        axis=0,
    )

    def cap_columns(mask):
        return lax.dynamic_slice_in_dim(cap_partial, (own ^ mask) * part, part, 1)

    cap_sent = jnp.stack([cap_columns(3), cap_columns(1)])
    cap_kept = jnp.stack([cap_columns(2), cap_columns(0)])
    cap_inner = hop(cap_sent, 1)
    cap_passed = (cap_kept[0].astype(f32) + cap_inner[0].astype(f32)).astype(bf16)
    token_two = jnp.stack([token_own, token_far])
    (
        token_two, thin_all, fetched_beside, small_near, cap_inner, cap_kept, cap_passed
    ) = join(token_two, thin_all, fetched_beside, small_near, cap_inner, cap_kept, cap_passed)
    cap_passed = hop(cap_passed, 2)

    token_near = hop(token_two, 1)
    token_all = jnp.concatenate([token_two[0], token_near[0], token_two[1], token_near[1]], axis=0)
    fetched_all = jnp.concatenate(
        [jnp.where(near == 0, fetched, fetched_beside), jnp.where(near == 0, fetched_beside, fetched)],
        axis=1,
    )
    fetched_near = hop(jnp.stack([head_columns(1, 0, depth), fetched_all[1]]), 1)
    top = dp_bits() - 1

    def cap_split(values, bit):
        half = values.shape[2] // 2
        return [
            lax.dynamic_slice_in_dim(values, side * half, half, 2)
            for side in (dp_place(bit), 1 - dp_place(bit))
        ]

    token_all, fetched_near = join(token_all, fetched_near)

    small = small + small_near
    modulation = small[: 6 * width].reshape(6, 1, width)
    shift_mix, scale_mix, gate_mix, shift_feed, scale_feed, gate_feed = [modulation[i] for i in range(6)]
    gain_mix = small[6 * width : 7 * width][None]
    gain_feed = small[7 * width : 8 * width][None]
    places = small[8 * width :].reshape(2, count, rows)
    order = own ^ jnp.arange(count, dtype=jnp.int32)
    places_rel = jnp.concatenate(natural_order([places[:, m] for m in masks], own), axis=1)
    slots_rel = (order[:, None] * rows + jnp.arange(rows, dtype=jnp.int32)[None]).reshape(seq)
    live_bias = jnp.where(slots_rel < item_lengths[0], 0.0, masked_score).astype(f32)[:, None]
    text_live = caption_mask[0] > 0
    text_bias = jnp.where(text_live, 0.0, masked_score).astype(f32)[:, None]
    quarter = head_size // 4
    lane = jnp.arange(128, dtype=jnp.int32)
    frequency = jnp.exp(-jnp.log(rope_base) * (lane % quarter).astype(f32) / quarter)[None]
    by_row = (lane % head_size < 2 * quarter)[None]
    angles = jnp.where(by_row, places_rel[0][:, None], places_rel[1][:, None]) * frequency
    sign = jnp.where((lane // quarter) % 2 == 0, -1.0, 1.0).astype(f32)[None]
    tables = (jnp.cos(angles), jnp.sin(angles) * sign)

    qkv_rel = [head_columns(0, 0, depth), fetched_near[0], fetched_all[0], fetched_near[1]]
    normed_all, qkv, query_square, key_square = project(
        own, token_all, gain_mix, scale_mix, shift_mix, qkv_rel
    )
    cap_passed, query_square, key_square = join(cap_passed, query_square, key_square)
    cap_raw = cap_kept[1].astype(f32) + cap_inner[1].astype(f32) + cap_passed.astype(f32)
    capkey_raw, capvalue_low = cap_raw[:text], cap_raw[text:].astype(bf16)

    query_square, key_square, cap_square = sum_rows_rel(
        [
            query_square[0],
            key_square[0],
        ],
        count,
        [jnp.sum(capkey_raw * capkey_raw, axis=-1)],
    )
    query_inverse = lax.rsqrt(query_square / width + norm_eps)[None]
    key_inverse = lax.rsqrt(key_square / width + norm_eps)[None]
    capkey_inverse = lax.rsqrt(cap_square / width + norm_eps)[:, None]
    own_gains = norm_gains.astype(f32)
    capkey_low = (capkey_raw * capkey_inverse * own_gains[3:4]).astype(bf16)
    tanh_gate = jnp.tanh(head_gate.astype(f32))
    own_tanh = lax.dynamic_slice_in_dim(tanh_gate, own * own_heads, own_heads, 0)
    tanh_lane = jnp.repeat(own_tanh, head_size)[None]
    block_rows = seq if seq <= 1024 else 256

    query_live = (own * rows + jnp.arange(rows, dtype=jnp.int32)) < item_lengths[0]
    grad_out = cotangent[0].astype(f32) * query_live[:, None].astype(f32)
    grad_ffn = (gate_feed * grad_out).astype(bf16)
    grad_ffn, query_inverse, key_inverse, capkey_low = join(
        grad_ffn, query_inverse, key_inverse, capkey_low
    )
    grad_ffn_far = hop(grad_ffn, 2)
    attended, query_low, key_low, value_low, lse = attend_forward(
        qkv, (query_inverse, key_inverse), (own_gains[1:2], own_gains[2:3]), tables,
        capkey_low, capvalue_low, live_bias, text_bias, tanh_lane, block_rows,
    )
    attended, grad_ffn_far = join(attended, grad_ffn_far)

    branch_part = mm(attended, outproj_weight).astype(bf16)
    branch_near = hop(
        jnp.stack([branch_part[3 * rows :], branch_part[rows : 2 * rows]]), 1
    )
    branch_passed = (
        branch_part[2 * rows : 3 * rows].astype(f32) + branch_near[0].astype(f32)
    ).astype(bf16)
    branch_kept = branch_part[:rows].astype(f32) + branch_near[1].astype(f32)
    branch_passed, branch_kept, grad_ffn_far = join(branch_passed, branch_kept, grad_ffn_far)
    branch_passed = hop(branch_passed, 2)
    grad_ffn_near = hop(jnp.stack([grad_ffn, grad_ffn_far]), 1)
    grad_ffn_rel = [grad_ffn, grad_ffn_near[0], grad_ffn_far, grad_ffn_near[1]]
    grad_ffn_all = jnp.concatenate(grad_ffn_rel, axis=0)
    branch_passed, gateup_weight, grad_ffn_all, *grad_ffn_rel = join(
        branch_passed, gateup_weight, grad_ffn_all, *grad_ffn_rel
    )
    branch = branch_kept + branch_passed.astype(f32)
    token_float = token_own.astype(f32)
    middle = token_float + gate_mix * branch

    unit_feed, inverse_feed = rms_parts(middle)
    normed_feed = (unit_feed * gain_feed * (1.0 + scale_feed) + shift_feed).astype(bf16)
    feed_far = hop(normed_feed, 2)
    feed_near = hop(normed_feed, 1)
    hidden_early, grads_early = feed_forward(
        [normed_feed, feed_near], grad_ffn_rel[:2], gateup_weight, down_weight, units_block
    )
    early = mm_nt(grads_early, gateup_weight).astype(bf16)
    feed_far, hidden_early, early = join(feed_far, hidden_early, early)
    feed_rel = [normed_feed, feed_near, feed_far, hop(feed_far, 1)]
    hidden_late, grads_late = feed_forward(
        feed_rel[2:], grad_ffn_rel[2:], gateup_weight, down_weight, units_block
    )
    late = mm_nt(grads_late, gateup_weight).astype(bf16)
    late_near = hop(late[rows:], 1)
    passed = (late[:rows].astype(f32) + late_near.astype(f32)).astype(bf16)
    cap_items, cap_items_sent = cap_split(caption[0][None], top)
    passed, early, hidden_late, grads_late, cap_items_sent = join(
        passed, early, hidden_late, grads_late, cap_items_sent
    )

    passed = hop(passed, 2)
    early_near = hop(early[rows:], 1)
    cap_items = jnp.concatenate([cap_items, dp_hop(cap_items_sent, top)], axis=0)
    hidden = jnp.concatenate([hidden_early, hidden_late], axis=0)
    down_blocks = dp_blocks(mm_tn(hidden, grad_ffn_all).astype(bf16))
    down_cut = width // 3
    down_first = dp_hop(dp_sent(down_blocks, 0, down_cut), 0)
    feed_all = jnp.concatenate(feed_rel, axis=0)
    grad_units = jnp.concatenate([grads_early, grads_late], axis=0)
    gateup_blocks = dp_blocks(mm_tn(feed_all, grad_units).astype(bf16))
    down_sent = dp_sent(down_blocks, down_cut, width)
    passed, early_near, down_first, gateup_blocks, down_sent, cap_items = join(
        passed, early_near, down_first, gateup_blocks, down_sent, cap_items
    )
    down_second = dp_hop(down_sent, 0)
    grad_normfeed = early[:rows].astype(f32) + early_near.astype(f32) + passed.astype(f32)

    dshift_feed = jnp.sum(grad_normfeed, axis=0)
    dscale_feed = jnp.sum(grad_normfeed * (unit_feed * gain_feed), axis=0)
    grad_scaledfeed = grad_normfeed * (1.0 + scale_feed)
    gain_feed_grad = jnp.sum(grad_scaledfeed * unit_feed, axis=0)
    grad_middle = grad_out + rms_back(unit_feed, inverse_feed, grad_scaledfeed * gain_feed)
    dgate_mix = jnp.sum(grad_middle * branch, axis=0)

    grad_branch = (gate_mix * grad_middle).astype(bf16)
    grad_branch, gateup_blocks = join(grad_branch, gateup_blocks)
    grad_branch_far = hop(grad_branch, 2)
    ffn_part = mm(hidden, down_weight).astype(bf16)
    cuts = [2 * units * i // 16 for i in (0, 4, 7, 11, 16)]
    gateup_sent = dp_sent(gateup_blocks, cuts[0], cuts[1])
    for bit in reversed(range(1, top)):
        cap_items, cap_items_sent = cap_split(cap_items, bit)
        cap_items = jnp.concatenate([cap_items, dp_hop(cap_items_sent, bit)], axis=0)
    cap_items, cap_items_sent = cap_split(cap_items, 0)
    grad_branch_far, down_second, ffn_part, gateup_sent, cap_items_sent = join(
        grad_branch_far, down_second, ffn_part, gateup_sent, cap_items_sent
    )
    gateup_first = dp_hop(gateup_sent, 0)
    cap_items = jnp.concatenate([cap_items, dp_hop(cap_items_sent, 0)], axis=0)
    grad_branch_two = jnp.stack([grad_branch, grad_branch_far])
    grad_branch_near = hop(grad_branch_two, 1)
    ffn_near = hop(jnp.stack([ffn_part[3 * rows :], ffn_part[rows : 2 * rows]]), 1)
    grad_branch_all = jnp.concatenate(
        [grad_branch, grad_branch_near[0], grad_branch_far, grad_branch_near[1]], axis=0
    )
    down_joined = [
        dp_joined(down_blocks, down_first, 0, down_cut),
        dp_joined(down_blocks, down_second, down_cut, width),
    ]
    down_kept = jnp.concatenate([kept for kept, _ in down_joined], axis=-1)
    down_line = dp_hop(jnp.concatenate([sent for _, sent in down_joined], axis=-1), 1)
    grad_attended = mm_nt(grad_branch_all, outproj_weight).astype(bf16)
    dquery_text, dcapkey, grad_capvalue, dtanh = text_backward(
        query_low, capkey_low, capvalue_low, grad_attended, lse, text_bias, tanh_lane, seq
    )
    outproj_part = mm_tn(attended, grad_branch_all).astype(bf16)
    outproj_blocks = (
        outproj_part.reshape(data_count, -1, count, part)
        .transpose(0, 2, 1, 3)
        .reshape(data_count, width // data_count, part)
    )
    gateup_sent = dp_sent(gateup_blocks, cuts[1], cuts[2])
    (
        dquery_text, dcapkey, grad_capvalue, dtanh, gateup_first, down_line, ffn_near, cap_items,
        outproj_blocks, gateup_sent,
    ) = join(
        dquery_text, dcapkey, grad_capvalue, dtanh, gateup_first, down_line, ffn_near, cap_items,
        outproj_blocks, gateup_sent,
    )
    gateup_more = dp_hop(gateup_sent, 0)
    cap_items_far = hop(cap_items, 2)
    capkey_unit = capkey_raw * capkey_inverse
    capkey_scaled = dcapkey * own_gains[3:4]
    (cap_dot,) = sum_rows_rel([], count, [jnp.sum(capkey_scaled * capkey_unit, axis=-1)])
    grad_capkey = (
        capkey_inverse * (capkey_scaled - capkey_unit * (cap_dot[:, None] / width))
    ).astype(bf16)
    gain_capkey_grad = jnp.sum(dcapkey * capkey_unit, axis=0)
    grad_cap = jnp.concatenate([grad_capkey, grad_capvalue], axis=1)
    ffn_passed = (
        ffn_part[2 * rows : 3 * rows].astype(f32) + ffn_near[0].astype(f32)
    ).astype(bf16)
    gateup_sent = jnp.concatenate(
        [dp_sent(gateup_blocks, cuts[2], cuts[3]), dp_sent(outproj_blocks, 0, part)], axis=-1
    )
    dquery_text, grad_cap, ffn_passed, gateup_sent, gateup_more, cap_items_far = join(
        dquery_text, grad_cap, ffn_passed, gateup_sent, gateup_more, cap_items_far
    )

    ffn_passed = hop(ffn_passed, 2)
    gateup_second = dp_hop(gateup_sent, 0)
    down_state = dp_next((down_kept, down_line), 2) if top >= 2 else (down_kept, down_line)
    gateup_joined = [
        dp_joined(gateup_blocks, gateup_first, cuts[0], cuts[1]),
        dp_joined(gateup_blocks, gateup_more, cuts[1], cuts[2]),
    ]
    gateup_kept = jnp.concatenate([kept for kept, _ in gateup_joined], axis=-1)
    gateup_line = dp_hop(jnp.concatenate([sent for _, sent in gateup_joined], axis=-1), 1)
    cap_grads = jnp.stack([grad_cap, dp_hop(grad_cap, top)])
    query_unrot, key_unrot, grad_value = self_backward(
        query_low, key_low, value_low, grad_attended, lse, dquery_text, tables, live_bias, block_rows
    )
    gateup_sent = dp_sent(gateup_blocks, cuts[3], cuts[4])
    (
        query_unrot, key_unrot, grad_value, ffn_passed, gateup_second, down_arrived, gateup_line,
        cap_grads, gateup_sent,
    ) = join(
        query_unrot, key_unrot, grad_value, ffn_passed, gateup_second, down_state[1], gateup_line,
        cap_grads, gateup_sent,
    )
    down_state = (down_state[0], down_arrived)
    cap_items_two = jnp.stack([cap_items, cap_items_far], axis=1)

    gateup_third = dp_hop(gateup_sent, 0)
    second_width = cuts[3] - cuts[2]
    second_joined = [
        dp_joined(gateup_blocks, gateup_second[..., :second_width], cuts[2], cuts[3]),
        dp_joined(outproj_blocks, gateup_second[..., second_width:], 0, part),
    ]
    second_kept = jnp.concatenate([kept for kept, _ in second_joined], axis=-1)
    second_line = dp_hop(jnp.concatenate([sent for _, sent in second_joined], axis=-1), 1)
    down_sum = dp_total(down_state) if top <= 2 else dp_rest_from(down_state, 3)
    owned_down = to_owner(down_sum)
    first_state = dp_next((gateup_kept, gateup_line), 2) if top >= 2 else (gateup_kept, gateup_line)
    query_inverse, key_inverse = query_inverse[0][:, None], key_inverse[0][:, None]
    query_unit = qkv[:, :part] * query_inverse
    key_unit = qkv[:, part : 2 * part] * key_inverse
    query_scaled = query_unrot * own_gains[1:2]
    key_scaled = key_unrot * own_gains[2:3]
    query_dot, key_dot = sum_rows_rel(
        [
            jnp.sum(query_scaled * query_unit, axis=-1),
            jnp.sum(key_scaled * key_unit, axis=-1),
        ],
        count,
    )
    gain_query_grad = jnp.sum(query_unrot * query_unit, axis=0)
    gain_key_grad = jnp.sum(key_unrot * key_unit, axis=0)
    grad_qkv = jnp.concatenate(
        [
            (query_inverse * (query_scaled - query_unit * (query_dot[:, None] / width))).astype(bf16),
            (key_inverse * (key_scaled - key_unit * (key_dot[:, None] / width))).astype(bf16),
            grad_value,
        ],
        axis=1,
    )
    qkv_blocks = dp_blocks(mm_tn(normed_all, grad_qkv).astype(bf16))
    qkv_sent = dp_sent(qkv_blocks, 0, 3 * part)
    qkv_sent, gateup_third, first_arrived, second_line, owned_down = join(
        qkv_sent, gateup_third, first_state[1], second_line, owned_down
    )
    first_state = (first_state[0], first_arrived)

    qkv_beside = dp_hop(qkv_sent, 0)
    third_kept, third_line = dp_joined(gateup_blocks, gateup_third, cuts[3], cuts[4])
    third_line = dp_hop(third_line, 1)
    second_state = dp_next((second_kept, second_line), 2) if top >= 2 else (second_kept, second_line)
    for bit in reversed(range(1, top)):
        cap_grads = jnp.concatenate([cap_grads, dp_hop(cap_grads, bit)], axis=0)
    normmix_part = project_back(own, grad_qkv, qkv_rel)
    normmix_near = hop(jnp.stack([normmix_part[3 * rows :], normmix_part[rows : 2 * rows]]), 1)
    normmix_passed = hop(
        (normmix_part[2 * rows : 3 * rows].astype(f32) + normmix_near[0].astype(f32)).astype(bf16), 2
    )
    qkv_beside, third_line, normmix_passed, cap_grads, second_arrived, cap_items_two = join(
        qkv_beside, third_line, normmix_passed, cap_grads, second_state[1], cap_items_two
    )
    second_state = (second_state[0], second_arrived)
    cap_items_near = hop(cap_items_two, 1)
    cap_items_all = jnp.stack(
        natural_order(
            [cap_items_two[:, 0], cap_items_near[:, 0], cap_items_two[:, 1], cap_items_near[:, 1]], own
        ),
        axis=1,
    ).reshape(data_count * text, -1)

    qkv_kept, qkv_line = dp_joined(qkv_blocks, qkv_beside, 0, 3 * part)
    qkv_line = dp_hop(qkv_line, 1)
    third_state = dp_next((third_kept, third_line), 2) if top >= 2 else (third_kept, third_line)
    cap_grads = jnp.concatenate([cap_grads, dp_hop(cap_grads, 0)], axis=0)
    grad_normmix = (
        normmix_part[:rows].astype(f32) + normmix_near[1].astype(f32) + normmix_passed.astype(f32)
    )
    ffn_out = ffn_part[:rows].astype(f32) + ffn_near[1].astype(f32) + ffn_passed.astype(f32)
    block_out = (middle + gate_feed * ffn_out).astype(bf16)
    dgate_feed = jnp.sum(grad_out * ffn_out, axis=0)
    unit_mix, inverse_mix = rms_parts(token_float)
    dshift_mix = jnp.sum(grad_normmix, axis=0)
    dscale_mix = jnp.sum(grad_normmix * (unit_mix * gain_mix), axis=0)
    grad_scaledmix = grad_normmix * (1.0 + scale_mix)
    gain_mix_grad = jnp.sum(grad_scaledmix * unit_mix, axis=0)
    tokens_grad = (
        grad_middle + rms_back(unit_mix, inverse_mix, grad_scaledmix * gain_mix)
    ).astype(bf16)

    own_rows = jnp.zeros((3, width), f32)
    own_rows = lax.dynamic_update_slice(
        own_rows, jnp.stack([gain_query_grad, gain_key_grad, gain_capkey_grad]), (0, own * part)
    )
    gate_sums = lax.dynamic_update_slice(
        jnp.zeros((head_count,), f32), dtanh[0, ::head_size], (own * own_heads,)
    )
    sums = jnp.concatenate([gain_mix_grad, own_rows.reshape(-1), gain_feed_grad, gate_sums])
    grad_modulation = jnp.concatenate(
        [dshift_mix, dscale_mix, dgate_mix, dshift_feed, dscale_feed, dgate_feed]
    )
    message = jnp.concatenate([grad_modulation, sums])
    message = message + hop(message, 1)
    message = message + hop(message, 2)
    mod_width = 6 * width
    item_rows = jnp.concatenate([message[:mod_width], silu_low[0].astype(f32)]).astype(bf16)[None]
    totals = message[mod_width:]

    def wider(item_rows, totals, bit):
        high = totals.astype(bf16)
        low = (totals - high.astype(f32)).astype(bf16)
        arrived = dp_hop(jnp.concatenate([item_rows.reshape(-1), high, low]), bit)
        rest = arrived[item_rows.size :].astype(f32)
        return (
            jnp.concatenate([item_rows, arrived[: item_rows.size].reshape(item_rows.shape)], axis=0),
            totals + (rest[: totals.size] + rest[totals.size :]),
        )

    first_sum = dp_total(first_state) if top <= 2 else dp_rest_from(first_state, 3)
    second_sum = dp_total(second_state) if top <= 2 else dp_rest_from(second_state, 3)
    outproj_sum = (
        second_sum[:, second_width:].reshape(count, -1, part).transpose(1, 0, 2).reshape(-1, width)
    )
    owned_outproj = to_owner(outproj_sum)
    second_sum = second_sum[:, :second_width]
    qkv_line, item_rows, totals, third_arrived, first_sum, second_sum, owned_outproj = join(
        qkv_line, item_rows, totals, third_state[1], first_sum, second_sum, owned_outproj
    )

    qkv_state = dp_next((qkv_kept, qkv_line), 2) if top >= 2 else (qkv_kept, qkv_line)
    third_state = (third_state[0], third_arrived)
    third_sum = dp_total(third_state) if top <= 2 else dp_rest_from(third_state, 3)
    gateup_pieces, gateup_sent = spread_pieces([first_sum, second_sum, third_sum], own)
    gateup_far = hop(gateup_sent, 2)
    item_rows, totals = wider(item_rows, totals, 0)
    cap_sum = mm_tn(cap_items_all, cap_grads.reshape(-1, cap_grads.shape[-1]))
    cap_pieces, cap_sent_far = spread_pieces([cap_sum], own)
    qkv_arrived, gateup_far, item_rows, totals, cap_sent_far = join(
        qkv_state[1], gateup_far, item_rows, totals, cap_sent_far
    )
    qkv_state = (qkv_state[0], qkv_arrived)

    qkv_sum = dp_total(qkv_state) if top <= 2 else dp_rest_from(qkv_state, 3)
    qkv_pieces, qkv_sent_far = spread_pieces([qkv_sum], own)
    qkv_far = hop(qkv_sent_far, 2)
    cap_far_rows = hop(cap_sent_far, 2)
    gateup_near = spread_near(gateup_pieces, gateup_far)
    item_rows, totals = wider(item_rows, totals, 1)
    qkv_far, cap_far_rows, gateup_near, item_rows, totals = join(
        qkv_far, cap_far_rows, gateup_near, item_rows, totals
    )
    qkv_near = spread_near(qkv_pieces, qkv_far)
    cap_near_rows = spread_near(cap_pieces, cap_far_rows)
    for bit in range(2, top + 1):
        item_rows, totals = wider(item_rows, totals, bit)
    gate_grad, up_grad = spread_result(gateup_pieces, gateup_far, gateup_near, [units] * 2, own)
    query_grad, key_grad, value_grad = spread_result(qkv_pieces, qkv_far, qkv_near, [part] * 3, own)
    capkey_grad, capvalue_grad = spread_result(cap_pieces, cap_far_rows, cap_near_rows, [part] * 2, own)
    modulation_rows = item_rows[:, :mod_width].astype(f32)
    silu_rows = item_rows[:, mod_width:].astype(f32)
    owner = place * count + own
    devices = count * data_count
    cd_rows = silu_rows.shape[1] // devices
    adaln_wgrad = lax.dot_general(
        lax.dynamic_slice_in_dim(silu_rows, owner * cd_rows, cd_rows, 1),
        modulation_rows,
        (((0,), (0,)), ((), ())),
        precision=lax.Precision.HIGHEST,
        preferred_element_type=f32,
    )
    bias_rows = mod_width // devices
    adaln_bgrad = lax.dynamic_slice_in_dim(
        jnp.sum(modulation_rows, axis=0), owner * bias_rows, bias_rows, 0
    )
    gains_grad = lax.dynamic_slice_in_dim(
        totals[: 5 * width].reshape(5, width), owner * (width // devices), width // devices, 1
    )
    headgate_grad = totals[5 * width :] * (1.0 - tanh_gate * tanh_gate)

    down_grad, outproj_grad = owned_down, owned_outproj
    return (
        block_out[None],
        tokens_grad[None],
        adaln_wgrad,
        adaln_bgrad,
        query_grad,
        key_grad,
        value_grad,
        outproj_grad,
        capkey_grad,
        capvalue_grad,
        gains_grad,
        headgate_grad,
        gate_grad,
        up_grad,
        down_grad,
    )


def solution(mesh):
    return jax.shard_map(
        on_device,
        mesh=mesh,
        in_specs=(
            P("dp", "fsdp", None),
            P("dp", "fsdp", None),
            P("dp", None),
            P("dp"),
            P("dp"),
            P("dp", None, "fsdp"),
            P(),
            P("fsdp", None),
            P("fsdp"),
            P("fsdp", None),
            P("fsdp", None),
            P("fsdp", None),
            P("fsdp", None),
            P("fsdp", None),
            P("fsdp", None),
            P(None, "fsdp"),
            P(),
            P("fsdp", None),
            P("fsdp", None),
            P("fsdp", None),
            P("dp", "fsdp", None),
        ),
        out_specs=(
            P("dp", "fsdp", None),
            P("dp", "fsdp", None),
            P(("dp", "fsdp"), None),
            P(("dp", "fsdp")),
            P(("dp", "fsdp"), None),
            P(("dp", "fsdp"), None),
            P(("dp", "fsdp"), None),
            P(("dp", "fsdp"), None),
            P(("dp", "fsdp"), None),
            P(("dp", "fsdp"), None),
            P(None, ("dp", "fsdp")),
            P(),
            P(("dp", "fsdp"), None),
            P(("dp", "fsdp"), None),
            P(("dp", "fsdp"), None),
        ),
        check_vma=False,
    )
```

```python
import jax
import jax.numpy as jnp
from jax import lax
from jax.experimental import pallas as pl
from jax.experimental.pallas import tpu as pltpu
from jax.sharding import PartitionSpec as P

norm_eps = 1e-06
rope_base = 10000.0
masked_score = -1e30
f32 = jnp.float32
bf16 = jnp.bfloat16


def mm(left_side, right_side):
    return lax.dot_general(
        left_side, right_side, (((1,), (0,)), ((), ())), preferred_element_type=f32
    )


def mm_nt(left_side, right_side):
    return lax.dot_general(
        left_side, right_side, (((1,), (1,)), ((), ())), preferred_element_type=f32
    )


def mm_tn(left_side, right_side):
    return lax.dot_general(
        left_side, right_side, (((0,), (0,)), ((), ())), preferred_element_type=f32
    )


def rms_parts(values):
    inverse = lax.rsqrt(jnp.mean(values * values, axis=-1, keepdims=True) + norm_eps)
    return (values * inverse, inverse)


def rms_back(unit_rows, inverse, grad_unit):
    return inverse * (
        grad_unit - unit_rows * jnp.mean(grad_unit * unit_rows, axis=-1, keepdims=True)
    )


def hop(values, mask):
    count = lax.axis_size("fsdp")
    return lax.ppermute(values, "fsdp", [(i, i ^ mask) for i in range(count)])


def gather_rel(values):
    two = jnp.stack([values, hop(values, 2)])
    other = hop(two, 1)
    return [values, other[0], two[1], other[1]]


def scatter_rel(blocks):
    arrived = hop(jnp.stack([blocks[3], blocks[1]]), 1)
    passed = hop((blocks[2].astype(f32) + arrived[0].astype(f32)).astype(bf16), 2)
    return blocks[0].astype(f32) + arrived[1].astype(f32) + passed.astype(f32)


def trade_rel(blocks, middle=None):
    far = hop(jnp.stack([blocks[2], blocks[3]]), 2)
    if middle is not None:
        far = middle(far)
    beside = hop(jnp.stack([blocks[1], far[1]]), 1)
    return [blocks[0], beside[0], far[0], beside[1]]


def swap_blocks(values, mask, count):
    rows = values.shape[0] // count
    return jnp.concatenate(
        [values[(m ^ mask) * rows : ((m ^ mask) + 1) * rows] for m in range(count)], axis=0
    )


def sum_rows_rel(columns, count, plain=()):
    swapped = len(columns)
    columns = list(columns) + list(plain)
    ends = [0]
    for column in columns:
        ends.append(ends[-1] + column.shape[0])
    total = jnp.concatenate(columns)
    for mask in (1, 2):
        arrived = hop(total, mask)
        total = total + jnp.concatenate(
            [swap_blocks(arrived[i:j], mask, count) for i, j in zip(ends, ends[1 : swapped + 1])]
            + [arrived[ends[swapped] :]]
        )
    return [total[i:j] for i, j in zip(ends, ends[1:])]


def natural_order(pieces, own):
    far, near = own // 2, own % 2
    mixed = [[jnp.where(near == 0, pieces[2 * i + j], pieces[2 * i + 1 - j]) for j in range(2)] for i in range(2)]
    return [jnp.where(far == 0, mixed[i][j], mixed[1 - i][j]) for i in range(2) for j in range(2)]


def join(*values):
    return lax.optimization_barrier(values)


def dp_bits():
    return lax.axis_size("dp").bit_length() - 1


def dp_hop(values, bit):
    count = lax.axis_size("dp")
    return lax.ppermute(values, "dp", [(i, i ^ (1 << bit)) for i in range(count)])


def dp_place(bit):
    return (lax.axis_index("dp") >> bit) & 1


def pick(values, axis, index):
    return lax.dynamic_index_in_dim(values, index, axis, keepdims=False)


def dp_blocks(partial):
    return partial.reshape(lax.axis_size("dp"), -1, partial.shape[1])


def dp_half(blocks, bit, other):
    pairs = blocks.reshape((-1, 2) + blocks.shape[1:])
    return pick(pairs, 1, 1 - dp_place(bit) if other else dp_place(bit))


def dp_sent(blocks, start, stop):
    return dp_half(blocks[..., start:stop], 0, True)


def dp_joined(blocks, arrived, start, stop):
    return dp_sums((dp_half(blocks[..., start:stop], 0, False), arrived), 1)


def dp_sums(state, bit):
    kept, arrived = state

    def half(other):
        return (
            dp_half(kept, bit, other).astype(f32) + dp_half(arrived, bit, other).astype(f32)
        ).astype(bf16)

    return (half(False), half(True))


def dp_next(state, bit):
    kept, sent = dp_sums(state, bit)
    return (kept, dp_hop(sent, bit))


def dp_total(state):
    return state[0][0].astype(f32) + state[1][0].astype(f32)


def dp_rest_from(state, start):
    for bit in range(start, dp_bits()):
        state = dp_next(state, bit)
    return dp_total(state)


def dp_rest(state):
    return dp_rest_from(state, 1)


def cap_order(values, top):
    return values.reshape(-1, values.shape[-1])


def spread_pieces(totals, own):
    count = lax.axis_size("fsdp")
    low = jnp.concatenate([total.astype(bf16) for total in totals], axis=1)
    rows = low.shape[0] // count
    pieces = [lax.dynamic_slice_in_dim(low, (own ^ m) * rows, rows, 0) for m in range(count)]
    return (jnp.stack(pieces[:2]), jnp.stack(pieces[2:]))


def spread_near(pieces, far):
    return hop(jnp.stack([pieces[1], far[1]]), 1)


def spread_result(pieces, far, near, widths, own):
    results, start = [], 0
    for width in widths:
        part = [
            piece[:, start : start + width] for piece in (pieces[0], near[0], far[0], near[1])
        ]
        results.append(jnp.concatenate(natural_order(part, own), axis=1).astype(f32))
        start += width
    return results


def to_owner(total):
    data_count, count = lax.axis_size("dp"), lax.axis_size("fsdp")
    pairs = [(d * count + f, f * data_count + d) for d in range(data_count) for f in range(count)]
    return lax.ppermute(total.astype(bf16), ("dp", "fsdp"), pairs).astype(f32)


def lane_of(shape):
    return lax.broadcasted_iota(jnp.int32, shape, len(shape) - 1)


def rotate_lanes(values, cosines, sines):
    lanes = lane_of(values.shape)
    even = lax.rem(lax.div(lanes, 16), 2) == 0
    width = values.shape[-1]
    partner = jnp.where(even, pltpu.roll(values, width - 16, 1), pltpu.roll(values, 16, 1))
    return values * cosines + partner * sines


def as_column(row):
    return jnp.transpose(jnp.broadcast_to(row, (8, row.shape[1])))[:, :1]


def head_lanes(values, head, spare):
    lanes = lane_of(values.shape)
    mine = (lanes < 64) if head == 0 else (lanes >= 64)
    mark = 64 if head == 0 else 0
    return jnp.where(mine, values, jnp.where(lanes == mark, spare, jnp.zeros_like(values)))


def attend_body(
    q_ref, k_ref, v_ref, qinv_ref, kinv_ref, qg_ref, kg_ref, cosq_ref, sinq_ref, cosk_ref, sink_ref,
    ck_ref, cv_ref, live_ref, text_ref, tanh_ref,
    out_ref, qlow_ref, klow_ref, vlow_ref, lse_ref,
    km, vm, cm, cvm,
):
    @pl.when(pl.program_id(1) == 0)
    def _():
        key = rotate_lanes(
            k_ref[...] * as_column(kinv_ref[...]) * kg_ref[...], cosk_ref[...], sink_ref[...]
        ).astype(bf16)
        value = v_ref[...].astype(bf16)
        klow_ref[...] = key
        vlow_ref[...] = value
        one = jnp.ones((), bf16)
        for head in range(2):
            km[head] = head_lanes(key, head, live_ref[...].astype(bf16))
            vm[head] = head_lanes(value, head, one)
            cm[head] = head_lanes(ck_ref[...], head, text_ref[...].astype(bf16))
            cvm[head] = head_lanes(cv_ref[...], head, one)

    query = rotate_lanes(
        q_ref[...] * as_column(qinv_ref[...]) * qg_ref[...], cosq_ref[...], sinq_ref[...]
    ).astype(bf16)
    qlow_ref[...] = query
    scaled = query * jnp.asarray(0.125, bf16)
    lanes = lane_of(out_ref.shape)
    results, stats = [], []
    for head in range(2):
        part = head_lanes(scaled, head, jnp.ones((), bf16))
        mark = 64 if head == 0 else 0

        def one_side(keys, values):
            scores = mm_nt(part, keys)
            peak = jnp.max(scores, axis=-1, keepdims=True)
            weights = jnp.exp(scores - peak).astype(bf16)
            mixed = mm(weights, values)
            amount = mixed[:, mark : mark + 1]
            stats.append(peak + jnp.log(amount))
            return mixed / amount

        own = one_side(km[head], vm[head])
        text = one_side(cm[head], cvm[head])
        results.append(own + tanh_ref[...] * text)
    out_ref[...] = jnp.where(lanes < 64, results[0], results[1]).astype(bf16)
    table = jnp.where(lanes == 0, stats[0], stats[1])
    table = jnp.where(lanes == 2, stats[2], table)
    lse_ref[...] = jnp.where(lanes == 3, stats[3], table)


def attend_forward(qkv, inverses, gains, tables, capkey, capvalue, live_bias, text_bias, tanh_lane, rows):
    seq, width = qkv.shape[0], qkv.shape[1] // 3
    pairs, text = width // 128, capkey.shape[0]
    full = lambda p, i: (0, p)
    block = lambda p, i: (i, p)
    qrow = lambda p, i: (i, 0)
    whole = lambda p, i: (0, 0)
    return pl.pallas_call(
        attend_body,
        grid=(pairs, seq // rows),
        in_specs=[
            pl.BlockSpec((rows, 128), block),
            pl.BlockSpec((seq, 128), lambda p, i: (0, p + pairs)),
            pl.BlockSpec((seq, 128), lambda p, i: (0, p + 2 * pairs)),
            pl.BlockSpec((1, rows), lambda p, i: (0, i)),
            pl.BlockSpec((1, seq), whole),
            pl.BlockSpec((1, 128), full),
            pl.BlockSpec((1, 128), full),
            pl.BlockSpec((rows, 128), qrow),
            pl.BlockSpec((rows, 128), qrow),
            pl.BlockSpec((seq, 128), whole),
            pl.BlockSpec((seq, 128), whole),
            pl.BlockSpec((text, 128), full),
            pl.BlockSpec((text, 128), full),
            pl.BlockSpec((seq, 1), whole),
            pl.BlockSpec((text, 1), whole),
            pl.BlockSpec((1, 128), full),
        ],
        out_specs=[
            pl.BlockSpec((rows, 128), block),
            pl.BlockSpec((rows, 128), block),
            pl.BlockSpec((seq, 128), full),
            pl.BlockSpec((seq, 128), full),
            pl.BlockSpec((rows, 128), block),
        ],
        out_shape=[
            jax.ShapeDtypeStruct((seq, width), bf16),
            jax.ShapeDtypeStruct((seq, width), bf16),
            jax.ShapeDtypeStruct((seq, width), bf16),
            jax.ShapeDtypeStruct((seq, width), bf16),
            jax.ShapeDtypeStruct((seq, width), f32),
        ],
        scratch_shapes=[
            pltpu.VMEM((2, seq, 128), bf16),
            pltpu.VMEM((2, seq, 128), bf16),
            pltpu.VMEM((2, text, 128), bf16),
            pltpu.VMEM((2, text, 128), bf16),
        ],
        compiler_params=pltpu.CompilerParams(
            dimension_semantics=("arbitrary", "arbitrary"), vmem_limit_bytes=20 << 20
        ),
        cost_estimate=pl.CostEstimate(
            flops=seq * width,
            transcendentals=0,
            bytes_accessed=seq * width,
        ),
        name="attend_forward",
    )(
        qkv, qkv, qkv, inverses[0], inverses[1], gains[0], gains[1], tables[0], tables[1],
        tables[0], tables[1], capkey, capvalue, live_bias, text_bias, tanh_lane,
    )


def text_back_body(
    q_ref, ck_ref, cv_ref, do_ref, lse_ref, text_ref, tanh_ref,
    dq_ref, dck_ref, dcv_ref, dtanh_ref,
    cm, dck, dcv,
):
    step = pl.program_id(1)

    @pl.when(step == 0)
    def _():
        for head in range(2):
            cm[head] = head_lanes(ck_ref[...], head, text_ref[...].astype(bf16))
        dck[...] = jnp.zeros_like(dck)
        dcv[...] = jnp.zeros_like(dcv)
        dtanh_ref[...] = jnp.zeros_like(dtanh_ref)

    scaled = q_ref[...] * jnp.asarray(0.125, bf16)
    grad = do_ref[...]
    lse = lse_ref[...]
    grads = []
    for head in range(2):
        part = head_lanes(scaled, head, jnp.ones((), bf16))
        grad_part = head_lanes(grad, head, jnp.zeros((), bf16))
        gate = tanh_ref[:, 64 * head : 64 * head + 1]
        probs = jnp.exp(mm_nt(part, cm[head]) - lse[:, 2 * head + 1 : 2 * head + 2])
        dprob = mm_nt(grad_part, cv_ref[...])
        total = jnp.sum(probs * dprob, axis=-1, keepdims=True)
        dscore = (probs * ((dprob - total) * gate)).astype(bf16)
        grads.append(mm(dscore, ck_ref[...]))

        def add(target, update):
            lanes = lane_of(target.shape)
            mine = (lanes < 64) if head == 0 else (lanes >= 64)
            target[...] += jnp.where(mine, update, jnp.zeros_like(update))

        add(dck, mm_tn(dscore, scaled))
        add(dcv, mm_tn(probs.astype(bf16), grad))
        add(dtanh_ref, jnp.broadcast_to(jnp.sum(total, axis=0, keepdims=True), dtanh_ref.shape))
    lanes = lane_of(dq_ref.shape)
    dq_ref[...] = jnp.where(lanes < 64, grads[0], grads[1])

    @pl.when(step == pl.num_programs(1) - 1)
    def _():
        dck_ref[...] = dck[...]
        dcv_ref[...] = (dcv[...] * tanh_ref[...]).astype(bf16)


def text_backward(query, capkey, capvalue, grad, lse, text_bias, tanh_lane, rows):
    seq, width = query.shape
    pairs, text = width // 128, capkey.shape[0]
    full = lambda p, i: (0, p)
    block = lambda p, i: (i, p)
    whole = lambda p, i: (0, 0)
    return pl.pallas_call(
        text_back_body,
        grid=(pairs, seq // rows),
        in_specs=[
            pl.BlockSpec((rows, 128), block),
            pl.BlockSpec((text, 128), full),
            pl.BlockSpec((text, 128), full),
            pl.BlockSpec((rows, 128), block),
            pl.BlockSpec((rows, 128), block),
            pl.BlockSpec((text, 1), whole),
            pl.BlockSpec((1, 128), full),
        ],
        out_specs=[
            pl.BlockSpec((rows, 128), block),
            pl.BlockSpec((text, 128), full),
            pl.BlockSpec((text, 128), full),
            pl.BlockSpec((8, 128), full),
        ],
        out_shape=[
            jax.ShapeDtypeStruct((seq, width), f32),
            jax.ShapeDtypeStruct((text, width), f32),
            jax.ShapeDtypeStruct((text, width), bf16),
            jax.ShapeDtypeStruct((8, width), f32),
        ],
        scratch_shapes=[
            pltpu.VMEM((2, text, 128), bf16),
            pltpu.VMEM((text, 128), f32),
            pltpu.VMEM((text, 128), f32),
        ],
        compiler_params=pltpu.CompilerParams(
            dimension_semantics=("arbitrary", "arbitrary"), vmem_limit_bytes=20 << 20
        ),
        cost_estimate=pl.CostEstimate(
            flops=40 * seq * text * width,
            transcendentals=seq * text * width // 64,
            bytes_accessed=seq * width * 16,
        ),
        name="text_backward",
    )(query, capkey, capvalue, grad, lse, text_bias, tanh_lane)


def self_back_body(
    q_ref, k_ref, v_ref, do_ref, lse_ref, dqt_ref, cosq_ref, sinq_ref, cosk_ref, sink_ref, live_ref,
    dq_ref, dk_ref, dv_ref,
    km, dk, dv,
):
    step = pl.program_id(1)

    @pl.when(step == 0)
    def _():
        for head in range(2):
            km[head] = head_lanes(k_ref[...], head, live_ref[...].astype(bf16))
        dk[...] = jnp.zeros_like(dk)
        dv[...] = jnp.zeros_like(dv)

    scaled = q_ref[...] * jnp.asarray(0.125, bf16)
    grad = do_ref[...]
    lse = lse_ref[...]
    grads = []
    for head in range(2):
        part = head_lanes(scaled, head, jnp.ones((), bf16))
        grad_part = head_lanes(grad, head, jnp.zeros((), bf16))
        probs = jnp.exp(mm_nt(part, km[head]) - lse[:, 2 * head : 2 * head + 1])
        dprob = mm_nt(grad_part, v_ref[...])
        total = jnp.sum(probs * dprob, axis=-1, keepdims=True)
        dscore = (probs * (dprob - total)).astype(bf16)
        grads.append(mm(dscore, k_ref[...]))

        def add(target, update):
            lanes = lane_of(target.shape)
            mine = (lanes < 64) if head == 0 else (lanes >= 64)
            target[...] += jnp.where(mine, update, jnp.zeros_like(update))

        add(dk, mm_tn(dscore, scaled))
        add(dv, mm_tn(probs.astype(bf16), grad))
    lanes = lane_of(dq_ref.shape)
    dq_ref[...] = rotate_lanes(
        (jnp.where(lanes < 64, grads[0], grads[1]) + dqt_ref[...]) * 0.125,
        cosq_ref[...],
        -sinq_ref[...],
    )

    @pl.when(step == pl.num_programs(1) - 1)
    def _():
        dk_ref[...] = rotate_lanes(dk[...], cosk_ref[...], -sink_ref[...])
        dv_ref[...] = dv[...].astype(bf16)


def self_backward(query, key, value, grad, lse, dquery_text, tables, live_bias, rows):
    seq, width = query.shape
    pairs = width // 128
    full = lambda p, i: (0, p)
    block = lambda p, i: (i, p)
    qrow = lambda p, i: (i, 0)
    whole = lambda p, i: (0, 0)
    return pl.pallas_call(
        self_back_body,
        grid=(pairs, seq // rows),
        in_specs=[
            pl.BlockSpec((rows, 128), block),
            pl.BlockSpec((seq, 128), full),
            pl.BlockSpec((seq, 128), full),
            pl.BlockSpec((rows, 128), block),
            pl.BlockSpec((rows, 128), block),
            pl.BlockSpec((rows, 128), block),
            pl.BlockSpec((rows, 128), qrow),
            pl.BlockSpec((rows, 128), qrow),
            pl.BlockSpec((seq, 128), whole),
            pl.BlockSpec((seq, 128), whole),
            pl.BlockSpec((seq, 1), whole),
        ],
        out_specs=[
            pl.BlockSpec((rows, 128), block),
            pl.BlockSpec((seq, 128), full),
            pl.BlockSpec((seq, 128), full),
        ],
        out_shape=[
            jax.ShapeDtypeStruct((seq, width), f32),
            jax.ShapeDtypeStruct((seq, width), f32),
            jax.ShapeDtypeStruct((seq, width), bf16),
        ],
        scratch_shapes=[
            pltpu.VMEM((2, seq, 128), bf16),
            pltpu.VMEM((seq, 128), f32),
            pltpu.VMEM((seq, 128), f32),
        ],
        compiler_params=pltpu.CompilerParams(
            dimension_semantics=("arbitrary", "arbitrary"), vmem_limit_bytes=20 << 20
        ),
        cost_estimate=pl.CostEstimate(
            flops=40 * seq * seq * width,
            transcendentals=seq * seq * width // 64,
            bytes_accessed=seq * width * 28,
        ),
        name="self_backward",
    )(query, key, value, grad, lse, dquery_text, tables[0], tables[1], tables[0], tables[1], live_bias)


def feed_body(x0_ref, x1_ref, g0_ref, g1_ref, gate_ref, up_ref, down_ref, hidden_ref, grads_ref):
    step = pl.program_id(0)
    block = down_ref.shape[0]
    units = grads_ref.shape[1] // 2
    rows_in = jnp.concatenate([x0_ref[...], x1_ref[...]], axis=0)
    grads_in = jnp.concatenate([g0_ref[...], g1_ref[...]], axis=0)
    gate = mm(rows_in, gate_ref[...])
    up = mm(rows_in, up_ref[...])
    grad_hidden = mm_nt(grads_in, down_ref[...])
    sigmoid = 1.0 / (1.0 + jnp.exp(-gate))
    silu = gate * sigmoid
    hidden_ref[...] = (silu * up).astype(bf16)
    start = pl.multiple_of(step * block, block)
    grads_ref[:, pl.ds(start, block)] = (
        grad_hidden * up * (sigmoid * (1.0 + gate * (1.0 - sigmoid)))
    ).astype(bf16)
    grads_ref[:, pl.ds(pl.multiple_of(units + start, block), block)] = (grad_hidden * silu).astype(bf16)


def feed_forward(rows_in, grads_in, gateup, down, units_block):
    rows, width = rows_in[0].shape
    units = down.shape[0]
    steps = units // units_block
    whole = pl.BlockSpec((rows, width), lambda j: (0, 0))
    return pl.pallas_call(
        feed_body,
        grid=(steps,),
        in_specs=[whole] * 4
        + [
            pl.BlockSpec((width, units_block), lambda j: (0, j)),
            pl.BlockSpec((width, units_block), lambda j: (0, j + steps)),
            pl.BlockSpec((units_block, width), lambda j: (j, 0)),
        ],
        out_specs=[
            pl.BlockSpec((2 * rows, units_block), lambda j: (0, j)),
            pl.BlockSpec((2 * rows, 2 * units), lambda j: (0, 0)),
        ],
        out_shape=[
            jax.ShapeDtypeStruct((2 * rows, units), bf16),
            jax.ShapeDtypeStruct((2 * rows, 2 * units), bf16),
        ],
        compiler_params=pltpu.CompilerParams(
            dimension_semantics=("arbitrary",), vmem_limit_bytes=32 << 20
        ),
        cost_estimate=pl.CostEstimate(
            flops=12 * rows * width * units,
            transcendentals=2 * rows * units,
            bytes_accessed=6 * width * units + 8 * rows * width + 12 * rows * units,
        ),
        name="feed_forward",
    )(*rows_in, *grads_in, gateup, gateup, down)


def project_body(
    own_ref, x_ref, gain_ref, scale_ref, shift_ref, w0_ref, w1_ref, w2_ref, w3_ref,
    normed_ref, out_ref, query_ref, key_ref,
):
    values = x_ref[...].astype(f32)
    inverse = lax.rsqrt(jnp.mean(values * values, axis=-1, keepdims=True) + norm_eps)
    normed_ref[...] = (
        values * inverse * gain_ref[...] * (1.0 + scale_ref[...]) + shift_ref[...]
    ).astype(bf16)
    depth = w0_ref.shape[0]
    total = None
    for m, w_ref in enumerate((w0_ref, w1_ref, w2_ref, w3_ref)):
        start = pl.multiple_of((own_ref[0] ^ m) * depth, depth)
        term = mm(normed_ref[:, pl.ds(start, depth)], w_ref[...])
        total = term if total is None else total + term
    out_ref[...] = total
    part = out_ref.shape[1] // 3
    ones = jnp.ones((8, part), f32)

    def squares(rows):
        return lax.dot_general(
            ones,
            rows * rows,
            (((1,), (1,)), ((), ())),
            precision=lax.Precision.HIGHEST,
            preferred_element_type=f32,
        )

    query_ref[...] = squares(total[:, :part])
    key_ref[...] = squares(total[:, part : 2 * part])


def project(own, tokens, gain, scale, shift, weights):
    seq, width = tokens.shape
    columns = weights[0].shape[1]
    rows = 512 if seq % 512 == 0 else seq
    row = lambda i, own: (0, 0)
    block = lambda i, own: (i, 0)
    flat = lambda i, own: (0, i)
    return pl.pallas_call(
        project_body,
        grid_spec=pltpu.PrefetchScalarGridSpec(
            num_scalar_prefetch=1,
            grid=(seq // rows,),
            in_specs=[pl.BlockSpec((rows, width), block)]
            + [pl.BlockSpec((1, width), row)] * 3
            + [pl.BlockSpec(weights[0].shape, row)] * 4,
            out_specs=[
                pl.BlockSpec((rows, width), block),
                pl.BlockSpec((rows, columns), block),
                pl.BlockSpec((8, rows), flat),
                pl.BlockSpec((8, rows), flat),
            ],
        ),
        out_shape=[
            jax.ShapeDtypeStruct((seq, width), bf16),
            jax.ShapeDtypeStruct((seq, columns), f32),
            jax.ShapeDtypeStruct((8, seq), f32),
            jax.ShapeDtypeStruct((8, seq), f32),
        ],
        compiler_params=pltpu.CompilerParams(
            dimension_semantics=("arbitrary",), vmem_limit_bytes=24 << 20
        ),
        cost_estimate=pl.CostEstimate(
            flops=seq * width, transcendentals=0, bytes_accessed=seq * width
        ),
        name="project",
    )(own[None], tokens, gain, scale, shift, *weights)


def project_back_body(own_ref, d_ref, w0_ref, w1_ref, w2_ref, w3_ref, out_ref):
    depth = w0_ref.shape[0]
    for m, w_ref in enumerate((w0_ref, w1_ref, w2_ref, w3_ref)):
        start = pl.multiple_of((own_ref[0] ^ m) * depth, depth)
        out_ref[:, pl.ds(start, depth)] = mm_nt(d_ref[...], w_ref[...]).astype(bf16)


def project_back(own, grads, weights):
    seq, columns = grads.shape
    width = weights[0].shape[0] * 4
    rows = 512 if seq % 512 == 0 else seq
    block = lambda i, own: (i, 0)
    return pl.pallas_call(
        project_back_body,
        grid_spec=pltpu.PrefetchScalarGridSpec(
            num_scalar_prefetch=1,
            grid=(seq // rows,),
            in_specs=[pl.BlockSpec((rows, columns), block)]
            + [pl.BlockSpec(weights[0].shape, lambda i, own: (0, 0))] * 4,
            out_specs=pl.BlockSpec((rows, width), block),
        ),
        out_shape=jax.ShapeDtypeStruct((seq, width), bf16),
        compiler_params=pltpu.CompilerParams(
            dimension_semantics=("arbitrary",), vmem_limit_bytes=24 << 20
        ),
        cost_estimate=pl.CostEstimate(
            flops=seq * width, transcendentals=0, bytes_accessed=seq * width
        ),
        name="project_back",
    )(own[None], grads, *weights)


def on_device(
    tokens,
    caption,
    caption_mask,
    item_lengths,
    item_band,
    positions,
    band_table,
    adaln_weight,
    adaln_bias,
    query_weight,
    key_weight,
    value_weight,
    outproj_weight,
    capkey_weight,
    capvalue_weight,
    norm_gains,
    head_gate,
    gate_weight,
    up_weight,
    down_weight,
    cotangent,
):
    own = lax.axis_index("fsdp")
    place = lax.axis_index("dp")
    count = lax.axis_size("fsdp")
    data_count = lax.axis_size("dp")
    near = dp_place(0)
    rows, width = tokens.shape[1:]
    seq = rows * count
    part = width // count
    head_count = head_gate.shape[0]
    head_size = width // head_count
    own_heads = head_count // count
    units = down_weight.shape[0]
    text_rows = caption.shape[1]
    text = text_rows * count
    cap_depth = capkey_weight.shape[0]
    masks = (0, 1, 2, 3)

    def split_rel(values):
        return [values[m * rows : (m + 1) * rows] for m in masks]

    band_onehot = item_band[:, None] == jnp.arange(band_table.shape[0], dtype=jnp.int32)[None, :]
    band_vector = jnp.dot(band_onehot.astype(bf16), band_table, preferred_element_type=f32)
    silu_low = jax.nn.silu(band_vector).astype(bf16)
    slice_depth = adaln_weight.shape[0]
    modulation_part = mm(
        lax.dynamic_slice_in_dim(silu_low, own * slice_depth, slice_depth, 1), adaln_weight
    )[0]
    modulation_part = modulation_part + lax.dynamic_update_slice(
        jnp.zeros_like(modulation_part), adaln_bias.astype(f32), (own * adaln_bias.shape[0],)
    )
    gains_part = lax.dynamic_update_slice(
        jnp.zeros((2, width), f32), norm_gains[0::4].astype(f32), (0, own * part)
    )
    places_part = lax.dynamic_update_slice(
        jnp.zeros((2, seq), f32), positions[0].astype(f32), (0, own * rows)
    )
    small = jnp.concatenate([modulation_part, gains_part.reshape(-1), places_part.reshape(-1)])

    def cap_slice(mask):
        return lax.dynamic_slice_in_dim(caption[0], (own ^ mask) * cap_depth, cap_depth, 1)

    depth = query_weight.shape[0]

    def head_columns(mask, start, length):
        return jnp.concatenate(
            [
                lax.dynamic_slice(w, (start, (own ^ mask) * part), (length, part))
                for w in (query_weight, key_weight, value_weight)
            ],
            axis=1,
        )

    thin = gate_weight.shape[0] // data_count
    units_block = 256 if units % 256 == 0 else units

    def unit_columns(mask):
        return jnp.concatenate(
            [
                lax.dynamic_slice(w, (place * thin, (own ^ mask) * units), (thin, units))
                for w in (gate_weight, up_weight)
            ],
            axis=1,
        )

    small_far = hop(small, 2)
    cap_far = hop(jnp.stack([cap_slice(2), cap_slice(3)]), 2)
    fetched = hop(jnp.stack([head_columns(m, 0, depth) for m in (2, 3)]), 2)
    thin_far = hop(jnp.stack([unit_columns(2), unit_columns(3)]), 2)
    token_own = tokens[0]
    thin_near = hop(jnp.stack([unit_columns(1), thin_far[1]]), 1)
    thin_all = jnp.stack(natural_order([unit_columns(0), thin_near[0], thin_far[0], thin_near[1]], own))
    gateup_weight = lax.all_gather(thin_all, "dp", axis=1, tiled=True).reshape(width, 2 * units)
    small, small_far, cap_far, fetched, token_own, thin_all = join(
        small, small_far, cap_far, fetched, token_own, thin_all
    )

    token_far = hop(token_own, 2)
    fetched_near = hop(jnp.stack([head_columns(1, 0, depth), fetched[1]]), 1)
    small = small + small_far
    small_near = hop(small, 1)
    cap_near = hop(jnp.stack([cap_slice(1), cap_far[1]]), 1)
    caption_part = jnp.concatenate(
        natural_order([cap_slice(0), cap_near[0], cap_far[0], cap_near[1]], own), axis=0
    )
    cap_partial = jnp.concatenate(
        [mm(caption_part, capkey_weight).astype(bf16), mm(caption_part, capvalue_weight).astype(bf16)],
        axis=0,
    )

    def cap_columns(mask):
        return lax.dynamic_slice_in_dim(cap_partial, (own ^ mask) * part, part, 1)

    cap_sent = jnp.stack([cap_columns(3), cap_columns(1)])
    cap_kept = jnp.stack([cap_columns(2), cap_columns(0)])
    cap_inner = hop(cap_sent, 1)
    cap_passed = (cap_kept[0].astype(f32) + cap_inner[0].astype(f32)).astype(bf16)
    token_two = jnp.stack([token_own, token_far])
    (
        token_two, thin_all, fetched_near, small_near, cap_inner, cap_kept, cap_passed
    ) = join(token_two, thin_all, fetched_near, small_near, cap_inner, cap_kept, cap_passed)
    cap_passed = hop(cap_passed, 2)

    token_near = hop(token_two, 1)
    token_all = jnp.concatenate([token_two[0], token_near[0], token_two[1], token_near[1]], axis=0)
    top = dp_bits() - 1

    def cap_split(values, bit):
        half = values.shape[2] // 2
        return [
            lax.dynamic_slice_in_dim(values, side * half, half, 2)
            for side in (dp_place(bit), 1 - dp_place(bit))
        ]

    (token_all,) = join(token_all)

    small = small + small_near
    modulation = small[: 6 * width].reshape(6, 1, width)
    shift_mix, scale_mix, gate_mix, shift_feed, scale_feed, gate_feed = [modulation[i] for i in range(6)]
    gain_mix = small[6 * width : 7 * width][None]
    gain_feed = small[7 * width : 8 * width][None]
    places = small[8 * width :].reshape(2, count, rows)
    order = own ^ jnp.arange(count, dtype=jnp.int32)
    places_rel = jnp.concatenate(natural_order([places[:, m] for m in masks], own), axis=1)
    slots_rel = (order[:, None] * rows + jnp.arange(rows, dtype=jnp.int32)[None]).reshape(seq)
    live_bias = jnp.where(slots_rel < item_lengths[0], 0.0, masked_score).astype(f32)[:, None]
    text_live = caption_mask[0] > 0
    text_bias = jnp.where(text_live, 0.0, masked_score).astype(f32)[:, None]
    quarter = head_size // 4
    lane = jnp.arange(128, dtype=jnp.int32)
    frequency = jnp.exp(-jnp.log(rope_base) * (lane % quarter).astype(f32) / quarter)[None]
    by_row = (lane % head_size < 2 * quarter)[None]
    angles = jnp.where(by_row, places_rel[0][:, None], places_rel[1][:, None]) * frequency
    sign = jnp.where((lane // quarter) % 2 == 0, -1.0, 1.0).astype(f32)[None]
    tables = (jnp.cos(angles), jnp.sin(angles) * sign)

    qkv_rel = [head_columns(0, 0, depth), fetched_near[0], fetched[0], fetched_near[1]]
    normed_all, qkv, query_square, key_square = project(
        own, token_all, gain_mix, scale_mix, shift_mix, qkv_rel
    )
    cap_passed, query_square, key_square = join(cap_passed, query_square, key_square)
    cap_raw = cap_kept[1].astype(f32) + cap_inner[1].astype(f32) + cap_passed.astype(f32)
    capkey_raw, capvalue_low = cap_raw[:text], cap_raw[text:].astype(bf16)

    query_square, key_square, cap_square = sum_rows_rel(
        [
            query_square[0],
            key_square[0],
        ],
        count,
        [jnp.sum(capkey_raw * capkey_raw, axis=-1)],
    )
    query_inverse = lax.rsqrt(query_square / width + norm_eps)[None]
    key_inverse = lax.rsqrt(key_square / width + norm_eps)[None]
    capkey_inverse = lax.rsqrt(cap_square / width + norm_eps)[:, None]
    own_gains = norm_gains.astype(f32)
    capkey_low = (capkey_raw * capkey_inverse * own_gains[3:4]).astype(bf16)
    tanh_gate = jnp.tanh(head_gate.astype(f32))
    own_tanh = lax.dynamic_slice_in_dim(tanh_gate, own * own_heads, own_heads, 0)
    tanh_lane = jnp.repeat(own_tanh, head_size)[None]
    block_rows = seq if seq <= 1024 else 256

    query_live = (own * rows + jnp.arange(rows, dtype=jnp.int32)) < item_lengths[0]
    grad_out = cotangent[0].astype(f32) * query_live[:, None].astype(f32)
    grad_ffn = (gate_feed * grad_out).astype(bf16)
    grad_ffn, query_inverse, key_inverse, capkey_low = join(
        grad_ffn, query_inverse, key_inverse, capkey_low
    )
    grad_ffn_far = hop(grad_ffn, 2)
    attended, query_low, key_low, value_low, lse = attend_forward(
        qkv, (query_inverse, key_inverse), (own_gains[1:2], own_gains[2:3]), tables,
        capkey_low, capvalue_low, live_bias, text_bias, tanh_lane, block_rows,
    )
    attended, grad_ffn_far = join(attended, grad_ffn_far)

    branch_part = mm(attended, outproj_weight).astype(bf16)
    branch_near = hop(
        jnp.stack([branch_part[3 * rows :], branch_part[rows : 2 * rows]]), 1
    )
    branch_passed = (
        branch_part[2 * rows : 3 * rows].astype(f32) + branch_near[0].astype(f32)
    ).astype(bf16)
    branch_kept = branch_part[:rows].astype(f32) + branch_near[1].astype(f32)
    branch_passed, branch_kept, grad_ffn_far = join(branch_passed, branch_kept, grad_ffn_far)
    branch_passed = hop(branch_passed, 2)
    grad_ffn_near = hop(jnp.stack([grad_ffn, grad_ffn_far]), 1)
    grad_ffn_rel = [grad_ffn, grad_ffn_near[0], grad_ffn_far, grad_ffn_near[1]]
    grad_ffn_all = jnp.concatenate(grad_ffn_rel, axis=0)
    branch_passed, gateup_weight, grad_ffn_all, *grad_ffn_rel = join(
        branch_passed, gateup_weight, grad_ffn_all, *grad_ffn_rel
    )
    branch = branch_kept + branch_passed.astype(f32)
    token_float = token_own.astype(f32)
    middle = token_float + gate_mix * branch

    unit_feed, inverse_feed = rms_parts(middle)
    normed_feed = (unit_feed * gain_feed * (1.0 + scale_feed) + shift_feed).astype(bf16)
    feed_far = hop(normed_feed, 2)
    feed_near = hop(normed_feed, 1)
    hidden_early, grads_early = feed_forward(
        [normed_feed, feed_near], grad_ffn_rel[:2], gateup_weight, down_weight, units_block
    )
    early = mm_nt(grads_early, gateup_weight).astype(bf16)
    feed_far, hidden_early, early = join(feed_far, hidden_early, early)
    feed_rel = [normed_feed, feed_near, feed_far, hop(feed_far, 1)]
    hidden_late, grads_late = feed_forward(
        feed_rel[2:], grad_ffn_rel[2:], gateup_weight, down_weight, units_block
    )
    late = mm_nt(grads_late, gateup_weight).astype(bf16)
    late_near = hop(late[rows:], 1)
    passed = (late[:rows].astype(f32) + late_near.astype(f32)).astype(bf16)
    cap_items, cap_items_sent = cap_split(caption[0][None], top)
    passed, early, hidden_late, grads_late, cap_items_sent = join(
        passed, early, hidden_late, grads_late, cap_items_sent
    )

    passed = hop(passed, 2)
    early_near = hop(early[rows:], 1)
    cap_items = jnp.concatenate([cap_items, dp_hop(cap_items_sent, top)], axis=0)
    hidden = jnp.concatenate([hidden_early, hidden_late], axis=0)
    down_blocks = dp_blocks(mm_tn(hidden, grad_ffn_all).astype(bf16))
    down_cut = width // 3
    down_first = dp_hop(dp_sent(down_blocks, 0, down_cut), 0)
    feed_all = jnp.concatenate(feed_rel, axis=0)
    grad_units = jnp.concatenate([grads_early, grads_late], axis=0)
    gateup_blocks = dp_blocks(mm_tn(feed_all, grad_units).astype(bf16))
    down_sent = dp_sent(down_blocks, down_cut, width)
    passed, early_near, down_first, gateup_blocks, down_sent, cap_items = join(
        passed, early_near, down_first, gateup_blocks, down_sent, cap_items
    )
    down_second = dp_hop(down_sent, 0)
    grad_normfeed = early[:rows].astype(f32) + early_near.astype(f32) + passed.astype(f32)

    dshift_feed = jnp.sum(grad_normfeed, axis=0)
    dscale_feed = jnp.sum(grad_normfeed * (unit_feed * gain_feed), axis=0)
    grad_scaledfeed = grad_normfeed * (1.0 + scale_feed)
    gain_feed_grad = jnp.sum(grad_scaledfeed * unit_feed, axis=0)
    grad_middle = grad_out + rms_back(unit_feed, inverse_feed, grad_scaledfeed * gain_feed)
    dgate_mix = jnp.sum(grad_middle * branch, axis=0)

    grad_branch = (gate_mix * grad_middle).astype(bf16)
    grad_branch, gateup_blocks = join(grad_branch, gateup_blocks)
    grad_branch_far = hop(grad_branch, 2)
    ffn_part = mm(hidden, down_weight).astype(bf16)
    cuts = [2 * units * i // 16 for i in (0, 4, 7, 11, 16)]
    gateup_sent = dp_sent(gateup_blocks, cuts[0], cuts[1])
    for bit in reversed(range(1, top)):
        cap_items, cap_items_sent = cap_split(cap_items, bit)
        cap_items = jnp.concatenate([cap_items, dp_hop(cap_items_sent, bit)], axis=0)
    cap_items, cap_items_sent = cap_split(cap_items, 0)
    grad_branch_far, down_second, ffn_part, gateup_sent, cap_items_sent = join(
        grad_branch_far, down_second, ffn_part, gateup_sent, cap_items_sent
    )
    gateup_first = dp_hop(gateup_sent, 0)
    cap_items = jnp.concatenate([cap_items, dp_hop(cap_items_sent, 0)], axis=0)
    grad_branch_two = jnp.stack([grad_branch, grad_branch_far])
    grad_branch_near = hop(grad_branch_two, 1)
    ffn_near = hop(jnp.stack([ffn_part[3 * rows :], ffn_part[rows : 2 * rows]]), 1)
    grad_branch_all = jnp.concatenate(
        [grad_branch, grad_branch_near[0], grad_branch_far, grad_branch_near[1]], axis=0
    )
    down_joined = [
        dp_joined(down_blocks, down_first, 0, down_cut),
        dp_joined(down_blocks, down_second, down_cut, width),
    ]
    down_kept = jnp.concatenate([kept for kept, _ in down_joined], axis=-1)
    down_line = dp_hop(jnp.concatenate([sent for _, sent in down_joined], axis=-1), 1)
    grad_attended = mm_nt(grad_branch_all, outproj_weight).astype(bf16)
    dquery_text, dcapkey, grad_capvalue, dtanh = text_backward(
        query_low, capkey_low, capvalue_low, grad_attended, lse, text_bias, tanh_lane, seq
    )
    outproj_part = mm_tn(attended, grad_branch_all).astype(bf16)
    outproj_blocks = (
        outproj_part.reshape(data_count, -1, count, part)
        .transpose(0, 2, 1, 3)
        .reshape(data_count, width // data_count, part)
    )
    gateup_sent = dp_sent(gateup_blocks, cuts[1], cuts[2])
    (
        dquery_text, dcapkey, grad_capvalue, dtanh, gateup_first, down_line, ffn_near, cap_items,
        outproj_blocks, gateup_sent,
    ) = join(
        dquery_text, dcapkey, grad_capvalue, dtanh, gateup_first, down_line, ffn_near, cap_items,
        outproj_blocks, gateup_sent,
    )
    gateup_more = dp_hop(gateup_sent, 0)
    cap_items_far = hop(cap_items, 2)
    capkey_unit = capkey_raw * capkey_inverse
    capkey_scaled = dcapkey * own_gains[3:4]
    (cap_dot,) = sum_rows_rel([], count, [jnp.sum(capkey_scaled * capkey_unit, axis=-1)])
    grad_capkey = (
        capkey_inverse * (capkey_scaled - capkey_unit * (cap_dot[:, None] / width))
    ).astype(bf16)
    gain_capkey_grad = jnp.sum(dcapkey * capkey_unit, axis=0)
    grad_cap = jnp.concatenate([grad_capkey, grad_capvalue], axis=1)
    ffn_passed = (
        ffn_part[2 * rows : 3 * rows].astype(f32) + ffn_near[0].astype(f32)
    ).astype(bf16)
    gateup_sent = jnp.concatenate(
        [dp_sent(gateup_blocks, cuts[2], cuts[3]), dp_sent(outproj_blocks, 0, part)], axis=-1
    )
    dquery_text, grad_cap, ffn_passed, gateup_sent, gateup_more, cap_items_far = join(
        dquery_text, grad_cap, ffn_passed, gateup_sent, gateup_more, cap_items_far
    )

    ffn_passed = hop(ffn_passed, 2)
    gateup_second = dp_hop(gateup_sent, 0)
    down_state = dp_next((down_kept, down_line), 2) if top >= 2 else (down_kept, down_line)
    gateup_joined = [
        dp_joined(gateup_blocks, gateup_first, cuts[0], cuts[1]),
        dp_joined(gateup_blocks, gateup_more, cuts[1], cuts[2]),
    ]
    gateup_kept = jnp.concatenate([kept for kept, _ in gateup_joined], axis=-1)
    gateup_line = dp_hop(jnp.concatenate([sent for _, sent in gateup_joined], axis=-1), 1)
    cap_grads = jnp.stack([grad_cap, dp_hop(grad_cap, top)])
    query_unrot, key_unrot, grad_value = self_backward(
        query_low, key_low, value_low, grad_attended, lse, dquery_text, tables, live_bias, block_rows
    )
    gateup_sent = dp_sent(gateup_blocks, cuts[3], cuts[4])
    (
        query_unrot, key_unrot, grad_value, ffn_passed, gateup_second, down_arrived, gateup_line,
        cap_grads, gateup_sent,
    ) = join(
        query_unrot, key_unrot, grad_value, ffn_passed, gateup_second, down_state[1], gateup_line,
        cap_grads, gateup_sent,
    )
    down_state = (down_state[0], down_arrived)
    cap_items_two = jnp.stack([cap_items, cap_items_far], axis=1)

    gateup_third = dp_hop(gateup_sent, 0)
    second_width = cuts[3] - cuts[2]
    second_joined = [
        dp_joined(gateup_blocks, gateup_second[..., :second_width], cuts[2], cuts[3]),
        dp_joined(outproj_blocks, gateup_second[..., second_width:], 0, part),
    ]
    second_kept = jnp.concatenate([kept for kept, _ in second_joined], axis=-1)
    second_line = dp_hop(jnp.concatenate([sent for _, sent in second_joined], axis=-1), 1)
    down_sum = dp_total(down_state) if top <= 2 else dp_rest_from(down_state, 3)
    owned_down = to_owner(down_sum)
    first_state = dp_next((gateup_kept, gateup_line), 2) if top >= 2 else (gateup_kept, gateup_line)
    query_inverse, key_inverse = query_inverse[0][:, None], key_inverse[0][:, None]
    query_unit = qkv[:, :part] * query_inverse
    key_unit = qkv[:, part : 2 * part] * key_inverse
    query_scaled = query_unrot * own_gains[1:2]
    key_scaled = key_unrot * own_gains[2:3]
    query_dot, key_dot = sum_rows_rel(
        [
            jnp.sum(query_scaled * query_unit, axis=-1),
            jnp.sum(key_scaled * key_unit, axis=-1),
        ],
        count,
    )
    gain_query_grad = jnp.sum(query_unrot * query_unit, axis=0)
    gain_key_grad = jnp.sum(key_unrot * key_unit, axis=0)
    grad_qkv = jnp.concatenate(
        [
            (query_inverse * (query_scaled - query_unit * (query_dot[:, None] / width))).astype(bf16),
            (key_inverse * (key_scaled - key_unit * (key_dot[:, None] / width))).astype(bf16),
            grad_value,
        ],
        axis=1,
    )
    qkv_blocks = dp_blocks(mm_tn(normed_all, grad_qkv).astype(bf16))
    qkv_sent = dp_sent(qkv_blocks, 0, 3 * part)
    qkv_sent, gateup_third, first_arrived, second_line, owned_down = join(
        qkv_sent, gateup_third, first_state[1], second_line, owned_down
    )
    first_state = (first_state[0], first_arrived)

    qkv_beside = dp_hop(qkv_sent, 0)
    third_kept, third_line = dp_joined(gateup_blocks, gateup_third, cuts[3], cuts[4])
    third_line = dp_hop(third_line, 1)
    second_state = dp_next((second_kept, second_line), 2) if top >= 2 else (second_kept, second_line)
    for bit in reversed(range(1, top)):
        cap_grads = jnp.concatenate([cap_grads, dp_hop(cap_grads, bit)], axis=0)
    normmix_part = project_back(own, grad_qkv, qkv_rel)
    normmix_near = hop(jnp.stack([normmix_part[3 * rows :], normmix_part[rows : 2 * rows]]), 1)
    normmix_passed = hop(
        (normmix_part[2 * rows : 3 * rows].astype(f32) + normmix_near[0].astype(f32)).astype(bf16), 2
    )
    qkv_beside, third_line, normmix_passed, cap_grads, second_arrived, cap_items_two = join(
        qkv_beside, third_line, normmix_passed, cap_grads, second_state[1], cap_items_two
    )
    second_state = (second_state[0], second_arrived)
    cap_items_near = hop(cap_items_two, 1)
    cap_items_all = jnp.stack(
        natural_order(
            [cap_items_two[:, 0], cap_items_near[:, 0], cap_items_two[:, 1], cap_items_near[:, 1]], own
        ),
        axis=1,
    ).reshape(data_count * text, -1)

    qkv_kept, qkv_line = dp_joined(qkv_blocks, qkv_beside, 0, 3 * part)
    qkv_line = dp_hop(qkv_line, 1)
    third_state = dp_next((third_kept, third_line), 2) if top >= 2 else (third_kept, third_line)
    cap_grads = jnp.concatenate([cap_grads, dp_hop(cap_grads, 0)], axis=0)
    grad_normmix = (
        normmix_part[:rows].astype(f32) + normmix_near[1].astype(f32) + normmix_passed.astype(f32)
    )
    ffn_out = ffn_part[:rows].astype(f32) + ffn_near[1].astype(f32) + ffn_passed.astype(f32)
    block_out = (middle + gate_feed * ffn_out).astype(bf16)
    dgate_feed = jnp.sum(grad_out * ffn_out, axis=0)
    unit_mix, inverse_mix = rms_parts(token_float)
    dshift_mix = jnp.sum(grad_normmix, axis=0)
    dscale_mix = jnp.sum(grad_normmix * (unit_mix * gain_mix), axis=0)
    grad_scaledmix = grad_normmix * (1.0 + scale_mix)
    gain_mix_grad = jnp.sum(grad_scaledmix * unit_mix, axis=0)
    tokens_grad = (
        grad_middle + rms_back(unit_mix, inverse_mix, grad_scaledmix * gain_mix)
    ).astype(bf16)

    own_rows = jnp.zeros((3, width), f32)
    own_rows = lax.dynamic_update_slice(
        own_rows, jnp.stack([gain_query_grad, gain_key_grad, gain_capkey_grad]), (0, own * part)
    )
    gate_sums = lax.dynamic_update_slice(
        jnp.zeros((head_count,), f32), dtanh[0, ::head_size], (own * own_heads,)
    )
    sums = jnp.concatenate([gain_mix_grad, own_rows.reshape(-1), gain_feed_grad, gate_sums])
    grad_modulation = jnp.concatenate(
        [dshift_mix, dscale_mix, dgate_mix, dshift_feed, dscale_feed, dgate_feed]
    )
    message = jnp.concatenate([grad_modulation, sums])
    message = message + hop(message, 1)
    message = message + hop(message, 2)
    mod_width = 6 * width
    item_rows = jnp.concatenate([message[:mod_width], silu_low[0].astype(f32)]).astype(bf16)[None]
    totals = message[mod_width:]

    def wider(item_rows, totals, bit):
        high = totals.astype(bf16)
        low = (totals - high.astype(f32)).astype(bf16)
        arrived = dp_hop(jnp.concatenate([item_rows.reshape(-1), high, low]), bit)
        rest = arrived[item_rows.size :].astype(f32)
        return (
            jnp.concatenate([item_rows, arrived[: item_rows.size].reshape(item_rows.shape)], axis=0),
            totals + (rest[: totals.size] + rest[totals.size :]),
        )

    first_sum = dp_total(first_state) if top <= 2 else dp_rest_from(first_state, 3)
    second_sum = dp_total(second_state) if top <= 2 else dp_rest_from(second_state, 3)
    outproj_sum = (
        second_sum[:, second_width:].reshape(count, -1, part).transpose(1, 0, 2).reshape(-1, width)
    )
    owned_outproj = to_owner(outproj_sum)
    second_sum = second_sum[:, :second_width]
    qkv_line, item_rows, totals, third_arrived, first_sum, second_sum, owned_outproj = join(
        qkv_line, item_rows, totals, third_state[1], first_sum, second_sum, owned_outproj
    )

    qkv_state = dp_next((qkv_kept, qkv_line), 2) if top >= 2 else (qkv_kept, qkv_line)
    third_state = (third_state[0], third_arrived)
    third_sum = dp_total(third_state) if top <= 2 else dp_rest_from(third_state, 3)
    gateup_pieces, gateup_sent = spread_pieces([first_sum, second_sum, third_sum], own)
    gateup_far = hop(gateup_sent, 2)
    item_rows, totals = wider(item_rows, totals, 0)
    cap_sum = mm_tn(cap_items_all, cap_grads.reshape(-1, cap_grads.shape[-1]))
    cap_pieces, cap_sent_far = spread_pieces([cap_sum], own)
    qkv_arrived, gateup_far, item_rows, totals, cap_sent_far = join(
        qkv_state[1], gateup_far, item_rows, totals, cap_sent_far
    )
    qkv_state = (qkv_state[0], qkv_arrived)

    qkv_sum = dp_total(qkv_state) if top <= 2 else dp_rest_from(qkv_state, 3)
    qkv_pieces, qkv_sent_far = spread_pieces([qkv_sum], own)
    qkv_far = hop(qkv_sent_far, 2)
    cap_far_rows = hop(cap_sent_far, 2)
    gateup_near = spread_near(gateup_pieces, gateup_far)
    item_rows, totals = wider(item_rows, totals, 1)
    qkv_far, cap_far_rows, gateup_near, item_rows, totals = join(
        qkv_far, cap_far_rows, gateup_near, item_rows, totals
    )
    qkv_near = spread_near(qkv_pieces, qkv_far)
    cap_near_rows = spread_near(cap_pieces, cap_far_rows)
    for bit in range(2, top + 1):
        item_rows, totals = wider(item_rows, totals, bit)
    gate_grad, up_grad = spread_result(gateup_pieces, gateup_far, gateup_near, [units] * 2, own)
    query_grad, key_grad, value_grad = spread_result(qkv_pieces, qkv_far, qkv_near, [part] * 3, own)
    capkey_grad, capvalue_grad = spread_result(cap_pieces, cap_far_rows, cap_near_rows, [part] * 2, own)
    modulation_rows = item_rows[:, :mod_width].astype(f32)
    silu_rows = item_rows[:, mod_width:].astype(f32)
    owner = place * count + own
    devices = count * data_count
    cd_rows = silu_rows.shape[1] // devices
    adaln_wgrad = lax.dot_general(
        lax.dynamic_slice_in_dim(silu_rows, owner * cd_rows, cd_rows, 1),
        modulation_rows,
        (((0,), (0,)), ((), ())),
        precision=lax.Precision.HIGHEST,
        preferred_element_type=f32,
    )
    bias_rows = mod_width // devices
    adaln_bgrad = lax.dynamic_slice_in_dim(
        jnp.sum(modulation_rows, axis=0), owner * bias_rows, bias_rows, 0
    )
    gains_grad = lax.dynamic_slice_in_dim(
        totals[: 5 * width].reshape(5, width), owner * (width // devices), width // devices, 1
    )
    headgate_grad = totals[5 * width :] * (1.0 - tanh_gate * tanh_gate)

    down_grad, outproj_grad = owned_down, owned_outproj
    return (
        block_out[None],
        tokens_grad[None],
        adaln_wgrad,
        adaln_bgrad,
        query_grad,
        key_grad,
        value_grad,
        outproj_grad,
        capkey_grad,
        capvalue_grad,
        gains_grad,
        headgate_grad,
        gate_grad,
        up_grad,
        down_grad,
    )


def solution(mesh):
    return jax.shard_map(
        on_device,
        mesh=mesh,
        in_specs=(
            P("dp", "fsdp", None),
            P("dp", "fsdp", None),
            P("dp", None),
            P("dp"),
            P("dp"),
            P("dp", None, "fsdp"),
            P(),
            P("fsdp", None),
            P("fsdp"),
            P("fsdp", None),
            P("fsdp", None),
            P("fsdp", None),
            P("fsdp", None),
            P("fsdp", None),
            P("fsdp", None),
            P(None, "fsdp"),
            P(),
            P("fsdp", None),
            P("fsdp", None),
            P("fsdp", None),
            P("dp", "fsdp", None),
        ),
        out_specs=(
            P("dp", "fsdp", None),
            P("dp", "fsdp", None),
            P(("dp", "fsdp"), None),
            P(("dp", "fsdp")),
            P(("dp", "fsdp"), None),
            P(("dp", "fsdp"), None),
            P(("dp", "fsdp"), None),
            P(("dp", "fsdp"), None),
            P(("dp", "fsdp"), None),
            P(("dp", "fsdp"), None),
            P(None, ("dp", "fsdp")),
            P(),
            P(("dp", "fsdp"), None),
            P(("dp", "fsdp"), None),
            P(("dp", "fsdp"), None),
        ),
        check_vma=False,
    )
```
